32 devices in a mesh: groups: 2 (over x), lat: 16 (over z, y, core).
Axes of the slice: x: 2, y: 2, z: 4, core: 2. Of those that a mesh axis runs over, the one named last changes fastest.
Arguments:
- ocean_state: float32 [4, 16, 64, 384], P(None, None, ('groups', 'lat')), parts along dimension 2, may hold values from -4 to 4
- bottom: int32 [64, 384], P(('groups', 'lat')), parts along dimension 0, may hold values from 4 to 16
- tracers: float32 [16, 16, 768, 32], P(None, None, ('groups', 'lat')), parts along dimension 2, may hold values from -4 to 4
- land_sea: int32 [16, 768, 32], P(None, ('groups', 'lat')), parts along dimension 1, may hold values 0 or 1
- biome_id: int32 [768, 32], P(('groups', 'lat')), parts along dimension 0, may hold values from 0 to 3
- rate_table: float32 [4, 16, 16], replicated, may hold values from -1.5 to 1.5
Outputs:
- state_out: float32 [4, 16, 64, 384], P(None, None, ('groups', 'lat')), parts along dimension 2
- tracers_out: float32 [16, 16, 768, 32], P(None, None, ('groups', 'lat')), parts along dimension 2
The draws below stay inside these ranges and needn't reach their ends.
There are 2 independent parts, one for each index of `groups`. The reference program is written for one: setup_inputs(seed, part) draws one part's arguments, and reference() takes and returns one part's arrays. A program takes and returns all parts, laid end to end along the dimension named above; an argument that names none is the same for every part. Nothing has to cross between parts.
All inputs are finite; a program needn't handle non-finite values. No bound on the sum of `land_sea` on one device may be relied on, other than what follows from the above.
Results may differ from the reference program's by a relative error of at most 0.00014.
Values sent between devices are 32-bit elements; how exact they have to be, the bound alone decides.
No kernel may reach another device: no remote copies, remote signals or barrier semaphores. Data moves between devices by JAX's collectives and lax.ppermute only.
A program may use at most 128 MiB of HBM per device.

```python
import jax
import jax.numpy as jnp
from jax import lax

NZ = 16
NX = 384
NTR = 16
NB = 4
STEPS = 2
SUB = 2
NY = 32


def touch_ends(array, rng, smallest, top_value):
    extent = array.shape
    spot = [jax.random.randint(jax.random.fold_in(rng, axis), (), 0, extent[axis]) for axis in range(len(extent))]
    array = array.at[tuple(spot)].set(smallest)
    longest = extent.index(max(extent))
    spot[longest] = (spot[longest] + 1) % extent[longest]
    return array.at[tuple(spot)].set(top_value)


def block_scale(rng, shape, cuts, least, high):
    loudness = 1.0
    for position, blocks in cuts:
        draws = jax.random.uniform(jax.random.fold_in(jax.random.fold_in(rng, 6), position), (blocks,), jnp.float32, least / len(cuts), high / len(cuts))
        loudness = loudness * jnp.repeat(jnp.exp(draws), shape[position] // blocks).reshape((-1,) + (1,) * (len(shape) - 1 - position))
    return loudness


def noise(own_key, shape, scale, limit, cuts=(), kind=jnp.bfloat16):
    factor_of = block_scale(own_key, shape, cuts, -0.22, 0.18) if cuts else 1.0
    result = jax.random.normal(own_key, shape, jnp.float32) * scale * factor_of
    return jnp.minimum(jnp.maximum(result, -limit), limit).astype(kind)


def setup_inputs(seed: int = 0, part: int = 0) -> dict:
    splits = jax.random.split(jax.random.key(seed), 7)
    part_splits = jax.random.split(jax.random.fold_in(splits[6], part), 7)
    ocean_state = noise(part_splits[0], (4, NZ, NY, NX), 1.0, 4.0, ((2, 16),), jnp.float32)
    bottom = touch_ends(jax.random.randint(part_splits[1], (NY, NX), NZ // 4, NZ + 1), jax.random.fold_in(part_splits[1], 1), NZ // 4, NZ).astype(jnp.int32)
    tracers = noise(part_splits[2], (NTR, NZ, NX, NY), 1.0, 4.0, ((2, 16),), jnp.float32)
    land_sea = touch_ends((jax.random.randint(part_splits[3], (NZ, NX, NY), 0, 8) < 7).astype(jnp.int32), jax.random.fold_in(part_splits[3], 1), 0, 1)
    biome_id = touch_ends(jax.random.randint(part_splits[4], (NX, NY), 0, NB), jax.random.fold_in(part_splits[4], 1), 0, NB - 1).astype(jnp.int32)
    rate_table = noise(splits[5], (NB, NTR, NTR), NTR ** -0.5, 1.5, (), jnp.float32)
    return dict(ocean_state=ocean_state, bottom=bottom, tracers=tracers, land_sea=land_sea, biome_id=biome_id, rate_table=rate_table)


time_step = 0.1
viscosity = 0.1
heat_diff = 0.08
salt_diff = 0.06
therm_coef = 0.2
haline_coef = 0.15
gravity = 0.5
coriolis = 0.6
vert_ratio = 0.25
tracer_step = 0.1
tracer_diff = 0.1
water_atten = 0.04
chl_atten = 0.05
growth_rate = 0.8
heat_gain = 10.0


def laplace_rows(field):
    center = field[:, 1:-1, :]
    return jnp.roll(center, 1, 2) + jnp.roll(center, -1, 2) + field[:, 2:, :] + field[:, :-2, :] - 4.0 * center


def ocean_core(padded, wet_mask, lat_start, total_lat):
    speed_u, speed_v, temper, salty = padded[0], padded[1], padded[2], padded[3]
    east_mid = speed_u[:, 1:-1, :]
    north_mid = speed_v[:, 1:-1, :]
    temp_mid = temper[:, 1:-1, :]
    salt_mid = salty[:, 1:-1, :]
    pressure = gravity * jnp.cumsum(haline_coef * salty - therm_coef * temper, axis=0)
    press_mid = pressure[:, 1:-1, :]
    row_index = (lat_start + jnp.arange(wet_mask.shape[1], dtype=jnp.int32)).astype(jnp.float32)
    spin_rate = (coriolis * (2.0 * (row_index + 0.5) / total_lat - 1.0))[None, :, None]
    slope_east = 0.5 * (jnp.roll(press_mid, -1, 2) - jnp.roll(press_mid, 1, 2))
    slope_north = 0.5 * (pressure[:, 2:, :] - pressure[:, :-2, :])
    new_u = wet_mask * (east_mid + time_step * (spin_rate * north_mid - slope_east + viscosity * laplace_rows(speed_u)))
    new_v = wet_mask * (north_mid + time_step * (-spin_rate * east_mid - slope_north + viscosity * laplace_rows(speed_v)))
    new_s = wet_mask * (salt_mid + time_step * salt_diff * laplace_rows(salty))
    part_t = temp_mid + time_step * heat_diff * laplace_rows(temper)
    spread = 0.5 * (jnp.roll(east_mid, -1, 2) - jnp.roll(east_mid, 1, 2)) + 0.5 * (speed_v[:, 2:, :] - speed_v[:, :-2, :])
    rise_flux = -vert_ratio * jnp.flip(jnp.cumsum(jnp.flip(spread, 0), axis=0), 0)
    fluxes = jnp.stack([east_mid, north_mid, rise_flux])
    return new_u, new_v, part_t, new_s, fluxes


def light_field(plankton):
    chloro = jax.nn.softplus(plankton)
    attenuate = water_atten + chl_atten * chloro
    depth = jnp.cumsum(attenuate, axis=0) - attenuate
    row_index = jnp.arange(plankton.shape[-1], dtype=jnp.int32).astype(jnp.float32)
    place = 2.0 * (row_index + 0.5) / plankton.shape[-1] - 1.0
    surface = 1.0 - 0.5 * place * place
    top_light = surface * jnp.exp(-depth)
    return chloro, top_light, top_light * (1.0 - jnp.exp(-attenuate))


def tracer_core(tracer_ext, flux_ext, sea_mask, onehot, rate_table):
    center = tracer_ext[:, :, 1:-1, :]
    east_face = 0.5 * (flux_ext[0, :, :-1, :] + flux_ext[0, :, 1:, :])
    across = jnp.maximum(east_face, 0.0) * tracer_ext[:, :, :-1, :] + jnp.minimum(east_face, 0.0) * tracer_ext[:, :, 1:, :]
    div_east = across[:, :, 1:, :] - across[:, :, :-1, :]
    north_speed = flux_ext[1, :, 1:-1, :]
    north_face = 0.5 * (north_speed[:, :, :-1] + north_speed[:, :, 1:])
    along = jnp.maximum(north_face, 0.0) * center[..., :-1] + jnp.minimum(north_face, 0.0) * center[..., 1:]
    along = jnp.pad(along, ((0, 0), (0, 0), (0, 0), (1, 1)))
    div_north = along[..., 1:] - along[..., :-1]
    rise_face = flux_ext[2, 1:, 1:-1, :]
    upward = jnp.maximum(rise_face, 0.0) * center[:, 1:] + jnp.minimum(rise_face, 0.0) * center[:, :-1]
    upward = jnp.pad(upward, ((0, 0), (1, 1), (0, 0), (0, 0)))
    div_up = upward[:, :-1] - upward[:, 1:]
    side = jnp.pad(center, ((0, 0), (0, 0), (0, 0), (1, 1)))
    diffuse = tracer_ext[:, :, 2:, :] + tracer_ext[:, :, :-2, :] + side[..., 2:] + side[..., :-2] - 4.0 * center
    chloro, top_light, absorbed = light_field(center[0])
    nutrient = center[1] * center[1]
    uptake = growth_rate * top_light * chloro * nutrient / (1.0 + nutrient)
    rate_cell = jnp.einsum("bst,bij->stij", rate_table, onehot, precision=lax.Precision.HIGHEST)
    reaction = jnp.einsum("stij,tkij->skij", rate_cell, center, precision=lax.Precision.HIGHEST)
    reaction = reaction.at[0].add(uptake).at[1].add(-uptake)
    tendency = tracer_diff * diffuse + reaction - (div_east + div_north + div_up)
    return sea_mask[None] * (center + tracer_step * tendency)


def reference(ocean_state, bottom, tracers, land_sea, biome_id, rate_table):
    levels = ocean_state.shape[1]
    total_lat = ocean_state.shape[2]
    wet_mask = (jnp.arange(levels, dtype=jnp.int32)[:, None, None] < bottom[None]).astype(jnp.float32)
    sea_mask = land_sea.astype(jnp.float32)
    onehot = (biome_id[None] == jnp.arange(rate_table.shape[0], dtype=jnp.int32)[:, None, None]).astype(jnp.float32)
    state = ocean_state
    tracer_now = tracers
    for cycle_index in range(STEPS):
        state = state * wet_mask[None]
        padded = jnp.pad(state, ((0, 0), (0, 0), (1, 1), (0, 0)))
        new_u, new_v, part_t, new_s, fluxes = ocean_core(padded, wet_mask, 0, total_lat)
        flux_t = jnp.transpose(fluxes, (0, 1, 3, 2))
        flux_ext = jnp.pad(flux_t, ((0, 0), (0, 0), (1, 1), (0, 0)), mode="wrap")
        tracer_now = tracer_now * sea_mask[None]
        for sub_index in range(SUB):
            tracer_ext = jnp.pad(tracer_now, ((0, 0), (0, 0), (1, 1), (0, 0)), mode="wrap")
            tracer_now = tracer_core(tracer_ext, flux_ext, sea_mask, onehot, rate_table)
        heating = heat_gain * sea_mask * light_field(tracer_now[0])[2]
        heat_ocean = jnp.transpose(heating, (0, 2, 1))
        new_t = wet_mask * (part_t + time_step * heat_ocean)
        state = jnp.stack([new_u, new_v, new_t, new_s])
    return state, tracer_now
```

```python
import jax
import jax.numpy as jnp
from jax import lax
from jax.experimental import pallas as pl
from jax.experimental.pallas import tpu as pltpu
from jax.sharding import PartitionSpec as P

STEPS = 2
SUB = 2


time_step = 0.1
viscosity = 0.1
heat_diff = 0.08
salt_diff = 0.06
therm_coef = 0.2
haline_coef = 0.15
gravity = 0.5
coriolis = 0.6
vert_ratio = 0.25
tracer_step = 0.1
tracer_diff = 0.1
water_atten = 0.04
chl_atten = 0.05
growth_rate = 0.8
heat_gain = 10.0


def extended(block, sides, width, periodic):
    for axis, dim in sides:
        count = lax.axis_size(axis)
        forward = [(i, i + 1) for i in range(count - 1)]
        if periodic:
            forward.append((count - 1, 0))
        backward = [(target, source) for source, target in forward]
        low = lax.ppermute(
            lax.slice_in_dim(block, block.shape[dim] - width, None, axis=dim), axis, forward
        )
        high = lax.ppermute(lax.slice_in_dim(block, 0, width, axis=dim), axis, backward)
        block = jnp.concatenate([low, block, high], axis=dim)
    return block


def laplace_rows(field):
    center = field[:, 1:-1, :]
    return (
        jnp.roll(center, 1, 2)
        + jnp.roll(center, -1, 2)
        + field[:, 2:, :]
        + field[:, :-2, :]
        - 4.0 * center
    )


def ocean_core(padded, wet_mask, lat_start, total_lat):
    speed_u, speed_v, temper, salty = (padded[0], padded[1], padded[2], padded[3])
    east_mid = speed_u[:, 1:-1, :]
    north_mid = speed_v[:, 1:-1, :]
    temp_mid = temper[:, 1:-1, :]
    salt_mid = salty[:, 1:-1, :]
    pressure = gravity * jnp.cumsum(haline_coef * salty - therm_coef * temper, axis=0)
    press_mid = pressure[:, 1:-1, :]
    row_index = (lat_start + jnp.arange(wet_mask.shape[1], dtype=jnp.int32)).astype(jnp.float32)
    spin_rate = (coriolis * (2.0 * (row_index + 0.5) / total_lat - 1.0))[None, :, None]
    slope_east = 0.5 * (jnp.roll(press_mid, -1, 2) - jnp.roll(press_mid, 1, 2))
    slope_north = 0.5 * (pressure[:, 2:, :] - pressure[:, :-2, :])
    new_u = wet_mask * (
        east_mid
        + time_step * (spin_rate * north_mid - slope_east + viscosity * laplace_rows(speed_u))
    )
    new_v = wet_mask * (
        north_mid
        + time_step * (-spin_rate * east_mid - slope_north + viscosity * laplace_rows(speed_v))
    )
    new_s = wet_mask * (salt_mid + time_step * salt_diff * laplace_rows(salty))
    part_t = temp_mid + time_step * heat_diff * laplace_rows(temper)
    spread = 0.5 * (jnp.roll(east_mid, -1, 2) - jnp.roll(east_mid, 1, 2)) + 0.5 * (
        speed_v[:, 2:, :] - speed_v[:, :-2, :]
    )
    rise_flux = -vert_ratio * jnp.flip(jnp.cumsum(jnp.flip(spread, 0), axis=0), 0)
    fluxes = jnp.stack([east_mid, north_mid, rise_flux])
    return (new_u, new_v, part_t, new_s, fluxes)


def light_field(plankton):
    chloro = jax.nn.softplus(plankton)
    attenuate = water_atten + chl_atten * chloro
    depth = jnp.cumsum(attenuate, axis=0) - attenuate
    row_index = jnp.arange(plankton.shape[-1], dtype=jnp.int32).astype(jnp.float32)
    place = 2.0 * (row_index + 0.5) / plankton.shape[-1] - 1.0
    surface = 1.0 - 0.5 * place * place
    top_light = surface * jnp.exp(-depth)
    return (chloro, top_light, top_light * (1.0 - jnp.exp(-attenuate)))


def tracer_core(tracer_ext, flux_ext, sea_mask, onehot, rate_table):
    center = tracer_ext[:, :, 1:-1, :]
    east_face = 0.5 * (flux_ext[0, :, :-1, :] + flux_ext[0, :, 1:, :])
    across = (
        jnp.maximum(east_face, 0.0) * tracer_ext[:, :, :-1, :]
        + jnp.minimum(east_face, 0.0) * tracer_ext[:, :, 1:, :]
    )
    div_east = across[:, :, 1:, :] - across[:, :, :-1, :]
    north_speed = flux_ext[1, :, 1:-1, :]
    north_face = 0.5 * (north_speed[:, :, :-1] + north_speed[:, :, 1:])
    along = (
        jnp.maximum(north_face, 0.0) * center[..., :-1]
        + jnp.minimum(north_face, 0.0) * center[..., 1:]
    )
    along = jnp.pad(along, ((0, 0), (0, 0), (0, 0), (1, 1)))
    div_north = along[..., 1:] - along[..., :-1]
    rise_face = flux_ext[2, 1:, 1:-1, :]
    upward = (
        jnp.maximum(rise_face, 0.0) * center[:, 1:] + jnp.minimum(rise_face, 0.0) * center[:, :-1]
    )
    upward = jnp.pad(upward, ((0, 0), (1, 1), (0, 0), (0, 0)))
    div_up = upward[:, :-1] - upward[:, 1:]
    side = jnp.pad(center, ((0, 0), (0, 0), (0, 0), (1, 1)))
    diffuse = (
        tracer_ext[:, :, 2:, :]
        + tracer_ext[:, :, :-2, :]
        + side[..., 2:]
        + side[..., :-2]
        - 4.0 * center
    )
    chloro, top_light, absorbed = light_field(center[0])
    nutrient = center[1] * center[1]
    uptake = growth_rate * top_light * chloro * nutrient / (1.0 + nutrient)
    rate_cell = jnp.einsum("bst,bij->stij", rate_table, onehot, precision=lax.Precision.HIGHEST)
    reaction = jnp.einsum("stij,tkij->skij", rate_cell, center, precision=lax.Precision.HIGHEST)
    reaction = reaction.at[0].add(uptake).at[1].add(-uptake)
    tendency = tracer_diff * diffuse + reaction - (div_east + div_north + div_up)
    return sea_mask[None] * (center + tracer_step * tendency)


def general_shards(ocean_state, bottom, tracers, land_sea, biome_id, rate_table):
    levels = ocean_state.shape[1]
    lat_rows = ocean_state.shape[2]
    lat_count = lax.axis_size("lat")
    total_lat = lat_rows * lat_count
    lat_start = lax.axis_index("lat") * lat_rows
    wet_mask = (jnp.arange(levels, dtype=jnp.int32)[:, None, None] < bottom[None]).astype(
        jnp.float32
    )
    sea_mask = land_sea.astype(jnp.float32)
    onehot = (
        biome_id[None] == jnp.arange(rate_table.shape[0], dtype=jnp.int32)[:, None, None]
    ).astype(jnp.float32)
    state = ocean_state
    tracer_now = tracers
    for cycle_index in range(STEPS):
        state = state * wet_mask[None]
        padded = extended(state, (("lat", 2),), 1, False)
        new_u, new_v, part_t, new_s, fluxes = ocean_core(padded, wet_mask, lat_start, total_lat)
        flux_t = lax.all_to_all(
            jnp.transpose(fluxes, (0, 1, 3, 2)), "lat", split_axis=2, concat_axis=3, tiled=True
        )
        tracer_now = tracer_now * sea_mask[None]
        flux_ext = extended(flux_t, (("lat", 2),), 1, True)
        for sub_index in range(SUB):
            tracer_ext = extended(tracer_now, (("lat", 2),), 1, True)
            tracer_now = tracer_core(tracer_ext, flux_ext, sea_mask, onehot, rate_table)
        heating = heat_gain * sea_mask * light_field(tracer_now[0])[2]
        heat_ocean = jnp.transpose(
            lax.all_to_all(heating, "lat", split_axis=2, concat_axis=1, tiled=True), (0, 2, 1)
        )
        new_t = wet_mask * (part_t + time_step * heat_ocean)
        state = jnp.stack([new_u, new_v, new_t, new_s])
    return (state, tracer_now)


HALO = STEPS * SUB
LANES = 128
TILE = 8
FIELDS = 4


def fits(ocean_state, tracers, rate_table, lat_count):
    _, levels, lat_rows, total_lon = ocean_state.shape
    species, _, columns, total_lat = tracers.shape
    return (
        lat_rows == 2
        and HALO == TILE // 2
        and lat_rows * lat_count == total_lat
        and columns * lat_count == total_lon
        and columns % TILE == 0
        and LANES % total_lat == 0
        and (columns + 2 * HALO) * total_lat == TILE * LANES
        and 2 * FIELDS * levels == LANES
        and levels <= columns + HALO
        and 2 * columns + 3 * HALO <= FIELDS * levels
        and species == 2 * TILE
        and levels % (LANES // total_lat) == 0
    )


def rows_of(shape=(TILE, LANES)):
    return lax.broadcasted_iota(jnp.int32, shape, 0)


def lanes_of(shape=(TILE, LANES)):
    return lax.broadcasted_iota(jnp.int32, shape, 1)


def spin(block, amount, axis):
    size = block.shape[axis]
    amount = amount % size
    return block if amount == 0 else pltpu.roll(block, amount, axis)


def swap_halves(block):
    low_row, low_lane = rows_of() < TILE // 2, lanes_of() < LANES // 2
    other = spin(spin(block, LANES // 2, 1), TILE // 2, 0)
    return jnp.where(low_row == low_lane, block, other)


def pack_ocean(ocean_ref, bottom_ref, out_ref, flat, depth):
    fields, levels, lat_rows, total_lon = ocean_ref.shape
    half = fields * levels
    count = out_ref.shape[0] // (4 * TILE)
    columns = total_lon // count
    own = columns // TILE
    for index in range(half):
        field, level = divmod(index, levels)
        for row in range(lat_rows):
            flat[row * half + index : row * half + index + 1, :] = ocean_ref[field, level, row : row + 1, :]
    turned = flat[...].T
    tiles = [turned[TILE * i : TILE * (i + 1), :] for i in range(total_lon // TILE)]
    swapped = [swap_halves(t) for t in tiles]
    depth[...] = jnp.zeros(depth.shape, jnp.float32)
    depth[3:4, :] = bottom_ref[0:1, :].astype(jnp.float32)
    depth[7:8, :] = bottom_ref[1:2, :].astype(jnp.float32)
    line = depth[...]
    row, lane = rows_of(), lanes_of()
    width = columns + 2 * HALO
    window = (row % 4 == 3) & (lane >= width - HALO) & (lane < 2 * width - HALO)
    for target in range(count):
        for q in range(own):
            out_ref[pl.ds((target * (own + 1) + q) * TILE, TILE), :] = swapped[target * own + q]
        east = tiles[(target * own + own) % len(tiles)]
        west = tiles[target * own - 1]
        edge = swap_halves(jnp.where(row < HALO, east, west))
        level_line = spin(line, width - target * columns, 1)[:, :LANES]
        out_ref[pl.ds((target * (own + 1) + own) * TILE, TILE), :] = jnp.where(window, level_line, edge)


def pack_edges(tracer_ref, sea_ref, biome_ref, west_ref, east_ref):
    species, levels, columns, total_lat = tracer_ref.shape
    blocks = LANES // total_lat
    groups = levels // blocks
    low = rows_of((TILE, total_lat)) < HALO
    last = columns - TILE
    for group in range(groups):
        wet = [
            jnp.where(low, sea_ref[group * blocks + b, 0:TILE, :], sea_ref[group * blocks + b, last:columns, :]).astype(
                jnp.float32
            )
            for b in range(blocks)
        ]
        joined = jnp.concatenate(wet, axis=1)
        start = species * groups * HALO + group * HALO
        west_ref[start : start + HALO, :] = joined[:HALO, :]
        east_ref[start : start + HALO, :] = joined[HALO:, :]
        for kind in range(species):
            parts = [
                jnp.where(
                    low,
                    tracer_ref[kind, group * blocks + b, 0:TILE, :],
                    tracer_ref[kind, group * blocks + b, last:columns, :],
                )
                for b in range(blocks)
            ]
            both = jnp.concatenate(parts, axis=1) * joined
            start = (kind * groups + group) * HALO
            west_ref[start : start + HALO, :] = both[:HALO, :]
            east_ref[start : start + HALO, :] = both[HALO:, :]
    biome = jnp.where(low, biome_ref[0:TILE, :], biome_ref[last:columns, :]).astype(jnp.float32)
    biome = jnp.concatenate([biome] * blocks, axis=1)
    start = (species + 1) * groups * HALO
    west_ref[start : start + 2 * HALO, :] = biome
    east_ref[start : start + 2 * HALO, :] = spin(biome, HALO, 0)


def light(plankton, surface):
    result = []
    depth = jnp.zeros(surface.shape, jnp.float32)
    for value in plankton:
        chloro = jnp.maximum(value, 0.0) + jnp.log1p(jnp.exp(-jnp.abs(value)))
        attenuate = water_atten + chl_atten * chloro
        result.append((chloro, surface * jnp.exp(-depth), attenuate))
        depth = depth + attenuate
    return result


def surface_light(total_lat):
    row_index = (lanes_of() % total_lat).astype(jnp.float32)
    place = 2.0 * (row_index + 0.5) / total_lat - 1.0
    return 1.0 - 0.5 * place * place


def planes_of(ref, kind, levels, species, base=0):
    return [ref[pl.ds(base + level * TILE * species + kind, TILE, stride=species), :] for level in range(levels)]


def put_growth(growth_ref, tracer_ref, levels, species, total_lat, base=0):
    lit = light(planes_of(tracer_ref, 0, levels, species, base), surface_light(total_lat))
    food = planes_of(tracer_ref, 1, levels, species, base)
    for level, (chloro, top_light, _) in enumerate(lit):
        nutrient = food[level] * food[level]
        uptake = growth_rate * top_light * chloro * nutrient / (1.0 + nutrient)
        growth_ref[level * TILE : (level + 1) * TILE, :] = tracer_step * uptake
    return lit


def spread_row(ref, index):
    return ref[pl.ds(index, TILE, stride=0), :]


def reaction(source_ref, base, rate_ref, growth_ref, row, levels, species):
    sums = [[None, None] for _ in levels]
    for kind in range(species):
        rates = [
            rate_ref[pl.ds((row * species + kind) * species + TILE * part, TILE), :] for part in range(2)
        ]
        for place, level in enumerate(levels):
            value = spread_row(source_ref, base + (level * TILE + row) * species + kind)
            for part in range(2):
                term = rates[part] * value
                sums[place][part] = term if sums[place][part] is None else sums[place][part] + term
    index = rows_of()
    sign = jnp.where(index == 0, 1.0, jnp.where(index == 1, -1.0, 0.0))
    for place, level in enumerate(levels):
        sums[place][0] = sums[place][0] + sign * spread_row(growth_ref, level * TILE + row)
    return sums


def prepare(tracer_ref, sea_ref, biome_ref, rate_table_ref, from_west, from_east, now_ref, wet_ref, rate_ref, first_ref, growth, rate_columns):
    species, levels, columns, total_lat = tracer_ref.shape
    kinds = rate_table_ref.shape[0]
    blocks = LANES // total_lat
    groups = levels // blocks
    own = columns // TILE

    def halo(start):
        return jnp.concatenate([from_east[start : start + HALO, :], from_west[start : start + HALO, :]], axis=0)

    def plane(parts, edge, block):
        return jnp.concatenate(parts + [edge[:, block * total_lat : (block + 1) * total_lat]], axis=1)

    for group in range(groups):
        edge = halo((species * groups + group) * HALO)
        for block in range(blocks):
            level = group * blocks + block
            parts = [sea_ref[level, TILE * q : TILE * (q + 1), :].astype(jnp.float32) for q in range(own)]
            wet_ref[level * TILE : (level + 1) * TILE, :] = plane(parts, edge, block)
    for kind in range(species):
        for group in range(groups):
            edge = halo((kind * groups + group) * HALO)
            for block in range(blocks):
                level = group * blocks + block
                parts = [tracer_ref[kind, level, TILE * q : TILE * (q + 1), :] for q in range(own)]
                whole = plane(parts, edge, block) * wet_ref[level * TILE : (level + 1) * TILE, :]
                now_ref[pl.ds(level * TILE * species + kind, TILE, stride=species), :] = whole
    start = (species + 1) * groups * HALO
    parts = [biome_ref[TILE * q : TILE * (q + 1), :].astype(jnp.float32) for q in range(own)]
    biome = plane(parts, halo(start), 0)
    for b in range(kinds):
        for kind in range(species):
            for part in range(2):
                column = rate_table_ref[b, TILE * part : TILE * (part + 1), kind : kind + 1]
                rate_columns[pl.ds(((b * species + kind) * 2 + part) * TILE, TILE), :] = tracer_step * jnp.broadcast_to(column, (TILE, LANES))
    for row in range(TILE):
        here = jnp.broadcast_to(biome[row : row + 1, :], (TILE, LANES))
        chosen = [here == float(b) for b in range(kinds)]
        for kind in range(species):
            for part in range(2):
                rate = jnp.zeros((TILE, LANES), jnp.float32)
                for b in range(kinds):
                    rate = jnp.where(chosen[b], rate_columns[pl.ds(((b * species + kind) * 2 + part) * TILE, TILE), :], rate)
                rate_ref[pl.ds((row * species + kind) * species + TILE * part, TILE), :] = rate
    put_growth(growth, now_ref, levels, species, total_lat)

    def react(group, carry):
        near = [group * 4 + i for i in range(4)]
        for row in range(TILE):
            for level, sums in zip(near, reaction(now_ref, 0, rate_ref, growth, row, near, species), strict=True):
                for part in range(2):
                    first_ref[pl.ds((level * TILE + row) * species + TILE * part, TILE), :] = sums[part]
        return carry

    lax.fori_loop(0, levels // 4, react, 0)


def advance(received, now_ref, wet_ref, rate_ref, first_ref, sent, last_ref, work, ocean, coef, tracer, growth, sizes):
    levels, species, total_lat, columns = sizes
    count = total_lat // 2
    own = columns // TILE
    half = FIELDS * levels
    row, lane = rows_of(), lanes_of()
    lat = lane % total_lat
    width = columns + 2 * HALO

    for r_low in range(4):
        for q in range(own + 1):
            for j in range(2):
                work[pl.ds(r_low * LANES + q * total_lat + j, count, stride=2), :] = received[
                    pl.ds(q * TILE + j * 4 + r_low, count, stride=(own + 1) * TILE), :
                ]
    turned = None
    for r_low in range(4):
        turned = work[r_low * LANES : (r_low + 1) * LANES, :].T
        for r_high in range(2):
            ocean[pl.ds(r_high * 4 + r_low, half, stride=TILE), :] = turned[r_high * half : (r_high + 1) * half, :]
    floors = [turned[width + TILE * q : width + TILE * (q + 1), :] for q in range(own)]
    floors.append(
        jnp.where(row < HALO, turned[width + columns : width + columns + TILE, :], turned[width - TILE : width, :])
    )
    floor = floors[own]
    for q in range(own):
        floor = jnp.where(lane // total_lat == q, spin(floors[q], (q - own) * total_lat, 1), floor)
    wet = [(float(level) < floor).astype(jnp.float32) for level in range(levels)]
    sea = [wet_ref[level * TILE : (level + 1) * TILE, :] for level in range(levels)]

    def read(field):
        return [ocean[(field * levels + k) * TILE : (field * levels + k + 1) * TILE, :] for k in range(levels)]

    def write(field, values):
        for k in range(levels):
            ocean[(field * levels + k) * TILE : (field * levels + k + 1) * TILE, :] = values[k]

    def east(x):
        y = spin(x, -1, 0)
        return jnp.where(row == TILE - 1, spin(y, -total_lat, 1), y)

    def west(x):
        y = spin(x, 1, 0)
        return jnp.where(row == 0, spin(y, total_lat, 1), y)

    def north(x):
        return jnp.where(lat == total_lat - 1, 0.0, spin(x, -1, 1))

    def south(x):
        return jnp.where(lat == 0, 0.0, spin(x, 1, 1))

    spin_rate = coriolis * (2.0 * (lat.astype(jnp.float32) + 0.5) / total_lat - 1.0)
    plane = levels * TILE

    def dynamics(step):
        speed_u, speed_v, temper, salty = read(0), read(1), read(2), read(3)
        spread, new_u, new_v = [], [], []
        pressure = None
        for k in range(levels):
            u, v = speed_u[k], speed_v[k]
            part = gravity * (haline_coef * salty[k] - therm_coef * temper[k])
            pressure = part if pressure is None else pressure + part
            slope_east = 0.5 * (east(pressure) - west(pressure))
            slope_north = 0.5 * (north(pressure) - south(pressure))
            u_east, u_west, v_north, v_south = east(u), west(u), north(v), south(v)
            lap_u = u_east + u_west + north(u) + south(u) - 4.0 * u
            lap_v = east(v) + west(v) + v_north + v_south - 4.0 * v
            new_u.append(wet[k] * (u + time_step * (spin_rate * v - slope_east + viscosity * lap_u)))
            new_v.append(wet[k] * (v + time_step * (-spin_rate * u - slope_north + viscosity * lap_v)))
            spread.append(0.5 * (u_east - u_west) + 0.5 * (v_north - v_south))
            face_east = 0.5 * (u + u_east)
            face_north = jnp.where(lat == total_lat - 1, 0.0, 0.5 * (v + v_north))
            up_east, down_east = jnp.maximum(face_east, 0.0), jnp.minimum(face_east, 0.0)
            up_north, down_north = jnp.maximum(face_north, 0.0), jnp.minimum(face_north, 0.0)
            mask = tracer_step * sea[k]
            at = step * 7 * plane + k * TILE
            coef[pl.ds(at + plane, TILE), :] = mask * (tracer_diff - down_east)
            coef[pl.ds(at + 2 * plane, TILE), :] = mask * (tracer_diff + west(up_east))
            coef[pl.ds(at + 3 * plane, TILE), :] = jnp.where(
                lat == total_lat - 1, 0.0, mask * (tracer_diff - down_north)
            )
            coef[pl.ds(at + 4 * plane, TILE), :] = jnp.where(lat == 0, 0.0, mask * (tracer_diff + south(up_north)))
            coef[pl.ds(at, TILE), :] = -4.0 * tracer_diff - up_east + west(down_east) - up_north + south(down_north)
        total = jnp.zeros((TILE, LANES), jnp.float32)
        below_up, below_down = total, total
        for k in reversed(range(levels)):
            total = total + spread[k]
            rise = -vert_ratio * total if k > 0 else jnp.zeros((TILE, LANES), jnp.float32)
            up, down = jnp.maximum(rise, 0.0), jnp.minimum(rise, 0.0)
            mask = tracer_step * sea[k]
            at = step * 7 * plane + k * TILE
            coef[pl.ds(at, TILE), :] = sea[k] + mask * (coef[pl.ds(at, TILE), :] - up + below_down)
            coef[pl.ds(at + 5 * plane, TILE), :] = -mask * down
            coef[pl.ds(at + 6 * plane, TILE), :] = mask * below_up
            below_up, below_down = up, down
        for field, values, rate in ((2, temper, heat_diff), (3, salty, salt_diff)):
            fresh = []
            for k in range(levels):
                x = values[k]
                lap = east(x) + west(x) + north(x) + south(x) - 4.0 * x
                y = x + time_step * rate * lap
                fresh.append(wet[k] * y if field == 3 else y)
            write(field, fresh)
        write(0, new_u)
        write(1, new_v)

    def substep(step, source, base, target, target_base, ready):
        start = step * 7 * plane

        def body(group, carry):
            near = [group * 4 + i for i in range(4)]
            for r in range(TILE):
                if ready is None:
                    sums = reaction(source, base, rate_ref, growth, r, near, species)
                for place, level in enumerate(near):
                    cell = level * TILE + r
                    weight = [spread_row(coef, start + i * plane + cell) for i in range(7)]
                    mask = spread_row(wet_ref, cell)
                    above = jnp.maximum(level - 1, 0) * TILE + r
                    under = jnp.minimum(level + 1, levels - 1) * TILE + r
                    for part in range(2):

                        def take(index, part=part):
                            return source[pl.ds(base + index * species + TILE * part, TILE), :]

                        x = take(cell)
                        x_east = take(cell + 1) if r < TILE - 1 else spin(take(cell - r), -total_lat, 1)
                        x_west = take(cell - 1) if r > 0 else spin(take(cell + TILE - 1), total_lat, 1)
                        if ready is None:
                            change = sums[place][part]
                        else:
                            change = ready[pl.ds(cell * species + TILE * part, TILE), :]
                        value = (
                            (weight[0] * x + weight[1] * x_east)
                            + (weight[2] * x_west + weight[3] * spin(x, -1, 1))
                            + (weight[4] * spin(x, 1, 1) + weight[5] * take(above))
                            + (weight[6] * take(under) + mask * change)
                        )
                        target[pl.ds(target_base + cell * species + TILE * part, TILE), :] = value
            return carry

        lax.fori_loop(0, levels // 4, body, 0)

    for field in range(FIELDS):
        write(field, [wet[k] * x for k, x in enumerate(read(field))])
    size = levels * TILE * species
    source, base = now_ref, 0
    lit = None
    for step in range(STEPS):
        dynamics(step)
        for sub in range(SUB):
            last = step == STEPS - 1 and sub == SUB - 1
            first = step == 0 and sub == 0
            target, target_base = (last_ref, 0) if last else (tracer, ((step * SUB + sub) % 2) * size)
            if not first:
                put_growth(growth, source, levels, species, total_lat, base)
            substep(step, source, base, target, target_base, first_ref if first else None)
            source, base = target, target_base
        lit = light(planes_of(source, 0, levels, species, base), surface_light(total_lat))
        warm = []
        for k, x in enumerate(read(2)):
            _, top_light, attenuate = lit[k]
            heating = heat_gain * sea[k] * (top_light * (1.0 - jnp.exp(-attenuate)))
            warm.append(wet[k] * (x + time_step * heating))
        write(2, warm)

    for r_low in range(4):
        both = jnp.concatenate(
            [ocean[pl.ds(r_high * 4 + r_low, half, stride=TILE), :] for r_high in range(2)], axis=0
        )
        work[r_low * LANES : (r_low + 1) * LANES, :] = both.T
        for q in range(own):
            for j in range(2):
                sent[pl.ds(q * TILE + j * 4 + r_low, count, stride=own * TILE), :] = work[
                    pl.ds(r_low * LANES + q * total_lat + j, count, stride=2), :
                ]


def unpack_tracers(last_ref, out_ref):
    species, levels, columns, total_lat = out_ref.shape
    for level in range(levels):
        for kind in range(species):
            whole = last_ref[pl.ds(level * TILE * species + kind, TILE, stride=species), :]
            for q in range(columns // TILE):
                out_ref[kind, level, TILE * q : TILE * (q + 1), :] = whole[:, q * total_lat : (q + 1) * total_lat]


def unpack_ocean(received, out_ref, turned, flat):
    fields, levels, lat_rows, total_lon = out_ref.shape
    half = fields * levels
    for i in range(total_lon // TILE):
        turned[TILE * i : TILE * (i + 1), :] = swap_halves(received[TILE * i : TILE * (i + 1), :])
    flat[...] = turned[...].T
    for index in range(half):
        field, level = divmod(index, levels)
        for row in range(lat_rows):
            out_ref[field, level, row : row + 1, :] = flat[row * half + index : row * half + index + 1, :]


def grids(*shapes):
    return [pltpu.VMEM(shape, jnp.float32) for shape in shapes]


def real(*shape):
    return jax.ShapeDtypeStruct(shape, jnp.float32)


def shards(ocean_state, bottom, tracers, land_sea, biome_id, rate_table):
    count = lax.axis_size("lat")
    if not fits(ocean_state, tracers, rate_table, count):
        return general_shards(ocean_state, bottom, tracers, land_sea, biome_id, rate_table)
    _, levels, _, total_lon = ocean_state.shape
    species, _, columns, total_lat = tracers.shape
    cells = levels * TILE
    size = cells * species
    own = columns // TILE

    packed = pl.pallas_call(
        pack_ocean,
        out_shape=real(count * (own + 1) * TILE, LANES),
        scratch_shapes=grids((LANES, total_lon), (TILE, total_lon)),
        name="pack_ocean",
    )(ocean_state, bottom)
    received = lax.all_to_all(
        packed.reshape(count, (own + 1) * TILE, LANES), "lat", split_axis=0, concat_axis=0, tiled=True
    ).reshape(packed.shape)

    edge_rows = (species + 1) * (levels * total_lat // LANES) * HALO + 2 * HALO
    to_west, to_east = pl.pallas_call(
        pack_edges, out_shape=[real(edge_rows, LANES)] * 2, name="pack_edges"
    )(tracers, land_sea, biome_id)
    forward = [(i, (i + 1) % count) for i in range(count)]
    from_west = lax.ppermute(to_east, "lat", forward)
    from_east = lax.ppermute(to_west, "lat", [(b, a) for a, b in forward])

    now, wet, rates, first = pl.pallas_call(
        prepare,
        out_shape=[real(size, LANES), real(cells, LANES), real(TILE * species * species, LANES), real(size, LANES)],
        scratch_shapes=grids((cells, LANES), (rate_table.shape[0] * species * 2 * TILE, LANES)),
        name="prepare",
    )(tracers, land_sea, biome_id, rate_table, from_west, from_east)

    def run(*refs):
        advance(*refs, (levels, species, total_lat, columns))

    sent, last = pl.pallas_call(
        run,
        out_shape=[real(count * own * TILE, LANES), real(size, LANES)],
        scratch_shapes=grids(
            (4 * LANES, LANES),
            (FIELDS * cells, LANES),
            (STEPS * 7 * cells, LANES),
            (2 * size, LANES),
            (cells, LANES),
        ),
        name="advance",
    )(received, now, wet, rates, first)
    back = lax.all_to_all(
        sent.reshape(count, own * TILE, LANES), "lat", split_axis=0, concat_axis=0, tiled=True
    ).reshape(sent.shape)
    tracers_out = pl.pallas_call(
        unpack_tracers, out_shape=jax.ShapeDtypeStruct(tracers.shape, jnp.float32), name="unpack_tracers"
    )(last)
    state_out = pl.pallas_call(
        unpack_ocean,
        out_shape=jax.ShapeDtypeStruct(ocean_state.shape, jnp.float32),
        scratch_shapes=grids((total_lon, LANES), (LANES, total_lon)),
        name="unpack_ocean",
    )(back)
    return (state_out, tracers_out)


def solution(mesh):
    in_specs = (
        P(None, None, ("groups", "lat"), None),
        P(("groups", "lat"), None),
        P(None, None, ("groups", "lat"), None),
        P(None, ("groups", "lat"), None),
        P(("groups", "lat"), None),
        P(),
    )
    out_specs = (P(None, None, ("groups", "lat"), None), P(None, None, ("groups", "lat"), None))
    return jax.shard_map(shards, mesh=mesh, in_specs=in_specs, out_specs=out_specs, check_vma=False)
```

```python
import jax
import jax.numpy as jnp
from jax import lax
from jax.experimental import pallas as pl
from jax.experimental.pallas import tpu as pltpu
from jax.sharding import PartitionSpec as P


STEPS = 2
SUB = 2


time_step = 0.1
viscosity = 0.1
heat_diff = 0.08
salt_diff = 0.06
therm_coef = 0.2
haline_coef = 0.15
gravity = 0.5
coriolis = 0.6
vert_ratio = 0.25
tracer_step = 0.1
tracer_diff = 0.1
water_atten = 0.04
chl_atten = 0.05
growth_rate = 0.8
heat_gain = 10.0


def extended(block, sides, width, periodic):
    for axis, dim in sides:
        count = lax.axis_size(axis)
        forward = [(i, i + 1) for i in range(count - 1)]
        if periodic:
            forward.append((count - 1, 0))
        backward = [(target, source) for source, target in forward]
        low = lax.ppermute(
            lax.slice_in_dim(block, block.shape[dim] - width, None, axis=dim), axis, forward
        )
        high = lax.ppermute(lax.slice_in_dim(block, 0, width, axis=dim), axis, backward)
        block = jnp.concatenate([low, block, high], axis=dim)
    return block


def laplace_rows(field):
    center = field[:, 1:-1, :]
    return (
        jnp.roll(center, 1, 2)
        + jnp.roll(center, -1, 2)
        + field[:, 2:, :]
        + field[:, :-2, :]
        - 4.0 * center
    )


def ocean_core(padded, wet_mask, lat_start, total_lat):
    speed_u, speed_v, temper, salty = (padded[0], padded[1], padded[2], padded[3])
    east_mid = speed_u[:, 1:-1, :]
    north_mid = speed_v[:, 1:-1, :]
    temp_mid = temper[:, 1:-1, :]
    salt_mid = salty[:, 1:-1, :]
    pressure = gravity * jnp.cumsum(haline_coef * salty - therm_coef * temper, axis=0)
    press_mid = pressure[:, 1:-1, :]
    row_index = (lat_start + jnp.arange(wet_mask.shape[1], dtype=jnp.int32)).astype(jnp.float32)
    spin_rate = (coriolis * (2.0 * (row_index + 0.5) / total_lat - 1.0))[None, :, None]
    slope_east = 0.5 * (jnp.roll(press_mid, -1, 2) - jnp.roll(press_mid, 1, 2))
    slope_north = 0.5 * (pressure[:, 2:, :] - pressure[:, :-2, :])
    new_u = wet_mask * (
        east_mid
        + time_step * (spin_rate * north_mid - slope_east + viscosity * laplace_rows(speed_u))
    )
    new_v = wet_mask * (
        north_mid
        + time_step * (-spin_rate * east_mid - slope_north + viscosity * laplace_rows(speed_v))
    )
    new_s = wet_mask * (salt_mid + time_step * salt_diff * laplace_rows(salty))
    part_t = temp_mid + time_step * heat_diff * laplace_rows(temper)
    spread = 0.5 * (jnp.roll(east_mid, -1, 2) - jnp.roll(east_mid, 1, 2)) + 0.5 * (
        speed_v[:, 2:, :] - speed_v[:, :-2, :]
    )
    rise_flux = -vert_ratio * jnp.flip(jnp.cumsum(jnp.flip(spread, 0), axis=0), 0)
    fluxes = jnp.stack([east_mid, north_mid, rise_flux])
    return (new_u, new_v, part_t, new_s, fluxes)


def light_field(plankton):
    chloro = jax.nn.softplus(plankton)
    attenuate = water_atten + chl_atten * chloro
    depth = jnp.cumsum(attenuate, axis=0) - attenuate
    row_index = jnp.arange(plankton.shape[-1], dtype=jnp.int32).astype(jnp.float32)
    place = 2.0 * (row_index + 0.5) / plankton.shape[-1] - 1.0
    surface = 1.0 - 0.5 * place * place
    top_light = surface * jnp.exp(-depth)
    return (chloro, top_light, top_light * (1.0 - jnp.exp(-attenuate)))


def tracer_core(tracer_ext, flux_ext, sea_mask, onehot, rate_table):
    center = tracer_ext[:, :, 1:-1, :]
    east_face = 0.5 * (flux_ext[0, :, :-1, :] + flux_ext[0, :, 1:, :])
    across = (
        jnp.maximum(east_face, 0.0) * tracer_ext[:, :, :-1, :]
        + jnp.minimum(east_face, 0.0) * tracer_ext[:, :, 1:, :]
    )
    div_east = across[:, :, 1:, :] - across[:, :, :-1, :]
    north_speed = flux_ext[1, :, 1:-1, :]
    north_face = 0.5 * (north_speed[:, :, :-1] + north_speed[:, :, 1:])
    along = (
        jnp.maximum(north_face, 0.0) * center[..., :-1]
        + jnp.minimum(north_face, 0.0) * center[..., 1:]
    )
    along = jnp.pad(along, ((0, 0), (0, 0), (0, 0), (1, 1)))
    div_north = along[..., 1:] - along[..., :-1]
    rise_face = flux_ext[2, 1:, 1:-1, :]
    upward = (
        jnp.maximum(rise_face, 0.0) * center[:, 1:] + jnp.minimum(rise_face, 0.0) * center[:, :-1]
    )
    upward = jnp.pad(upward, ((0, 0), (1, 1), (0, 0), (0, 0)))
    div_up = upward[:, :-1] - upward[:, 1:]
    side = jnp.pad(center, ((0, 0), (0, 0), (0, 0), (1, 1)))
    diffuse = (
        tracer_ext[:, :, 2:, :]
        + tracer_ext[:, :, :-2, :]
        + side[..., 2:]
        + side[..., :-2]
        - 4.0 * center
    )
    chloro, top_light, _ = light_field(center[0])
    nutrient = center[1] * center[1]
    uptake = growth_rate * top_light * chloro * nutrient / (1.0 + nutrient)
    rate_cell = jnp.einsum("bst,bij->stij", rate_table, onehot, precision=lax.Precision.HIGHEST)
    reaction = jnp.einsum("stij,tkij->skij", rate_cell, center, precision=lax.Precision.HIGHEST)
    reaction = reaction.at[0].add(uptake).at[1].add(-uptake)
    tendency = tracer_diff * diffuse + reaction - (div_east + div_north + div_up)
    return sea_mask[None] * (center + tracer_step * tendency)


def general_shards(ocean_state, bottom, tracers, land_sea, biome_id, rate_table):
    levels = ocean_state.shape[1]
    lat_rows = ocean_state.shape[2]
    lat_count = lax.axis_size("lat")
    total_lat = lat_rows * lat_count
    lat_start = lax.axis_index("lat") * lat_rows
    wet_mask = (jnp.arange(levels, dtype=jnp.int32)[:, None, None] < bottom[None]).astype(
        jnp.float32
    )
    sea_mask = land_sea.astype(jnp.float32)
    onehot = (
        biome_id[None] == jnp.arange(rate_table.shape[0], dtype=jnp.int32)[:, None, None]
    ).astype(jnp.float32)
    state = ocean_state
    tracer_now = tracers
    for _ in range(STEPS):
        state = state * wet_mask[None]
        padded = extended(state, (("lat", 2),), 1, False)
        new_u, new_v, part_t, new_s, fluxes = ocean_core(padded, wet_mask, lat_start, total_lat)
        flux_t = lax.all_to_all(
            jnp.transpose(fluxes, (0, 1, 3, 2)), "lat", split_axis=2, concat_axis=3, tiled=True
        )
        tracer_now = tracer_now * sea_mask[None]
        flux_ext = extended(flux_t, (("lat", 2),), 1, True)
        for _ in range(SUB):
            tracer_ext = extended(tracer_now, (("lat", 2),), 1, True)
            tracer_now = tracer_core(tracer_ext, flux_ext, sea_mask, onehot, rate_table)
        heating = heat_gain * sea_mask * light_field(tracer_now[0])[2]
        heat_ocean = jnp.transpose(
            lax.all_to_all(heating, "lat", split_axis=2, concat_axis=1, tiled=True), (0, 2, 1)
        )
        new_t = wet_mask * (part_t + time_step * heat_ocean)
        state = jnp.stack([new_u, new_v, new_t, new_s])
    return (state, tracer_now)


HALO = STEPS * SUB
LANES = 128
TILE = 8
FIELDS = 4
GRANT = 16 * 1024 * 1024


def fits(ocean_state, tracers, lat_count):
    _, levels, lat_rows, total_lon = ocean_state.shape
    species, _, columns, total_lat = tracers.shape
    return (
        lat_rows == 2
        and HALO == TILE // 2
        and lat_rows * lat_count == total_lat
        and columns * lat_count == total_lon
        and columns % TILE == 0
        and LANES % total_lat == 0
        and (columns + 2 * HALO) * total_lat == TILE * LANES
        and 2 * FIELDS * levels == LANES
        and levels <= columns + HALO
        and 2 * columns + 3 * HALO <= FIELDS * levels
        and species == 2 * TILE
        and levels % (LANES // total_lat) == 0
    )


def rows_of(shape=(TILE, LANES)):
    return lax.broadcasted_iota(jnp.int32, shape, 0)


def lanes_of(shape=(TILE, LANES)):
    return lax.broadcasted_iota(jnp.int32, shape, 1)


def spin(block, amount, axis):
    size = block.shape[axis]
    amount = amount % size
    return block if amount == 0 else pltpu.roll(block, amount, axis)


def swap_halves(block):
    low_row, low_lane = rows_of() < TILE // 2, lanes_of() < LANES // 2
    other = spin(spin(block, LANES // 2, 1), TILE // 2, 0)
    return jnp.where(low_row == low_lane, block, other)


def pack_ocean(ocean_ref, bottom_ref, out_ref, flat, depth):
    fields, levels, lat_rows, total_lon = ocean_ref.shape
    half = fields * levels
    count = out_ref.shape[0] // (4 * TILE)
    columns = total_lon // count
    own = columns // TILE
    for index in range(half):
        field, level = divmod(index, levels)
        for row in range(lat_rows):
            flat[row * half + index : row * half + index + 1, :] = ocean_ref[field, level, row : row + 1, :]
    turned = flat[...].T
    tiles = [turned[TILE * i : TILE * (i + 1), :] for i in range(total_lon // TILE)]
    swapped = [swap_halves(t) for t in tiles]
    depth[...] = jnp.zeros(depth.shape, jnp.float32)
    depth[3:4, :] = bottom_ref[0:1, :].astype(jnp.float32)
    depth[7:8, :] = bottom_ref[1:2, :].astype(jnp.float32)
    line = depth[...]
    row, lane = rows_of(), lanes_of()
    width = columns + 2 * HALO
    window = (row % 4 == 3) & (lane >= width - HALO) & (lane < 2 * width - HALO)
    for target in range(count):
        for q in range(own):
            out_ref[pl.ds((target * (own + 1) + q) * TILE, TILE), :] = swapped[target * own + q]
        east = tiles[(target * own + own) % len(tiles)]
        west = tiles[target * own - 1]
        edge = swap_halves(jnp.where(row < HALO, east, west))
        level_line = spin(line, width - target * columns, 1)[:, :LANES]
        out_ref[pl.ds((target * (own + 1) + own) * TILE, TILE), :] = jnp.where(window, level_line, edge)


def pack_edges(tracer_ref, sea_ref, biome_ref, west_ref, east_ref):
    species, levels, columns, total_lat = tracer_ref.shape
    blocks = LANES // total_lat
    groups = levels // blocks
    low = rows_of((TILE, total_lat)) < HALO
    last = columns - TILE
    for group in range(groups):
        wet = [
            jnp.where(low, sea_ref[group * blocks + b, 0:TILE, :], sea_ref[group * blocks + b, last:columns, :]).astype(
                jnp.float32
            )
            for b in range(blocks)
        ]
        joined = jnp.concatenate(wet, axis=1)
        start = species * groups * HALO + group * HALO
        west_ref[start : start + HALO, :] = joined[:HALO, :]
        east_ref[start : start + HALO, :] = joined[HALO:, :]
        for kind in range(species):
            parts = [
                jnp.where(
                    low,
                    tracer_ref[kind, group * blocks + b, 0:TILE, :],
                    tracer_ref[kind, group * blocks + b, last:columns, :],
                )
                for b in range(blocks)
            ]
            both = jnp.concatenate(parts, axis=1) * joined
            start = (kind * groups + group) * HALO
            west_ref[start : start + HALO, :] = both[:HALO, :]
            east_ref[start : start + HALO, :] = both[HALO:, :]
    biome = jnp.where(low, biome_ref[0:TILE, :], biome_ref[last:columns, :]).astype(jnp.float32)
    biome = jnp.concatenate([biome] * blocks, axis=1)
    start = (species + 1) * groups * HALO
    west_ref[start : start + 2 * HALO, :] = biome
    east_ref[start : start + 2 * HALO, :] = spin(biome, HALO, 0)


def fetch(sources, targets, ready):
    copies = [pltpu.make_async_copy(a, b, ready.at[i]) for i, (a, b) in enumerate(zip(sources, targets, strict=True))]
    for copy in copies:
        copy.start()
    return copies


def pack(*refs):
    sources, (packed_ref, west_ref, east_ref), (flat, depth) = refs[:5], refs[5:8], refs[8:10]
    held, ready = refs[10:15], refs[15]
    copies = fetch(sources, held, ready)
    copies[0].wait()
    copies[1].wait()
    pack_ocean(held[0], held[1], packed_ref, flat, depth)
    for copy in copies[2:]:
        copy.wait()
    pack_edges(held[2], held[3], held[4], west_ref, east_ref)


def prepare_from(*refs):
    sources, edges, outs, held, growth, ready = refs[:4], refs[4:6], refs[6:11], refs[11:15], refs[15], refs[16]
    for copy in fetch(sources, held, ready):
        copy.wait()
    prepare(*held, *edges, *outs, growth)


def light(plankton, surface):
    result = []
    depth = jnp.zeros(surface.shape, jnp.float32)
    for value in plankton:
        chloro = jnp.maximum(value, 0.0) + jnp.log1p(jnp.exp(-jnp.abs(value)))
        attenuate = water_atten + chl_atten * chloro
        result.append((chloro, surface * jnp.exp(-depth), attenuate))
        depth = depth + attenuate
    return result


def surface_light(total_lat):
    row_index = (lanes_of() % total_lat).astype(jnp.float32)
    place = 2.0 * (row_index + 0.5) / total_lat - 1.0
    return 1.0 - 0.5 * place * place


def planes_of(ref, kind, levels, species, base=0):
    return [ref[pl.ds(base + level * TILE * species + kind, TILE, stride=species), :] for level in range(levels)]


def put_growth(growth_ref, tracer_ref, levels, species, total_lat, base=0):
    lit = light(planes_of(tracer_ref, 0, levels, species, base), surface_light(total_lat))
    food = planes_of(tracer_ref, 1, levels, species, base)
    for level, (chloro, top_light, _) in enumerate(lit):
        nutrient = food[level] * food[level]
        uptake = growth_rate * top_light * chloro * nutrient / (1.0 + nutrient)
        growth_ref[level * TILE : (level + 1) * TILE, :] = tracer_step * uptake
    return lit


def rate_pieces(rate_table_ref):
    kinds, species, _ = rate_table_ref.shape
    rates = tracer_step * rate_table_ref[...].reshape(kinds * species, species)
    high = rates.astype(jnp.bfloat16)
    low = (rates - high.astype(jnp.float32)).astype(jnp.bfloat16)
    return jnp.concatenate([high, low, high], axis=1)


def reaction(source_ref, base, pieces, chosen, growth_ref, row, levels, species):
    index = rows_of((species, LANES))
    sign = jnp.where(index == 0, 1.0, jnp.where(index == 1, -1.0, 0.0))
    sums = []
    for pair in range(0, len(levels), 2):
        near = levels[pair : pair + 2]
        values = jnp.concatenate(
            [source_ref[pl.ds(base + (level * TILE + row) * species, species), :] for level in near], axis=1
        )
        high = values.astype(jnp.bfloat16)
        low = (values - high.astype(jnp.float32)).astype(jnp.bfloat16)
        every = jnp.dot(
            pieces, jnp.concatenate([high, high, low], axis=0), preferred_element_type=jnp.float32
        )
        for place, level in enumerate(near):
            mine = every[:, place * LANES : (place + 1) * LANES]
            total = mine[:species, :]
            for kind, mask in enumerate(chosen):
                total = jnp.where(mask, mine[(kind + 1) * species : (kind + 2) * species, :], total)
            uptake = growth_ref[pl.ds(level * TILE + row, species, stride=0), :]
            sums.append(total + sign * uptake)
    return sums


def biome_masks(biome_ref, row, kinds, species):
    here = jnp.broadcast_to(biome_ref[row : row + 1, :], (species, LANES))
    return [here == float(kind) for kind in range(1, kinds)]


def prepare(
    tracer_ref, sea_ref, biome_ref, rate_table_ref, from_west, from_east, now_ref, wet_ref, biomes_ref, pieces_ref,
    first_ref, growth,
):
    species, levels, columns, total_lat = tracer_ref.shape
    blocks = LANES // total_lat
    groups = levels // blocks
    own = columns // TILE

    def halo(start):
        return jnp.concatenate([from_east[start : start + HALO, :], from_west[start : start + HALO, :]], axis=0)

    def plane(parts, edge, block):
        return jnp.concatenate(parts + [edge[:, block * total_lat : (block + 1) * total_lat]], axis=1)

    for group in range(groups):
        edge = halo((species * groups + group) * HALO)
        for block in range(blocks):
            level = group * blocks + block
            parts = [sea_ref[level, TILE * q : TILE * (q + 1), :].astype(jnp.float32) for q in range(own)]
            wet_ref[level * TILE : (level + 1) * TILE, :] = plane(parts, edge, block)
    for kind in range(species):
        for group in range(groups):
            edge = halo((kind * groups + group) * HALO)
            for block in range(blocks):
                level = group * blocks + block
                parts = [tracer_ref[kind, level, TILE * q : TILE * (q + 1), :] for q in range(own)]
                whole = plane(parts, edge, block) * wet_ref[level * TILE : (level + 1) * TILE, :]
                now_ref[pl.ds(level * TILE * species + kind, TILE, stride=species), :] = whole
    parts = [biome_ref[TILE * q : TILE * (q + 1), :].astype(jnp.float32) for q in range(own)]
    biomes_ref[...] = plane(parts, halo((species + 1) * groups * HALO), 0)
    pieces = rate_pieces(rate_table_ref)
    pieces_ref[...] = pieces
    put_growth(growth, now_ref, levels, species, total_lat)

    def react(group, carry):
        near = [group * 4 + i for i in range(4)]
        for row in range(TILE):
            chosen = biome_masks(biomes_ref, row, rate_table_ref.shape[0], species)
            sums = reaction(now_ref, 0, pieces, chosen, growth, row, near, species)
            for level, change in zip(near, sums, strict=True):
                first_ref[pl.ds((level * TILE + row) * species, species), :] = change
        return carry

    lax.fori_loop(0, levels // 4, react, 0)


def advance(
    received, now_ref, wet_ref, biomes_ref, pieces_ref, first_ref, sent_out, last_out, sent, last_ref, work, ocean, coef,
    tracer, growth, done, sizes,
):
    levels, species, total_lat, columns, kinds = sizes
    pieces = pieces_ref[...]
    count = total_lat // 2
    own = columns // TILE
    half = FIELDS * levels
    row, lane = rows_of(), lanes_of()
    lat = lane % total_lat
    width = columns + 2 * HALO

    for r_low in range(4):
        for q in range(own + 1):
            for j in range(2):
                work[pl.ds(r_low * LANES + q * total_lat + j, count, stride=2), :] = received[
                    pl.ds(q * TILE + j * 4 + r_low, count, stride=(own + 1) * TILE), :
                ]
    turned = None
    for r_low in range(4):
        turned = work[r_low * LANES : (r_low + 1) * LANES, :].T
        for r_high in range(2):
            ocean[pl.ds(r_high * 4 + r_low, half, stride=TILE), :] = turned[r_high * half : (r_high + 1) * half, :]
    floors = [turned[width + TILE * q : width + TILE * (q + 1), :] for q in range(own)]
    floors.append(
        jnp.where(row < HALO, turned[width + columns : width + columns + TILE, :], turned[width - TILE : width, :])
    )
    floor = floors[own]
    for q in range(own):
        floor = jnp.where(lane // total_lat == q, spin(floors[q], (q - own) * total_lat, 1), floor)
    wet = [(float(level) < floor).astype(jnp.float32) for level in range(levels)]
    sea = [wet_ref[level * TILE : (level + 1) * TILE, :] for level in range(levels)]

    def read(field):
        return [ocean[(field * levels + k) * TILE : (field * levels + k + 1) * TILE, :] for k in range(levels)]

    def write(field, values):
        for k in range(levels):
            ocean[(field * levels + k) * TILE : (field * levels + k + 1) * TILE, :] = values[k]

    def east(x):
        y = spin(x, -1, 0)
        return jnp.where(row == TILE - 1, spin(y, -total_lat, 1), y)

    def west(x):
        y = spin(x, 1, 0)
        return jnp.where(row == 0, spin(y, total_lat, 1), y)

    def north(x):
        return jnp.where(lat == total_lat - 1, 0.0, spin(x, -1, 1))

    def south(x):
        return jnp.where(lat == 0, 0.0, spin(x, 1, 1))

    spin_rate = coriolis * (2.0 * (lat.astype(jnp.float32) + 0.5) / total_lat - 1.0)
    plane = levels * TILE

    def dynamics(step):
        speed_u, speed_v, temper, salty = read(0), read(1), read(2), read(3)
        spread, new_u, new_v = [], [], []
        pressure = None
        for k in range(levels):
            u, v = speed_u[k], speed_v[k]
            part = gravity * (haline_coef * salty[k] - therm_coef * temper[k])
            pressure = part if pressure is None else pressure + part
            slope_east = 0.5 * (east(pressure) - west(pressure))
            slope_north = 0.5 * (north(pressure) - south(pressure))
            u_east, u_west, v_north, v_south = east(u), west(u), north(v), south(v)
            lap_u = u_east + u_west + north(u) + south(u) - 4.0 * u
            lap_v = east(v) + west(v) + v_north + v_south - 4.0 * v
            new_u.append(wet[k] * (u + time_step * (spin_rate * v - slope_east + viscosity * lap_u)))
            new_v.append(wet[k] * (v + time_step * (-spin_rate * u - slope_north + viscosity * lap_v)))
            spread.append(0.5 * (u_east - u_west) + 0.5 * (v_north - v_south))
            face_east = 0.5 * (u + u_east)
            face_west = west(face_east)
            face_north = jnp.where(lat == total_lat - 1, 0.0, 0.5 * (v + v_north))
            face_south = spin(face_north, 1, 1)
            up_east, down_east = jnp.maximum(face_east, 0.0), jnp.minimum(face_east, 0.0)
            up_west, down_west = jnp.maximum(face_west, 0.0), jnp.minimum(face_west, 0.0)
            up_north, down_north = jnp.maximum(face_north, 0.0), jnp.minimum(face_north, 0.0)
            up_south, down_south = jnp.maximum(face_south, 0.0), jnp.minimum(face_south, 0.0)
            mask = tracer_step * sea[k]
            at = step * 7 * plane + k * TILE
            coef[pl.ds(at + plane, TILE), :] = mask * (tracer_diff - down_east)
            coef[pl.ds(at + 2 * plane, TILE), :] = mask * (tracer_diff + up_west)
            coef[pl.ds(at + 3 * plane, TILE), :] = jnp.where(
                lat == total_lat - 1, 0.0, mask * (tracer_diff - down_north)
            )
            coef[pl.ds(at + 4 * plane, TILE), :] = jnp.where(lat == 0, 0.0, mask * (tracer_diff + up_south))
            coef[pl.ds(at, TILE), :] = -4.0 * tracer_diff - up_east + down_west - up_north + down_south
        total = jnp.zeros((TILE, LANES), jnp.float32)
        below_up, below_down = total, total
        for k in reversed(range(levels)):
            total = total + spread[k]
            rise = -vert_ratio * total if k > 0 else jnp.zeros((TILE, LANES), jnp.float32)
            up, down = jnp.maximum(rise, 0.0), jnp.minimum(rise, 0.0)
            mask = tracer_step * sea[k]
            at = step * 7 * plane + k * TILE
            coef[pl.ds(at, TILE), :] = sea[k] + mask * (coef[pl.ds(at, TILE), :] - up + below_down)
            coef[pl.ds(at + 5 * plane, TILE), :] = -mask * down
            coef[pl.ds(at + 6 * plane, TILE), :] = mask * below_up
            below_up, below_down = up, down
        for field, values, rate in ((2, temper, heat_diff), (3, salty, salt_diff)):
            fresh = []
            for k in range(levels):
                x = values[k]
                lap = east(x) + west(x) + north(x) + south(x) - 4.0 * x
                y = x + time_step * rate * lap
                fresh.append(wet[k] * y if field == 3 else y)
            write(field, fresh)
        write(0, new_u)
        write(1, new_v)

    def substep(step, source, base, target, target_base, ready):
        start = step * 7 * plane

        def body(group, carry):
            near = [group * 4 + i for i in range(4)]
            for r in range(TILE):
                if ready is None:
                    chosen = biome_masks(biomes_ref, r, kinds, species)
                    sums = reaction(source, base, pieces, chosen, growth, r, near, species)
                for place, level in enumerate(near):
                    cell = level * TILE + r
                    above = jnp.maximum(level - 1, 0) * TILE + r
                    under = jnp.minimum(level + 1, levels - 1) * TILE + r
                    weight = [coef[pl.ds(start + i * plane + cell, species, stride=0), :] for i in range(7)]
                    mask = wet_ref[pl.ds(cell, species, stride=0), :]

                    def take(index):
                        return source[pl.ds(base + index * species, species), :]

                    x = take(cell)
                    x_east = take(cell + 1) if r < TILE - 1 else spin(take(cell - r), -total_lat, 1)
                    x_west = take(cell - 1) if r > 0 else spin(take(cell + TILE - 1), total_lat, 1)
                    change = sums[place] if ready is None else ready[pl.ds(cell * species, species), :]
                    value = (
                        (weight[0] * x + weight[1] * x_east)
                        + (weight[2] * x_west + weight[3] * spin(x, -1, 1))
                        + (weight[4] * spin(x, 1, 1) + weight[5] * take(above))
                        + (weight[6] * take(under) + mask * change)
                    )
                    target[pl.ds(target_base + cell * species, species), :] = value
            return carry

        lax.fori_loop(0, levels // 4, body, 0)

    for field in range(FIELDS):
        write(field, [wet[k] * x for k, x in enumerate(read(field))])
    size = levels * TILE * species
    source, base = now_ref, 0
    lit = None
    for step in range(STEPS):
        dynamics(step)
        for sub in range(SUB):
            last = step == STEPS - 1 and sub == SUB - 1
            first = step == 0 and sub == 0
            target, target_base = (last_ref, 0) if last else (tracer, ((step * SUB + sub) % 2) * size)
            if not first:
                put_growth(growth, source, levels, species, total_lat, base)
            substep(step, source, base, target, target_base, first_ref if first else None)
            source, base = target, target_base
        if step == STEPS - 1:
            keep = pltpu.make_async_copy(last_ref, last_out, done.at[0])
            keep.start()
        lit = light(planes_of(source, 0, levels, species, base), surface_light(total_lat))
        warm = []
        for k, x in enumerate(read(2)):
            _, top_light, attenuate = lit[k]
            heating = heat_gain * sea[k] * (top_light * (1.0 - jnp.exp(-attenuate)))
            warm.append(wet[k] * (x + time_step * heating))
        write(2, warm)

    for r_low in range(4):
        both = jnp.concatenate(
            [ocean[pl.ds(r_high * 4 + r_low, half, stride=TILE), :] for r_high in range(2)], axis=0
        )
        work[r_low * LANES : (r_low + 1) * LANES, :] = both.T
        for q in range(own):
            for j in range(2):
                sent[pl.ds(q * TILE + j * 4 + r_low, count, stride=own * TILE), :] = work[
                    pl.ds(r_low * LANES + q * total_lat + j, count, stride=2), :
                ]
    send = pltpu.make_async_copy(sent, sent_out, done.at[1])
    send.start()
    send.wait()
    keep.wait()


def unpack_tracers(last_ref, out_ref):
    species, levels, columns, total_lat = out_ref.shape
    for level in range(levels):
        for kind in range(species):
            whole = last_ref[pl.ds(level * TILE * species + kind, TILE, stride=species), :]
            for q in range(columns // TILE):
                out_ref[kind, level, TILE * q : TILE * (q + 1), :] = whole[:, q * total_lat : (q + 1) * total_lat]


def unpack_ocean(received, out_ref, turned, flat):
    fields, levels, lat_rows, total_lon = out_ref.shape
    half = fields * levels
    for i in range(total_lon // TILE):
        turned[TILE * i : TILE * (i + 1), :] = swap_halves(received[TILE * i : TILE * (i + 1), :])
    flat[...] = turned[...].T
    for index in range(half):
        field, level = divmod(index, levels)
        for row in range(lat_rows):
            out_ref[field, level, row : row + 1, :] = flat[row * half + index : row * half + index + 1, :]


def grids(*shapes):
    return [pltpu.VMEM(shape, jnp.float32) for shape in shapes]


def far(*shape):
    return pltpu.HBM(shape, jnp.float32)


def near(*shape, dtype=jnp.float32):
    return pltpu.VMEM(shape, dtype)


def placed(space, *arrays):
    return [pltpu.with_memory_space_constraint(x, space) for x in arrays]


def shards(ocean_state, bottom, tracers, land_sea, biome_id, rate_table):
    count = lax.axis_size("lat")
    if not fits(ocean_state, tracers, count):
        return general_shards(ocean_state, bottom, tracers, land_sea, biome_id, rate_table)
    _, levels, _, total_lon = ocean_state.shape
    species, _, columns, total_lat = tracers.shape
    cells = levels * TILE
    size = cells * species
    own = columns // TILE

    edge_rows = (species + 1) * (levels * total_lat // LANES) * HALO + 2 * HALO
    forward = [(i, (i + 1) % count) for i in range(count)]
    backward = [(b, a) for a, b in forward]
    kinds = rate_table.shape[0]
    roomy = pltpu.CompilerParams(vmem_limit_bytes=GRANT)
    ocean_state, bottom, tracers, land_sea, biome_id, rate_table = placed(
        pltpu.HBM, ocean_state, bottom, tracers, land_sea, biome_id, rate_table
    )
    vmem = pl.BlockSpec(memory_space=pltpu.VMEM)
    hbm = pl.BlockSpec(memory_space=pltpu.HBM)

    packed, to_west, to_east = pl.pallas_call(
        pack,
        out_shape=[far(count * (own + 1) * TILE, LANES), far(edge_rows, LANES), far(edge_rows, LANES)],
        in_specs=[hbm] * 5,
        out_specs=[vmem] * 3,
        scratch_shapes=grids((LANES, total_lon), (TILE, total_lon))
        + [pltpu.VMEM(x.shape, x.dtype) for x in (ocean_state, bottom, tracers, land_sea, biome_id)]
        + [pltpu.SemaphoreType.DMA((5,))],
        compiler_params=roomy,
        name="pack",
    )(ocean_state, bottom, tracers, land_sea, biome_id)
    from_west = lax.ppermute(to_east, "lat", forward)
    from_east = lax.ppermute(to_west, "lat", backward)
    received = lax.all_to_all(
        packed.reshape(count, (own + 1) * TILE, LANES), "lat", split_axis=0, concat_axis=0, tiled=True
    ).reshape(packed.shape)
    from_west, from_east, received = placed(pltpu.VMEM, from_west, from_east, received)

    now, wet, biomes, pieces, first = pl.pallas_call(
        prepare_from,
        out_shape=[
            near(size, LANES),
            near(cells, LANES),
            near(TILE, LANES),
            near(kinds * species, 3 * species, dtype=jnp.bfloat16),
            near(size, LANES),
        ],
        in_specs=[hbm] * 4 + [vmem] * 2,
        out_specs=[vmem] * 5,
        scratch_shapes=[pltpu.VMEM(x.shape, x.dtype) for x in (tracers, land_sea, biome_id, rate_table)]
        + grids((cells, LANES))
        + [pltpu.SemaphoreType.DMA((4,))],
        compiler_params=roomy,
        name="prepare",
    )(tracers, land_sea, biome_id, rate_table, from_west, from_east)

    def run(*refs):
        advance(*refs, (levels, species, total_lat, columns, kinds))

    sent, last = pl.pallas_call(
        run,
        out_shape=[far(count * own * TILE, LANES), far(size, LANES)],
        in_specs=[vmem] * 6,
        out_specs=[hbm] * 2,
        scratch_shapes=grids(
            (count * own * TILE, LANES),
            (size, LANES),
            (4 * LANES, LANES),
            (FIELDS * cells, LANES),
            (STEPS * 7 * cells, LANES),
            (2 * size, LANES),
            (cells, LANES),
        )
        + [pltpu.SemaphoreType.DMA((2,))],
        compiler_params=roomy,
        name="advance",
    )(received, now, wet, biomes, pieces, first)
    back = lax.all_to_all(
        sent.reshape(count, own * TILE, LANES), "lat", split_axis=0, concat_axis=0, tiled=True
    ).reshape(sent.shape)
    (back,) = placed(pltpu.VMEM, back)
    (last,) = placed(pltpu.HBM, last)
    tracers_out = pl.pallas_call(
        unpack_tracers, out_shape=far(*tracers.shape), name="unpack_tracers"
    )(last)
    state_out = pl.pallas_call(
        unpack_ocean,
        out_shape=far(*ocean_state.shape),
        in_specs=[vmem],
        out_specs=vmem,
        scratch_shapes=grids((total_lon, LANES), (LANES, total_lon)),
        compiler_params=roomy,
        name="unpack_ocean",
    )(back)
    return (state_out, tracers_out)


def solution(mesh):
    in_specs = (
        P(None, None, ("groups", "lat"), None),
        P(("groups", "lat"), None),
        P(None, None, ("groups", "lat"), None),
        P(None, ("groups", "lat"), None),
        P(("groups", "lat"), None),
        P(),
    )
    out_specs = (P(None, None, ("groups", "lat"), None), P(None, None, ("groups", "lat"), None))
    return jax.shard_map(shards, mesh=mesh, in_specs=in_specs, out_specs=out_specs, check_vma=False)
```

```python
import jax
import jax.numpy as jnp
from jax import lax
from jax.experimental import pallas as pl
from jax.experimental.pallas import tpu as pltpu
from jax.sharding import PartitionSpec as P


STEPS = 2
SUB = 2


time_step = 0.1
viscosity = 0.1
heat_diff = 0.08
salt_diff = 0.06
therm_coef = 0.2
haline_coef = 0.15
gravity = 0.5
coriolis = 0.6
vert_ratio = 0.25
tracer_step = 0.1
tracer_diff = 0.1
water_atten = 0.04
chl_atten = 0.05
growth_rate = 0.8
heat_gain = 10.0


def extended(block, sides, width, periodic):
    for axis, dim in sides:
        count = lax.axis_size(axis)
        forward = [(i, i + 1) for i in range(count - 1)]
        if periodic:
            forward.append((count - 1, 0))
        backward = [(target, source) for source, target in forward]
        low = lax.ppermute(
            lax.slice_in_dim(block, block.shape[dim] - width, None, axis=dim), axis, forward
        )
        high = lax.ppermute(lax.slice_in_dim(block, 0, width, axis=dim), axis, backward)
        block = jnp.concatenate([low, block, high], axis=dim)
    return block


def laplace_rows(field):
    center = field[:, 1:-1, :]
    return (
        jnp.roll(center, 1, 2)
        + jnp.roll(center, -1, 2)
        + field[:, 2:, :]
        + field[:, :-2, :]
        - 4.0 * center
    )


def ocean_core(padded, wet_mask, lat_start, total_lat):
    speed_u, speed_v, temper, salty = (padded[0], padded[1], padded[2], padded[3])
    east_mid = speed_u[:, 1:-1, :]
    north_mid = speed_v[:, 1:-1, :]
    temp_mid = temper[:, 1:-1, :]
    salt_mid = salty[:, 1:-1, :]
    pressure = gravity * jnp.cumsum(haline_coef * salty - therm_coef * temper, axis=0)
    press_mid = pressure[:, 1:-1, :]
    row_index = (lat_start + jnp.arange(wet_mask.shape[1], dtype=jnp.int32)).astype(jnp.float32)
    spin_rate = (coriolis * (2.0 * (row_index + 0.5) / total_lat - 1.0))[None, :, None]
    slope_east = 0.5 * (jnp.roll(press_mid, -1, 2) - jnp.roll(press_mid, 1, 2))
    slope_north = 0.5 * (pressure[:, 2:, :] - pressure[:, :-2, :])
    new_u = wet_mask * (
        east_mid
        + time_step * (spin_rate * north_mid - slope_east + viscosity * laplace_rows(speed_u))
    )
    new_v = wet_mask * (
        north_mid
        + time_step * (-spin_rate * east_mid - slope_north + viscosity * laplace_rows(speed_v))
    )
    new_s = wet_mask * (salt_mid + time_step * salt_diff * laplace_rows(salty))
    part_t = temp_mid + time_step * heat_diff * laplace_rows(temper)
    spread = 0.5 * (jnp.roll(east_mid, -1, 2) - jnp.roll(east_mid, 1, 2)) + 0.5 * (
        speed_v[:, 2:, :] - speed_v[:, :-2, :]
    )
    rise_flux = -vert_ratio * jnp.flip(jnp.cumsum(jnp.flip(spread, 0), axis=0), 0)
    fluxes = jnp.stack([east_mid, north_mid, rise_flux])
    return (new_u, new_v, part_t, new_s, fluxes)


def light_field(plankton):
    chloro = jax.nn.softplus(plankton)
    attenuate = water_atten + chl_atten * chloro
    depth = jnp.cumsum(attenuate, axis=0) - attenuate
    row_index = jnp.arange(plankton.shape[-1], dtype=jnp.int32).astype(jnp.float32)
    place = 2.0 * (row_index + 0.5) / plankton.shape[-1] - 1.0
    surface = 1.0 - 0.5 * place * place
    top_light = surface * jnp.exp(-depth)
    return (chloro, top_light, top_light * (1.0 - jnp.exp(-attenuate)))


def tracer_core(tracer_ext, flux_ext, sea_mask, onehot, rate_table):
    center = tracer_ext[:, :, 1:-1, :]
    east_face = 0.5 * (flux_ext[0, :, :-1, :] + flux_ext[0, :, 1:, :])
    across = (
        jnp.maximum(east_face, 0.0) * tracer_ext[:, :, :-1, :]
        + jnp.minimum(east_face, 0.0) * tracer_ext[:, :, 1:, :]
    )
    div_east = across[:, :, 1:, :] - across[:, :, :-1, :]
    north_speed = flux_ext[1, :, 1:-1, :]
    north_face = 0.5 * (north_speed[:, :, :-1] + north_speed[:, :, 1:])
    along = (
        jnp.maximum(north_face, 0.0) * center[..., :-1]
        + jnp.minimum(north_face, 0.0) * center[..., 1:]
    )
    along = jnp.pad(along, ((0, 0), (0, 0), (0, 0), (1, 1)))
    div_north = along[..., 1:] - along[..., :-1]
    rise_face = flux_ext[2, 1:, 1:-1, :]
    upward = (
        jnp.maximum(rise_face, 0.0) * center[:, 1:] + jnp.minimum(rise_face, 0.0) * center[:, :-1]
    )
    upward = jnp.pad(upward, ((0, 0), (1, 1), (0, 0), (0, 0)))
    div_up = upward[:, :-1] - upward[:, 1:]
    side = jnp.pad(center, ((0, 0), (0, 0), (0, 0), (1, 1)))
    diffuse = (
        tracer_ext[:, :, 2:, :]
        + tracer_ext[:, :, :-2, :]
        + side[..., 2:]
        + side[..., :-2]
        - 4.0 * center
    )
    chloro, top_light, _ = light_field(center[0])
    nutrient = center[1] * center[1]
    uptake = growth_rate * top_light * chloro * nutrient / (1.0 + nutrient)
    rate_cell = jnp.einsum("bst,bij->stij", rate_table, onehot, precision=lax.Precision.HIGHEST)
    reaction = jnp.einsum("stij,tkij->skij", rate_cell, center, precision=lax.Precision.HIGHEST)
    reaction = reaction.at[0].add(uptake).at[1].add(-uptake)
    tendency = tracer_diff * diffuse + reaction - (div_east + div_north + div_up)
    return sea_mask[None] * (center + tracer_step * tendency)


def general_shards(ocean_state, bottom, tracers, land_sea, biome_id, rate_table):
    levels = ocean_state.shape[1]
    lat_rows = ocean_state.shape[2]
    lat_count = lax.axis_size("lat")
    total_lat = lat_rows * lat_count
    lat_start = lax.axis_index("lat") * lat_rows
    wet_mask = (jnp.arange(levels, dtype=jnp.int32)[:, None, None] < bottom[None]).astype(
        jnp.float32
    )
    sea_mask = land_sea.astype(jnp.float32)
    onehot = (
        biome_id[None] == jnp.arange(rate_table.shape[0], dtype=jnp.int32)[:, None, None]
    ).astype(jnp.float32)
    state = ocean_state
    tracer_now = tracers
    for _ in range(STEPS):
        state = state * wet_mask[None]
        padded = extended(state, (("lat", 2),), 1, False)
        new_u, new_v, part_t, new_s, fluxes = ocean_core(padded, wet_mask, lat_start, total_lat)
        flux_t = lax.all_to_all(
            jnp.transpose(fluxes, (0, 1, 3, 2)), "lat", split_axis=2, concat_axis=3, tiled=True
        )
        tracer_now = tracer_now * sea_mask[None]
        flux_ext = extended(flux_t, (("lat", 2),), 1, True)
        for _ in range(SUB):
            tracer_ext = extended(tracer_now, (("lat", 2),), 1, True)
            tracer_now = tracer_core(tracer_ext, flux_ext, sea_mask, onehot, rate_table)
        heating = heat_gain * sea_mask * light_field(tracer_now[0])[2]
        heat_ocean = jnp.transpose(
            lax.all_to_all(heating, "lat", split_axis=2, concat_axis=1, tiled=True), (0, 2, 1)
        )
        new_t = wet_mask * (part_t + time_step * heat_ocean)
        state = jnp.stack([new_u, new_v, new_t, new_s])
    return (state, tracer_now)


HALO = STEPS * SUB
LANES = 128
TILE = 8
FIELDS = 4
GRANT = 16 * 1024 * 1024


def fits(ocean_state, tracers, lat_count):
    _, levels, lat_rows, total_lon = ocean_state.shape
    species, _, columns, total_lat = tracers.shape
    return (
        lat_rows == 2
        and HALO == TILE // 2
        and lat_rows * lat_count == total_lat
        and columns * lat_count == total_lon
        and columns % TILE == 0
        and LANES % total_lat == 0
        and (columns + 2 * HALO) * total_lat == TILE * LANES
        and 2 * FIELDS * levels == LANES
        and levels <= columns + HALO
        and 2 * columns + 3 * HALO <= FIELDS * levels
        and species == 2 * TILE
        and lat_count % 2 == 0
        and levels % (LANES // total_lat) == 0
    )


def rows_of(shape=(TILE, LANES)):
    return lax.broadcasted_iota(jnp.int32, shape, 0)


def lanes_of(shape=(TILE, LANES)):
    return lax.broadcasted_iota(jnp.int32, shape, 1)


def spin(block, amount, axis):
    size = block.shape[axis]
    amount = amount % size
    return block if amount == 0 else pltpu.roll(block, amount, axis)


def swap_halves(block):
    low_row, low_lane = rows_of() < TILE // 2, lanes_of() < LANES // 2
    other = spin(spin(block, LANES // 2, 1), TILE // 2, 0)
    return jnp.where(low_row == low_lane, block, other)


def pack_ocean(ocean_ref, bottom_ref, out_ref, flat, depth):
    fields, levels, lat_rows, total_lon = ocean_ref.shape
    half = fields * levels
    count = out_ref.shape[0] // (4 * TILE)
    columns = total_lon // count
    own = columns // TILE
    for index in range(half):
        field, level = divmod(index, levels)
        for row in range(lat_rows):
            flat[row * half + index : row * half + index + 1, :] = ocean_ref[field, level, row : row + 1, :]
    turned = flat[...].T
    tiles = [turned[TILE * i : TILE * (i + 1), :] for i in range(total_lon // TILE)]
    swapped = [swap_halves(t) for t in tiles]
    depth[...] = jnp.zeros(depth.shape, jnp.float32)
    depth[3:4, :] = bottom_ref[0:1, :].astype(jnp.float32)
    depth[7:8, :] = bottom_ref[1:2, :].astype(jnp.float32)
    line = depth[...]
    row, lane = rows_of(), lanes_of()
    width = columns + 2 * HALO
    window = (row % 4 == 3) & (lane >= width - HALO) & (lane < 2 * width - HALO)
    for target in range(count):
        for q in range(own):
            out_ref[pl.ds((target * (own + 1) + q) * TILE, TILE), :] = swapped[target * own + q]
        east = tiles[(target * own + own) % len(tiles)]
        west = tiles[target * own - 1]
        edge = swap_halves(jnp.where(row < HALO, east, west))
        level_line = spin(line, width - target * columns, 1)[:, :LANES]
        out_ref[pl.ds((target * (own + 1) + own) * TILE, TILE), :] = jnp.where(window, level_line, edge)


def pack_edges(low_ref, high_ref, sea_ref, biome_ref, first_ref, second_ref, even):
    species, levels, _, total_lat = low_ref.shape
    columns = sea_ref.shape[1]
    blocks = LANES // total_lat
    groups = levels // blocks
    low = rows_of((TILE, total_lat)) < HALO
    last = columns - TILE

    def put(start, both):
        flipped = spin(both, HALO, 0)
        here = jnp.where(even, flipped, both)
        first_ref[start : start + HALO, :] = here[:HALO, :]
        second_ref[start : start + HALO, :] = here[HALO:, :]

    for group in range(groups):
        wet = [
            jnp.where(low, sea_ref[group * blocks + b, 0:TILE, :], sea_ref[group * blocks + b, last:columns, :]).astype(
                jnp.float32
            )
            for b in range(blocks)
        ]
        joined = jnp.concatenate(wet, axis=1)
        put(species * groups * HALO + group * HALO, joined)
        for kind in range(species):
            parts = [
                jnp.where(low, low_ref[kind, group * blocks + b], high_ref[kind, group * blocks + b])
                for b in range(blocks)
            ]
            put((kind * groups + group) * HALO, jnp.concatenate(parts, axis=1) * joined)
    biome = jnp.where(low, biome_ref[0:TILE, :], biome_ref[last:columns, :]).astype(jnp.float32)
    start = (species + 1) * groups * HALO
    put(start, jnp.concatenate([biome] * blocks, axis=1))
    first_ref[start + HALO : start + 2 * HALO, :] = jnp.zeros((HALO, LANES), jnp.float32)
    second_ref[start + HALO : start + 2 * HALO, :] = jnp.zeros((HALO, LANES), jnp.float32)


def fetch(sources, targets, ready):
    copies = [pltpu.make_async_copy(a, b, ready.at[i]) for i, (a, b) in enumerate(zip(sources, targets, strict=True))]
    for copy in copies:
        copy.start()
    return copies


def is_even():
    return lax.axis_index("lat") % 2 == 0


def pack(ocean, bottom, tracers, sea, biome, *refs):
    out, edges, (flat, depth), held, result, ready, gone = refs[0], refs[1:3], refs[3:5], refs[5:11], refs[11], refs[12], refs[13]
    columns = tracers.shape[2]
    sources = [ocean, bottom, tracers.at[:, :, 0:TILE, :], tracers.at[:, :, columns - TILE : columns, :], sea, biome]
    copies = fetch(sources, held, ready)
    copies[0].wait()
    copies[1].wait()
    pack_ocean(held[0], held[1], result, flat, depth)
    leaving = pltpu.make_async_copy(result, out, gone)
    leaving.start()
    for copy in copies[2:]:
        copy.wait()
    pack_edges(*held[2:], *edges, is_even())
    leaving.wait()


def light(plankton, surface):
    result = []
    depth = jnp.zeros(surface.shape, jnp.float32)
    for value in plankton:
        chloro = jnp.maximum(value, 0.0) + jnp.log(1.0 + jnp.exp(-jnp.abs(value)))
        attenuate = water_atten + chl_atten * chloro
        result.append((chloro, surface * jnp.exp(-depth), attenuate))
        depth = depth + attenuate
    return result


def surface_light(total_lat):
    row_index = (lanes_of() % total_lat).astype(jnp.float32)
    place = 2.0 * (row_index + 0.5) / total_lat - 1.0
    return 1.0 - 0.5 * place * place


def planes_of(ref, kind, levels, species, base=0):
    return [ref[pl.ds(base + level * TILE * species + kind, TILE, stride=species), :] for level in range(levels)]


def put_growth(growth_ref, tracer_ref, levels, species, total_lat, base=0):
    lit = light(planes_of(tracer_ref, 0, levels, species, base), surface_light(total_lat))
    food = planes_of(tracer_ref, 1, levels, species, base)
    for level, (chloro, top_light, _) in enumerate(lit):
        nutrient = food[level] * food[level]
        uptake = growth_rate * top_light * chloro * nutrient / (1.0 + nutrient)
        growth_ref[level * TILE : (level + 1) * TILE, :] = tracer_step * uptake
    return lit


def rate_pieces(rate_table_ref):
    kinds, species, _ = rate_table_ref.shape
    rates = tracer_step * rate_table_ref[...].reshape(kinds * species, species)
    high = rates.astype(jnp.bfloat16)
    low = (rates - high.astype(jnp.float32)).astype(jnp.bfloat16)
    return jnp.concatenate([high, low, high], axis=1)


def reaction(source_ref, base, pieces, chosen, growth_ref, row, levels, species):
    index = rows_of()
    sign = jnp.where(index == 0, 1.0, jnp.where(index == 1, -1.0, 0.0))
    sums = []
    for pair in range(0, len(levels), 2):
        near = levels[pair : pair + 2]
        values = jnp.concatenate(
            [source_ref[pl.ds(base + (level * TILE + row) * species, species), :] for level in near], axis=1
        )
        high = values.astype(jnp.bfloat16)
        low = (values - high.astype(jnp.float32)).astype(jnp.bfloat16)
        every = jnp.dot(
            pieces, jnp.concatenate([high, high, low], axis=0), preferred_element_type=jnp.float32
        )
        for place, level in enumerate(near):
            mine = every[:, place * LANES : (place + 1) * LANES]
            total = mine[:species, :]
            for kind, mask in enumerate(chosen):
                total = jnp.where(mask, mine[(kind + 1) * species : (kind + 2) * species, :], total)
            uptake = sign * growth_ref[pl.ds(level * TILE + row, TILE, stride=0), :]
            sums.append(jnp.concatenate([total[:TILE, :] + uptake, total[TILE:, :]], axis=0))
    return sums


def biome_masks(biome_ref, row, kinds, species):
    here = jnp.broadcast_to(biome_ref[row : row + 1, :], (species, LANES))
    return [here == float(kind) for kind in range(1, kinds)]


def prepare_own(tracers, sea, biome, rate_table, own_ref, wet_ref, biomes_ref, pieces_ref, *refs):
    held, ready = refs[:4], refs[4]
    tracer_ref, sea_ref, biome_ref, rate_table_ref = held
    species, levels, columns, total_lat = tracers.shape
    own = columns // TILE
    copies = fetch([tracers, sea, biome, rate_table], held, ready)
    blank = jnp.zeros((TILE, total_lat), jnp.float32)
    for copy in copies[1:]:
        copy.wait()

    def plane(parts):
        return jnp.concatenate(parts + [blank], axis=1)

    pieces_ref[...] = rate_pieces(rate_table_ref)
    biomes_ref[...] = plane([biome_ref[TILE * q : TILE * (q + 1), :].astype(jnp.float32) for q in range(own)])
    for level in range(levels):
        parts = [sea_ref[level, TILE * q : TILE * (q + 1), :].astype(jnp.float32) for q in range(own)]
        wet_ref[level * TILE : (level + 1) * TILE, :] = plane(parts)
    copies[0].wait()
    for level in range(levels):
        wet = wet_ref[level * TILE : (level + 1) * TILE, :]
        for kind in range(species):
            parts = [tracer_ref[kind, level, TILE * q : TILE * (q + 1), :] for q in range(own)]
            own_ref[pl.ds(level * TILE * species + kind, TILE, stride=species), :] = plane(parts) * wet


def prepare_all(
    own_ref, own_wet_ref, own_biomes_ref, pieces_ref, from_first, from_second, now_ref, wet_ref, biomes_ref, first_ref, growth, sizes
):
    levels, species, total_lat, columns, kinds = sizes
    blocks = LANES // total_lat
    groups = levels // blocks
    inner = lanes_of() < columns // TILE * total_lat
    even = is_even()

    def halo(start):
        both = jnp.concatenate([from_first[start : start + HALO, :], from_second[start : start + HALO, :]], axis=0)
        return jnp.where(even, both, spin(both, HALO, 0))

    def joined(inside, edge, block):
        return jnp.where(inner, inside, spin(edge, LANES - (block + 1) * total_lat, 1))

    for group in range(groups):
        edge = halo((species * groups + group) * HALO)
        for block in range(blocks):
            place = slice((group * blocks + block) * TILE, (group * blocks + block + 1) * TILE)
            wet_ref[place, :] = joined(own_wet_ref[place, :], edge, block)
    biomes_ref[...] = joined(own_biomes_ref[...], halo((species + 1) * groups * HALO), 0)
    for kind in range(species):
        for group in range(groups):
            edge = halo((kind * groups + group) * HALO)
            for block in range(blocks):
                place = pl.ds((group * blocks + block) * TILE * species + kind, TILE, stride=species)
                now_ref[place, :] = joined(own_ref[place, :], edge, block)
    put_growth(growth, now_ref, levels, species, total_lat)
    pieces = pieces_ref[...]
    for row in range(TILE):
        chosen = biome_masks(biomes_ref, row, kinds, species)
        every = list(range(levels))
        for level, change in zip(every, reaction(now_ref, 0, pieces, chosen, growth, row, every, species), strict=True):
            first_ref[pl.ds((level * TILE + row) * species, species), :] = change


def advance(
    received, now_ref, wet_ref, biomes_ref, pieces_ref, first_ref, sent_out, last_out, sent, last_ref, work, ocean, coef,
    tracer, growth, done, sizes,
):
    levels, species, total_lat, columns, kinds = sizes
    pieces = pieces_ref[...]
    count = total_lat // 2
    own = columns // TILE
    half = FIELDS * levels
    row, lane = rows_of(), lanes_of()
    lat = lane % total_lat
    width = columns + 2 * HALO

    for r_low in range(4):
        for q in range(own + 1):
            for j in range(2):
                work[pl.ds(r_low * LANES + q * total_lat + j, count, stride=2), :] = received[
                    pl.ds(q * TILE + j * 4 + r_low, count, stride=(own + 1) * TILE), :
                ]
    turned = None
    for r_low in range(4):
        turned = work[r_low * LANES : (r_low + 1) * LANES, :].T
        for r_high in range(2):
            ocean[pl.ds(r_high * 4 + r_low, half, stride=TILE), :] = turned[r_high * half : (r_high + 1) * half, :]
    floors = [turned[width + TILE * q : width + TILE * (q + 1), :] for q in range(own)]
    floors.append(
        jnp.where(row < HALO, turned[width + columns : width + columns + TILE, :], turned[width - TILE : width, :])
    )
    floor = floors[own]
    for q in range(own):
        floor = jnp.where(lane // total_lat == q, spin(floors[q], (q - own) * total_lat, 1), floor)
    wet = [(float(level) < floor).astype(jnp.float32) for level in range(levels)]
    sea = [wet_ref[level * TILE : (level + 1) * TILE, :] for level in range(levels)]

    def read(field):
        return [ocean[(field * levels + k) * TILE : (field * levels + k + 1) * TILE, :] for k in range(levels)]

    def write(field, values):
        for k in range(levels):
            ocean[(field * levels + k) * TILE : (field * levels + k + 1) * TILE, :] = values[k]

    def east(x):
        y = spin(x, -1, 0)
        return jnp.where(row == TILE - 1, spin(y, -total_lat, 1), y)

    def west(x):
        y = spin(x, 1, 0)
        return jnp.where(row == 0, spin(y, total_lat, 1), y)

    def north(x):
        return jnp.where(lat == total_lat - 1, 0.0, spin(x, -1, 1))

    def south(x):
        return jnp.where(lat == 0, 0.0, spin(x, 1, 1))

    spin_rate = coriolis * (2.0 * (lat.astype(jnp.float32) + 0.5) / total_lat - 1.0)
    plane = levels * TILE

    def dynamics(step):
        speed_u, speed_v, temper, salty = read(0), read(1), read(2), read(3)
        spread, new_u, new_v = [], [], []
        pressure = None
        for k in range(levels):
            u, v = speed_u[k], speed_v[k]
            part = gravity * (haline_coef * salty[k] - therm_coef * temper[k])
            pressure = part if pressure is None else pressure + part
            slope_east = 0.5 * (east(pressure) - west(pressure))
            slope_north = 0.5 * (north(pressure) - south(pressure))
            u_east, u_west, v_north, v_south = east(u), west(u), north(v), south(v)
            lap_u = u_east + u_west + north(u) + south(u) - 4.0 * u
            lap_v = east(v) + west(v) + v_north + v_south - 4.0 * v
            new_u.append(wet[k] * (u + time_step * (spin_rate * v - slope_east + viscosity * lap_u)))
            new_v.append(wet[k] * (v + time_step * (-spin_rate * u - slope_north + viscosity * lap_v)))
            spread.append(0.5 * (u_east - u_west) + 0.5 * (v_north - v_south))
            face_east = 0.5 * (u + u_east)
            face_west = west(face_east)
            face_north = jnp.where(lat == total_lat - 1, 0.0, 0.5 * (v + v_north))
            face_south = spin(face_north, 1, 1)
            up_east, down_east = jnp.maximum(face_east, 0.0), jnp.minimum(face_east, 0.0)
            up_west, down_west = jnp.maximum(face_west, 0.0), jnp.minimum(face_west, 0.0)
            up_north, down_north = jnp.maximum(face_north, 0.0), jnp.minimum(face_north, 0.0)
            up_south, down_south = jnp.maximum(face_south, 0.0), jnp.minimum(face_south, 0.0)
            mask = tracer_step * sea[k]
            at = step * 7 * plane + k * TILE
            coef[pl.ds(at + plane, TILE), :] = mask * (tracer_diff - down_east)
            coef[pl.ds(at + 2 * plane, TILE), :] = mask * (tracer_diff + up_west)
            coef[pl.ds(at + 3 * plane, TILE), :] = jnp.where(
                lat == total_lat - 1, 0.0, mask * (tracer_diff - down_north)
            )
            coef[pl.ds(at + 4 * plane, TILE), :] = jnp.where(lat == 0, 0.0, mask * (tracer_diff + up_south))
            coef[pl.ds(at, TILE), :] = -4.0 * tracer_diff - up_east + down_west - up_north + down_south
        total = jnp.zeros((TILE, LANES), jnp.float32)
        below_up, below_down = total, total
        for k in reversed(range(levels)):
            total = total + spread[k]
            rise = -vert_ratio * total if k > 0 else jnp.zeros((TILE, LANES), jnp.float32)
            up, down = jnp.maximum(rise, 0.0), jnp.minimum(rise, 0.0)
            mask = tracer_step * sea[k]
            at = step * 7 * plane + k * TILE
            coef[pl.ds(at, TILE), :] = sea[k] + mask * (coef[pl.ds(at, TILE), :] - up + below_down)
            coef[pl.ds(at + 5 * plane, TILE), :] = -mask * down
            coef[pl.ds(at + 6 * plane, TILE), :] = mask * below_up
            below_up, below_down = up, down
        for field, values, rate in ((2, temper, heat_diff), (3, salty, salt_diff)):
            fresh = []
            for k in range(levels):
                x = values[k]
                lap = east(x) + west(x) + north(x) + south(x) - 4.0 * x
                y = x + time_step * rate * lap
                fresh.append(wet[k] * y if field == 3 else y)
            write(field, fresh)
        write(0, new_u)
        write(1, new_v)

    def substep(step, source, base, target, target_base, ready):
        start = step * 7 * plane

        def body(group, carry):
            near = [group * 4 + i for i in range(4)]
            for r in range(TILE):
                if ready is None:
                    chosen = biome_masks(biomes_ref, r, kinds, species)
                    sums = reaction(source, base, pieces, chosen, growth, r, near, species)
                for place, level in enumerate(near):
                    cell = level * TILE + r
                    above = max(level - 1, 0) * TILE + r
                    under = min(level + 1, levels - 1) * TILE + r
                    weight = [coef[pl.ds(start + i * plane + cell, species, stride=0), :] for i in range(7)]
                    mask = wet_ref[pl.ds(cell, species, stride=0), :]

                    def take(index):
                        return source[pl.ds(base + index * species, species), :]

                    x = take(cell)
                    x_east = take(cell + 1) if r < TILE - 1 else spin(take(cell - r), -total_lat, 1)
                    x_west = take(cell - 1) if r > 0 else spin(take(cell + TILE - 1), total_lat, 1)
                    change = sums[place] if ready is None else ready[pl.ds(cell * species, species), :]
                    value = (
                        (weight[0] * x + weight[1] * x_east)
                        + (weight[2] * x_west + weight[3] * spin(x, -1, 1))
                        + (weight[4] * spin(x, 1, 1) + weight[5] * take(above))
                        + (weight[6] * take(under) + mask * change)
                    )
                    target[pl.ds(target_base + cell * species, species), :] = value
            return carry

        for group in range(levels // 4):
            body(group, 0)

    for field in range(FIELDS):
        write(field, [wet[k] * x for k, x in enumerate(read(field))])
    size = levels * TILE * species
    source, base = now_ref, 0
    lit = None
    for step in range(STEPS):
        dynamics(step)
        for sub in range(SUB):
            last = step == STEPS - 1 and sub == SUB - 1
            first = step == 0 and sub == 0
            target, target_base = (last_ref, 0) if last else (tracer, ((step * SUB + sub) % 2) * size)
            if not first:
                put_growth(growth, source, levels, species, total_lat, base)
            substep(step, source, base, target, target_base, first_ref if first else None)
            source, base = target, target_base
        if step == STEPS - 1:
            keep = pltpu.make_async_copy(last_ref, last_out, done.at[0])
            keep.start()
        lit = light(planes_of(source, 0, levels, species, base), surface_light(total_lat))
        warm = []
        for k, x in enumerate(read(2)):
            _, top_light, attenuate = lit[k]
            heating = heat_gain * sea[k] * (top_light * (1.0 - jnp.exp(-attenuate)))
            warm.append(wet[k] * (x + time_step * heating))
        write(2, warm)

    for r_low in range(4):
        both = jnp.concatenate(
            [ocean[pl.ds(r_high * 4 + r_low, half, stride=TILE), :] for r_high in range(2)], axis=0
        )
        work[r_low * LANES : (r_low + 1) * LANES, :] = both.T
        for q in range(own):
            for j in range(2):
                sent[pl.ds(q * TILE + j * 4 + r_low, count, stride=own * TILE), :] = work[
                    pl.ds(r_low * LANES + q * total_lat + j, count, stride=2), :
                ]
    send = pltpu.make_async_copy(sent, sent_out, done.at[1])
    send.start()
    send.wait()
    keep.wait()


def unpack_tracers(last_ref, out_ref):
    species, levels, columns, total_lat = out_ref.shape
    for level in range(levels):
        for kind in range(species):
            whole = last_ref[pl.ds(level * TILE * species + kind, TILE, stride=species), :]
            for q in range(columns // TILE):
                out_ref[kind, level, TILE * q : TILE * (q + 1), :] = whole[:, q * total_lat : (q + 1) * total_lat]


def unpack_ocean(received, out_ref, turned, flat):
    fields, levels, lat_rows, total_lon = out_ref.shape
    half = fields * levels
    for i in range(total_lon // TILE):
        turned[TILE * i : TILE * (i + 1), :] = swap_halves(received[TILE * i : TILE * (i + 1), :])
    flat[...] = turned[...].T
    for index in range(half):
        field, level = divmod(index, levels)
        for row in range(lat_rows):
            out_ref[field, level, row : row + 1, :] = flat[row * half + index : row * half + index + 1, :]


def grids(*shapes):
    return [pltpu.VMEM(shape, jnp.float32) for shape in shapes]


def far(*shape):
    return pltpu.HBM(shape, jnp.float32)


def near(*shape, dtype=jnp.float32):
    return pltpu.VMEM(shape, dtype)


def placed(space, *arrays):
    return [pltpu.with_memory_space_constraint(x, space) for x in arrays]


def shards(ocean_state, bottom, tracers, land_sea, biome_id, rate_table):
    count = lax.axis_size("lat")
    if not fits(ocean_state, tracers, count):
        return general_shards(ocean_state, bottom, tracers, land_sea, biome_id, rate_table)
    _, levels, _, total_lon = ocean_state.shape
    species, _, columns, total_lat = tracers.shape
    cells = levels * TILE
    size = cells * species
    own = columns // TILE

    edge_rows = (species + 1) * (levels * total_lat // LANES) * HALO + 2 * HALO
    kinds = rate_table.shape[0]
    roomy = pltpu.CompilerParams(vmem_limit_bytes=GRANT)
    ocean_state, bottom, tracers, land_sea, biome_id, rate_table = placed(
        pltpu.HBM, ocean_state, bottom, tracers, land_sea, biome_id, rate_table
    )
    vmem = pl.BlockSpec(memory_space=pltpu.VMEM)
    hbm = pl.BlockSpec(memory_space=pltpu.HBM)

    pairs = [(i, i ^ 1) for i in range(count)]
    others = [((a + 1) % count, (b + 1) % count) for a, b in pairs]
    sizes = (levels, species, total_lat, columns, kinds)
    edge_shape = (species, levels, TILE, total_lat)

    packed, to_first, to_second = pl.pallas_call(
        pack,
        out_shape=[far(count * (own + 1) * TILE, LANES), near(edge_rows, LANES), near(edge_rows, LANES)],
        in_specs=[hbm] * 5,
        out_specs=[hbm, vmem, vmem],
        scratch_shapes=grids((LANES, total_lon), (TILE, total_lon), ocean_state.shape)
        + [pltpu.VMEM(bottom.shape, bottom.dtype)]
        + grids(edge_shape, edge_shape)
        + [pltpu.VMEM(x.shape, x.dtype) for x in (land_sea, biome_id)]
        + grids((count * (own + 1) * TILE, LANES))
        + [pltpu.SemaphoreType.DMA((6,)), pltpu.SemaphoreType.DMA],
        compiler_params=roomy,
        name="pack",
    )(ocean_state, bottom, tracers, land_sea, biome_id)
    received = lax.all_to_all(
        packed.reshape(count, (own + 1) * TILE, LANES), "lat", split_axis=0, concat_axis=0, tiled=True
    ).reshape(packed.shape)
    from_first = lax.ppermute(to_first, "lat", pairs)
    from_second = lax.ppermute(to_second, "lat", others)
    from_first, from_second, received = placed(pltpu.VMEM, from_first, from_second, received)

    inside = pl.pallas_call(
        prepare_own,
        out_shape=[
            near(size, LANES),
            near(cells, LANES),
            near(TILE, LANES),
            near(kinds * species, 3 * species, dtype=jnp.bfloat16),
        ],
        in_specs=[hbm] * 4,
        out_specs=[vmem] * 4,
        scratch_shapes=[pltpu.VMEM(x.shape, x.dtype) for x in (tracers, land_sea, biome_id, rate_table)]
        + [pltpu.SemaphoreType.DMA((4,))],
        compiler_params=roomy,
        name="prepare_own",
    )(tracers, land_sea, biome_id, rate_table)
    pieces = inside[3]

    def prepare(*refs):
        prepare_all(*refs, sizes)

    now, wet, biomes, first = pl.pallas_call(
        prepare,
        out_shape=[near(size, LANES), near(cells, LANES), near(TILE, LANES), near(size, LANES)],
        in_specs=[vmem] * 6,
        out_specs=[vmem] * 4,
        scratch_shapes=grids((cells, LANES)),
        compiler_params=roomy,
        name="prepare",
    )(*inside, from_first, from_second)

    def run(*refs):
        advance(*refs, sizes)

    sent, last = pl.pallas_call(
        run,
        out_shape=[far(count * own * TILE, LANES), far(size, LANES)],
        in_specs=[vmem] * 6,
        out_specs=[hbm] * 2,
        scratch_shapes=grids(
            (count * own * TILE, LANES),
            (size, LANES),
            (4 * LANES, LANES),
            (FIELDS * cells, LANES),
            (STEPS * 7 * cells, LANES),
            (2 * size, LANES),
            (cells, LANES),
        )
        + [pltpu.SemaphoreType.DMA((2,))],
        compiler_params=roomy,
        name="advance",
    )(received, now, wet, biomes, pieces, first)
    back = lax.all_to_all(
        sent.reshape(count, own * TILE, LANES), "lat", split_axis=0, concat_axis=0, tiled=True
    ).reshape(sent.shape)
    (back,) = placed(pltpu.VMEM, back)
    (last,) = placed(pltpu.HBM, last)
    tracers_out = pl.pallas_call(
        unpack_tracers, out_shape=far(*tracers.shape), name="unpack_tracers"
    )(last)
    state_out = pl.pallas_call(
        unpack_ocean,
        out_shape=far(*ocean_state.shape),
        in_specs=[vmem],
        out_specs=vmem,
        scratch_shapes=grids((total_lon, LANES), (LANES, total_lon)),
        compiler_params=roomy,
        name="unpack_ocean",
    )(back)
    return (state_out, tracers_out)


def solution(mesh):
    in_specs = (
        P(None, None, ("groups", "lat"), None),
        P(("groups", "lat"), None),
        P(None, None, ("groups", "lat"), None),
        P(None, ("groups", "lat"), None),
        P(("groups", "lat"), None),
        P(),
    )
    out_specs = (P(None, None, ("groups", "lat"), None), P(None, None, ("groups", "lat"), None))
    return jax.shard_map(shards, mesh=mesh, in_specs=in_specs, out_specs=out_specs, check_vma=False)
```

```python
import jax
import jax.numpy as jnp
from jax import lax
from jax.experimental import pallas as pl
from jax.experimental.pallas import tpu as pltpu
from jax.sharding import PartitionSpec as P


STEPS = 2
SUB = 2


time_step = 0.1
viscosity = 0.1
heat_diff = 0.08
salt_diff = 0.06
therm_coef = 0.2
haline_coef = 0.15
gravity = 0.5
coriolis = 0.6
vert_ratio = 0.25
tracer_step = 0.1
tracer_diff = 0.1
water_atten = 0.04
chl_atten = 0.05
growth_rate = 0.8
heat_gain = 10.0


def extended(block, sides, width, periodic):
    for axis, dim in sides:
        count = lax.axis_size(axis)
        forward = [(i, i + 1) for i in range(count - 1)]
        if periodic:
            forward.append((count - 1, 0))
        backward = [(target, source) for source, target in forward]
        low = lax.ppermute(
            lax.slice_in_dim(block, block.shape[dim] - width, None, axis=dim), axis, forward
        )
        high = lax.ppermute(lax.slice_in_dim(block, 0, width, axis=dim), axis, backward)
        block = jnp.concatenate([low, block, high], axis=dim)
    return block


def laplace_rows(field):
    center = field[:, 1:-1, :]
    return (
        jnp.roll(center, 1, 2)
        + jnp.roll(center, -1, 2)
        + field[:, 2:, :]
        + field[:, :-2, :]
        - 4.0 * center
    )


def ocean_core(padded, wet_mask, lat_start, total_lat):
    speed_u, speed_v, temper, salty = (padded[0], padded[1], padded[2], padded[3])
    east_mid = speed_u[:, 1:-1, :]
    north_mid = speed_v[:, 1:-1, :]
    temp_mid = temper[:, 1:-1, :]
    salt_mid = salty[:, 1:-1, :]
    pressure = gravity * jnp.cumsum(haline_coef * salty - therm_coef * temper, axis=0)
    press_mid = pressure[:, 1:-1, :]
    row_index = (lat_start + jnp.arange(wet_mask.shape[1], dtype=jnp.int32)).astype(jnp.float32)
    spin_rate = (coriolis * (2.0 * (row_index + 0.5) / total_lat - 1.0))[None, :, None]
    slope_east = 0.5 * (jnp.roll(press_mid, -1, 2) - jnp.roll(press_mid, 1, 2))
    slope_north = 0.5 * (pressure[:, 2:, :] - pressure[:, :-2, :])
    new_u = wet_mask * (
        east_mid
        + time_step * (spin_rate * north_mid - slope_east + viscosity * laplace_rows(speed_u))
    )
    new_v = wet_mask * (
        north_mid
        + time_step * (-spin_rate * east_mid - slope_north + viscosity * laplace_rows(speed_v))
    )
    new_s = wet_mask * (salt_mid + time_step * salt_diff * laplace_rows(salty))
    part_t = temp_mid + time_step * heat_diff * laplace_rows(temper)
    spread = 0.5 * (jnp.roll(east_mid, -1, 2) - jnp.roll(east_mid, 1, 2)) + 0.5 * (
        speed_v[:, 2:, :] - speed_v[:, :-2, :]
    )
    rise_flux = -vert_ratio * jnp.flip(jnp.cumsum(jnp.flip(spread, 0), axis=0), 0)
    fluxes = jnp.stack([east_mid, north_mid, rise_flux])
    return (new_u, new_v, part_t, new_s, fluxes)


def light_field(plankton):
    chloro = jax.nn.softplus(plankton)
    attenuate = water_atten + chl_atten * chloro
    depth = jnp.cumsum(attenuate, axis=0) - attenuate
    row_index = jnp.arange(plankton.shape[-1], dtype=jnp.int32).astype(jnp.float32)
    place = 2.0 * (row_index + 0.5) / plankton.shape[-1] - 1.0
    surface = 1.0 - 0.5 * place * place
    top_light = surface * jnp.exp(-depth)
    return (chloro, top_light, top_light * (1.0 - jnp.exp(-attenuate)))


def tracer_core(tracer_ext, flux_ext, sea_mask, onehot, rate_table):
    center = tracer_ext[:, :, 1:-1, :]
    east_face = 0.5 * (flux_ext[0, :, :-1, :] + flux_ext[0, :, 1:, :])
    across = (
        jnp.maximum(east_face, 0.0) * tracer_ext[:, :, :-1, :]
        + jnp.minimum(east_face, 0.0) * tracer_ext[:, :, 1:, :]
    )
    div_east = across[:, :, 1:, :] - across[:, :, :-1, :]
    north_speed = flux_ext[1, :, 1:-1, :]
    north_face = 0.5 * (north_speed[:, :, :-1] + north_speed[:, :, 1:])
    along = (
        jnp.maximum(north_face, 0.0) * center[..., :-1]
        + jnp.minimum(north_face, 0.0) * center[..., 1:]
    )
    along = jnp.pad(along, ((0, 0), (0, 0), (0, 0), (1, 1)))
    div_north = along[..., 1:] - along[..., :-1]
    rise_face = flux_ext[2, 1:, 1:-1, :]
    upward = (
        jnp.maximum(rise_face, 0.0) * center[:, 1:] + jnp.minimum(rise_face, 0.0) * center[:, :-1]
    )
    upward = jnp.pad(upward, ((0, 0), (1, 1), (0, 0), (0, 0)))
    div_up = upward[:, :-1] - upward[:, 1:]
    side = jnp.pad(center, ((0, 0), (0, 0), (0, 0), (1, 1)))
    diffuse = (
        tracer_ext[:, :, 2:, :]
        + tracer_ext[:, :, :-2, :]
        + side[..., 2:]
        + side[..., :-2]
        - 4.0 * center
    )
    chloro, top_light, _ = light_field(center[0])
    nutrient = center[1] * center[1]
    uptake = growth_rate * top_light * chloro * nutrient / (1.0 + nutrient)
    rate_cell = jnp.einsum("bst,bij->stij", rate_table, onehot, precision=lax.Precision.HIGHEST)
    reaction = jnp.einsum("stij,tkij->skij", rate_cell, center, precision=lax.Precision.HIGHEST)
    reaction = reaction.at[0].add(uptake).at[1].add(-uptake)
    tendency = tracer_diff * diffuse + reaction - (div_east + div_north + div_up)
    return sea_mask[None] * (center + tracer_step * tendency)


def general_shards(ocean_state, bottom, tracers, land_sea, biome_id, rate_table):
    levels = ocean_state.shape[1]
    lat_rows = ocean_state.shape[2]
    lat_count = lax.axis_size("lat")
    total_lat = lat_rows * lat_count
    lat_start = lax.axis_index("lat") * lat_rows
    wet_mask = (jnp.arange(levels, dtype=jnp.int32)[:, None, None] < bottom[None]).astype(
        jnp.float32
    )
    sea_mask = land_sea.astype(jnp.float32)
    onehot = (
        biome_id[None] == jnp.arange(rate_table.shape[0], dtype=jnp.int32)[:, None, None]
    ).astype(jnp.float32)
    state = ocean_state
    tracer_now = tracers
    for _ in range(STEPS):
        state = state * wet_mask[None]
        padded = extended(state, (("lat", 2),), 1, False)
        new_u, new_v, part_t, new_s, fluxes = ocean_core(padded, wet_mask, lat_start, total_lat)
        flux_t = lax.all_to_all(
            jnp.transpose(fluxes, (0, 1, 3, 2)), "lat", split_axis=2, concat_axis=3, tiled=True
        )
        tracer_now = tracer_now * sea_mask[None]
        flux_ext = extended(flux_t, (("lat", 2),), 1, True)
        for _ in range(SUB):
            tracer_ext = extended(tracer_now, (("lat", 2),), 1, True)
            tracer_now = tracer_core(tracer_ext, flux_ext, sea_mask, onehot, rate_table)
        heating = heat_gain * sea_mask * light_field(tracer_now[0])[2]
        heat_ocean = jnp.transpose(
            lax.all_to_all(heating, "lat", split_axis=2, concat_axis=1, tiled=True), (0, 2, 1)
        )
        new_t = wet_mask * (part_t + time_step * heat_ocean)
        state = jnp.stack([new_u, new_v, new_t, new_s])
    return (state, tracer_now)


HALO = STEPS * SUB
LANES = 128
TILE = 8
FIELDS = 4
GRANT = 16 * 1024 * 1024


def fits(ocean_state, tracers, lat_count):
    _, levels, lat_rows, total_lon = ocean_state.shape
    species, _, columns, total_lat = tracers.shape
    return (
        lat_rows == 2
        and HALO == TILE // 2
        and lat_rows * lat_count == total_lat
        and columns * lat_count == total_lon
        and columns % TILE == 0
        and LANES % total_lat == 0
        and (columns + 2 * HALO) * total_lat == TILE * LANES
        and 2 * FIELDS * levels == LANES
        and levels <= columns + HALO
        and 2 * columns + 3 * HALO <= FIELDS * levels
        and species == 2 * TILE
        and lat_count % 2 == 0
        and levels % (LANES // total_lat) == 0
    )


def rows_of(shape=(TILE, LANES)):
    return lax.broadcasted_iota(jnp.int32, shape, 0)


def lanes_of(shape=(TILE, LANES)):
    return lax.broadcasted_iota(jnp.int32, shape, 1)


def spin(block, amount, axis):
    size = block.shape[axis]
    amount = amount % size
    return block if amount == 0 else pltpu.roll(block, amount, axis)


def swap_halves(block):
    low_row, low_lane = rows_of() < TILE // 2, lanes_of() < LANES // 2
    other = spin(spin(block, LANES // 2, 1), TILE // 2, 0)
    return jnp.where(low_row == low_lane, block, other)


def pack_ocean(ocean_ref, bottom_ref, out_ref, flat, depth):
    fields, levels, lat_rows, total_lon = ocean_ref.shape
    half = fields * levels
    count = out_ref.shape[0] // (4 * TILE)
    columns = total_lon // count
    own = columns // TILE
    for index in range(half):
        field, level = divmod(index, levels)
        for row in range(lat_rows):
            flat[row * half + index : row * half + index + 1, :] = ocean_ref[field, level, row : row + 1, :]
    turned = flat[...].T
    tiles = [turned[TILE * i : TILE * (i + 1), :] for i in range(total_lon // TILE)]
    swapped = [swap_halves(t) for t in tiles]
    depth[...] = jnp.zeros(depth.shape, jnp.float32)
    depth[3:4, :] = bottom_ref[0:1, :].astype(jnp.float32)
    depth[7:8, :] = bottom_ref[1:2, :].astype(jnp.float32)
    line = depth[...]
    row, lane = rows_of(), lanes_of()
    width = columns + 2 * HALO
    window = (row % 4 == 3) & (lane >= width - HALO) & (lane < 2 * width - HALO)
    for target in range(count):
        for q in range(own):
            out_ref[pl.ds((target * (own + 1) + q) * TILE, TILE), :] = swapped[target * own + q]
        east = tiles[(target * own + own) % len(tiles)]
        west = tiles[target * own - 1]
        edge = swap_halves(jnp.where(row < HALO, east, west))
        level_line = spin(line, width - target * columns, 1)[:, :LANES]
        out_ref[pl.ds((target * (own + 1) + own) * TILE, TILE), :] = jnp.where(window, level_line, edge)


def pack_edges(low_ref, high_ref, sea_ref, biome_ref, first_ref, second_ref, even):
    species, levels, _, total_lat = low_ref.shape
    columns = sea_ref.shape[1]
    blocks = LANES // total_lat
    groups = levels // blocks
    low = rows_of((TILE, total_lat)) < HALO
    last = columns - TILE

    def put(start, both):
        flipped = spin(both, HALO, 0)
        here = jnp.where(even, flipped, both)
        first_ref[start : start + HALO, :] = here[:HALO, :]
        second_ref[start : start + HALO, :] = here[HALO:, :]

    for group in range(groups):
        wet = [
            jnp.where(low, sea_ref[group * blocks + b, 0:TILE, :], sea_ref[group * blocks + b, last:columns, :]).astype(
                jnp.float32
            )
            for b in range(blocks)
        ]
        joined = jnp.concatenate(wet, axis=1)
        put(species * groups * HALO + group * HALO, joined)
        for kind in range(species):
            parts = [
                jnp.where(low, low_ref[kind, group * blocks + b], high_ref[kind, group * blocks + b])
                for b in range(blocks)
            ]
            put((kind * groups + group) * HALO, jnp.concatenate(parts, axis=1) * joined)
    biome = jnp.where(low, biome_ref[0:TILE, :], biome_ref[last:columns, :]).astype(jnp.float32)
    start = (species + 1) * groups * HALO
    put(start, jnp.concatenate([biome] * blocks, axis=1))
    first_ref[start + HALO : start + 2 * HALO, :] = jnp.zeros((HALO, LANES), jnp.float32)
    second_ref[start + HALO : start + 2 * HALO, :] = jnp.zeros((HALO, LANES), jnp.float32)


def fetch(sources, targets, ready):
    copies = [pltpu.make_async_copy(a, b, ready.at[i]) for i, (a, b) in enumerate(zip(sources, targets, strict=True))]
    for copy in copies:
        copy.start()
    return copies


def is_even():
    return lax.axis_index("lat") % 2 == 0


def pack(ocean, bottom, tracers, sea, biome, *refs):
    out, edges, (flat, depth), held, result, ready, gone = refs[0], refs[1:3], refs[3:5], refs[5:11], refs[11], refs[12], refs[13]
    columns = tracers.shape[2]
    sources = [ocean, bottom, tracers.at[:, :, 0:TILE, :], tracers.at[:, :, columns - TILE : columns, :], sea, biome]
    copies = fetch(sources, held, ready)
    copies[0].wait()
    copies[1].wait()
    pack_ocean(held[0], held[1], result, flat, depth)
    leaving = pltpu.make_async_copy(result, out, gone)
    leaving.start()
    for copy in copies[2:]:
        copy.wait()
    pack_edges(*held[2:], *edges, is_even())
    leaving.wait()


def light(plankton, surface):
    result = []
    depth = jnp.zeros(surface.shape, jnp.float32)
    for value in plankton:
        chloro = jnp.maximum(value, 0.0) + jnp.log(1.0 + jnp.exp(-jnp.abs(value)))
        attenuate = water_atten + chl_atten * chloro
        result.append((chloro, surface * jnp.exp(-depth), attenuate))
        depth = depth + attenuate
    return result


def surface_light(total_lat):
    row_index = (lanes_of() % total_lat).astype(jnp.float32)
    place = 2.0 * (row_index + 0.5) / total_lat - 1.0
    return 1.0 - 0.5 * place * place


def planes_of(ref, kind, levels, species, base=0):
    return [ref[pl.ds(base + level * TILE * species + kind, TILE, stride=species), :] for level in range(levels)]


def put_growth(growth_ref, tracer_ref, levels, species, total_lat, base=0):
    lit = light(planes_of(tracer_ref, 0, levels, species, base), surface_light(total_lat))
    food = planes_of(tracer_ref, 1, levels, species, base)
    for level, (chloro, top_light, _) in enumerate(lit):
        nutrient = food[level] * food[level]
        uptake = growth_rate * top_light * chloro * nutrient / (1.0 + nutrient)
        growth_ref[level * TILE : (level + 1) * TILE, :] = tracer_step * uptake
    return lit


def rate_pieces(rate_table_ref):
    kinds, species, _ = rate_table_ref.shape
    rates = tracer_step * rate_table_ref[...].reshape(kinds * species, species)
    high = rates.astype(jnp.bfloat16)
    low = (rates - high.astype(jnp.float32)).astype(jnp.bfloat16)
    return jnp.concatenate([high, low, high], axis=1)


def reaction(source_ref, base, pieces, chosen, growth_ref, row, levels, species):
    index = rows_of()
    sign = jnp.where(index == 0, 1.0, jnp.where(index == 1, -1.0, 0.0))
    sums = []
    for pair in range(0, len(levels), 2):
        near = levels[pair : pair + 2]
        values = jnp.concatenate(
            [source_ref[pl.ds(base + (level * TILE + row) * species, species), :] for level in near], axis=1
        )
        high = values.astype(jnp.bfloat16)
        low = (values - high.astype(jnp.float32)).astype(jnp.bfloat16)
        every = jnp.dot(
            pieces, jnp.concatenate([high, high, low], axis=0), preferred_element_type=jnp.float32
        )
        for place, level in enumerate(near):
            mine = every[:, place * LANES : (place + 1) * LANES]
            total = mine[:species, :]
            for kind, mask in enumerate(chosen):
                total = jnp.where(mask, mine[(kind + 1) * species : (kind + 2) * species, :], total)
            uptake = sign * growth_ref[pl.ds(level * TILE + row, TILE, stride=0), :]
            sums.append(jnp.concatenate([total[:TILE, :] + uptake, total[TILE:, :]], axis=0))
    return sums


def biome_masks(biome_ref, row, kinds, species):
    here = jnp.broadcast_to(biome_ref[row : row + 1, :], (species, LANES))
    return [here == float(kind) for kind in range(1, kinds)]


def prepare_own(tracers, sea, biome, rate_table, own_ref, wet_ref, biomes_ref, pieces_ref, *refs):
    held, ready = refs[:4], refs[4]
    tracer_ref, sea_ref, biome_ref, rate_table_ref = held
    species, levels, columns, total_lat = tracers.shape
    own = columns // TILE
    copies = fetch([tracers, sea, biome, rate_table], held, ready)
    blank = jnp.zeros((TILE, total_lat), jnp.float32)
    for copy in copies[1:]:
        copy.wait()

    def plane(parts):
        return jnp.concatenate(parts + [blank], axis=1)

    pieces_ref[...] = rate_pieces(rate_table_ref)
    biomes_ref[...] = plane([biome_ref[TILE * q : TILE * (q + 1), :].astype(jnp.float32) for q in range(own)])
    for level in range(levels):
        parts = [sea_ref[level, TILE * q : TILE * (q + 1), :].astype(jnp.float32) for q in range(own)]
        wet_ref[level * TILE : (level + 1) * TILE, :] = plane(parts)
    copies[0].wait()
    for level in range(levels):
        wet = wet_ref[level * TILE : (level + 1) * TILE, :]
        for kind in range(species):
            parts = [tracer_ref[kind, level, TILE * q : TILE * (q + 1), :] for q in range(own)]
            own_ref[pl.ds(level * TILE * species + kind, TILE, stride=species), :] = plane(parts) * wet


def prepare_all(
    own_ref, own_wet_ref, own_biomes_ref, pieces_ref, from_first, from_second, now_ref, wet_ref, biomes_ref, first_ref, growth, sizes
):
    levels, species, total_lat, columns, kinds = sizes
    blocks = LANES // total_lat
    groups = levels // blocks
    inner = lanes_of() < columns // TILE * total_lat
    even = is_even()

    def halo(start):
        both = jnp.concatenate([from_first[start : start + HALO, :], from_second[start : start + HALO, :]], axis=0)
        return jnp.where(even, both, spin(both, HALO, 0))

    def joined(inside, edge, block):
        return jnp.where(inner, inside, spin(edge, LANES - (block + 1) * total_lat, 1))

    for group in range(groups):
        edge = halo((species * groups + group) * HALO)
        for block in range(blocks):
            place = slice((group * blocks + block) * TILE, (group * blocks + block + 1) * TILE)
            wet_ref[place, :] = joined(own_wet_ref[place, :], edge, block)
    biomes_ref[...] = joined(own_biomes_ref[...], halo((species + 1) * groups * HALO), 0)
    for kind in range(species):
        for group in range(groups):
            edge = halo((kind * groups + group) * HALO)
            for block in range(blocks):
                place = pl.ds((group * blocks + block) * TILE * species + kind, TILE, stride=species)
                now_ref[place, :] = joined(own_ref[place, :], edge, block)
    put_growth(growth, now_ref, levels, species, total_lat)
    pieces = pieces_ref[...]
    for row in range(TILE):
        chosen = biome_masks(biomes_ref, row, kinds, species)
        every = list(range(levels))
        for level, change in zip(every, reaction(now_ref, 0, pieces, chosen, growth, row, every, species), strict=True):
            mask = wet_ref[pl.ds(level * TILE + row, species, stride=0), :]
            first_ref[pl.ds((level * TILE + row) * species, species), :] = mask * change


def advance(
    received, now_ref, wet_ref, biomes_ref, pieces_ref, first_ref, sent_out, last_ref, sent, work, ocean, coef, tracer, growth,
    done, sizes,
):
    levels, species, total_lat, columns, kinds = sizes
    pieces = pieces_ref[...]
    count = total_lat // 2
    own = columns // TILE
    half = FIELDS * levels
    row, lane = rows_of(), lanes_of()
    lat = lane % total_lat
    width = columns + 2 * HALO

    for r_low in range(4):
        for q in range(own + 1):
            for j in range(2):
                work[pl.ds(r_low * LANES + q * total_lat + j, count, stride=2), :] = received[
                    pl.ds(q * TILE + j * 4 + r_low, count, stride=(own + 1) * TILE), :
                ]
    turned = None
    for r_low in range(4):
        turned = work[r_low * LANES : (r_low + 1) * LANES, :].T
        for r_high in range(2):
            ocean[pl.ds(r_high * 4 + r_low, half, stride=TILE), :] = turned[r_high * half : (r_high + 1) * half, :]
    floors = [turned[width + TILE * q : width + TILE * (q + 1), :] for q in range(own)]
    floors.append(
        jnp.where(row < HALO, turned[width + columns : width + columns + TILE, :], turned[width - TILE : width, :])
    )
    floor = floors[own]
    for q in range(own):
        floor = jnp.where(lane // total_lat == q, spin(floors[q], (q - own) * total_lat, 1), floor)
    wet = [(float(level) < floor).astype(jnp.float32) for level in range(levels)]
    sea = [wet_ref[level * TILE : (level + 1) * TILE, :] for level in range(levels)]

    def read(field):
        return [ocean[(field * levels + k) * TILE : (field * levels + k + 1) * TILE, :] for k in range(levels)]

    def write(field, values):
        for k in range(levels):
            ocean[(field * levels + k) * TILE : (field * levels + k + 1) * TILE, :] = values[k]

    def east(x):
        y = spin(x, -1, 0)
        return jnp.where(row == TILE - 1, spin(y, -total_lat, 1), y)

    def west(x):
        y = spin(x, 1, 0)
        return jnp.where(row == 0, spin(y, total_lat, 1), y)

    def north(x):
        return jnp.where(lat == total_lat - 1, 0.0, spin(x, -1, 1))

    def south(x):
        return jnp.where(lat == 0, 0.0, spin(x, 1, 1))

    spin_rate = coriolis * (2.0 * (lat.astype(jnp.float32) + 0.5) / total_lat - 1.0)
    plane = levels * TILE

    def dynamics(step):
        speed_u, speed_v, temper, salty = read(0), read(1), read(2), read(3)
        spread, new_u, new_v = [], [], []
        pressure = None
        for k in range(levels):
            u, v = speed_u[k], speed_v[k]
            part = gravity * (haline_coef * salty[k] - therm_coef * temper[k])
            pressure = part if pressure is None else pressure + part
            slope_east = 0.5 * (east(pressure) - west(pressure))
            slope_north = 0.5 * (north(pressure) - south(pressure))
            u_east, u_west, v_north, v_south = east(u), west(u), north(v), south(v)
            lap_u = u_east + u_west + north(u) + south(u) - 4.0 * u
            lap_v = east(v) + west(v) + v_north + v_south - 4.0 * v
            new_u.append(wet[k] * (u + time_step * (spin_rate * v - slope_east + viscosity * lap_u)))
            new_v.append(wet[k] * (v + time_step * (-spin_rate * u - slope_north + viscosity * lap_v)))
            spread.append(0.5 * (u_east - u_west) + 0.5 * (v_north - v_south))
            face_east = 0.5 * (u + u_east)
            face_west = west(face_east)
            face_north = jnp.where(lat == total_lat - 1, 0.0, 0.5 * (v + v_north))
            face_south = spin(face_north, 1, 1)
            up_east, down_east = jnp.maximum(face_east, 0.0), jnp.minimum(face_east, 0.0)
            up_west, down_west = jnp.maximum(face_west, 0.0), jnp.minimum(face_west, 0.0)
            up_north, down_north = jnp.maximum(face_north, 0.0), jnp.minimum(face_north, 0.0)
            up_south, down_south = jnp.maximum(face_south, 0.0), jnp.minimum(face_south, 0.0)
            mask = tracer_step * sea[k]
            at = step * 7 * plane + k * TILE
            coef[pl.ds(at + plane, TILE), :] = mask * (tracer_diff - down_east)
            coef[pl.ds(at + 2 * plane, TILE), :] = mask * (tracer_diff + up_west)
            coef[pl.ds(at + 3 * plane, TILE), :] = jnp.where(
                lat == total_lat - 1, 0.0, mask * (tracer_diff - down_north)
            )
            coef[pl.ds(at + 4 * plane, TILE), :] = jnp.where(lat == 0, 0.0, mask * (tracer_diff + up_south))
            coef[pl.ds(at, TILE), :] = -4.0 * tracer_diff - up_east + down_west - up_north + down_south
        total = jnp.zeros((TILE, LANES), jnp.float32)
        below_up, below_down = total, total
        for k in reversed(range(levels)):
            total = total + spread[k]
            rise = -vert_ratio * total if k > 0 else jnp.zeros((TILE, LANES), jnp.float32)
            up, down = jnp.maximum(rise, 0.0), jnp.minimum(rise, 0.0)
            mask = tracer_step * sea[k]
            at = step * 7 * plane + k * TILE
            coef[pl.ds(at, TILE), :] = sea[k] + mask * (coef[pl.ds(at, TILE), :] - up + below_down)
            coef[pl.ds(at + 5 * plane, TILE), :] = -mask * down
            coef[pl.ds(at + 6 * plane, TILE), :] = mask * below_up
            below_up, below_down = up, down
        for field, values, rate in ((2, temper, heat_diff), (3, salty, salt_diff)):
            fresh = []
            for k in range(levels):
                x = values[k]
                lap = east(x) + west(x) + north(x) + south(x) - 4.0 * x
                y = x + time_step * rate * lap
                fresh.append(wet[k] * y if field == 3 else y)
            write(field, fresh)
        write(0, new_u)
        write(1, new_v)

    def substep(step, source, base, target, target_base, ready):
        start = step * 7 * plane

        def body(group, carry):
            near = [group * 4 + i for i in range(4)]
            for r in range(TILE):
                if ready is None:
                    chosen = biome_masks(biomes_ref, r, kinds, species)
                    sums = reaction(source, base, pieces, chosen, growth, r, near, species)
                for place, level in enumerate(near):
                    cell = level * TILE + r
                    above = max(level - 1, 0) * TILE + r
                    under = min(level + 1, levels - 1) * TILE + r
                    weight = [coef[pl.ds(start + i * plane + cell, species, stride=0), :] for i in range(7)]
                    mask = None if ready is not None else wet_ref[pl.ds(cell, species, stride=0), :]

                    def take(index):
                        return source[pl.ds(base + index * species, species), :]

                    x = take(cell)
                    x_east = take(cell + 1) if r < TILE - 1 else spin(take(cell - r), -total_lat, 1)
                    x_west = take(cell - 1) if r > 0 else spin(take(cell + TILE - 1), total_lat, 1)
                    change = mask * sums[place] if ready is None else ready[pl.ds(cell * species, species), :]
                    value = (
                        (weight[0] * x + weight[1] * x_east)
                        + (weight[2] * x_west + weight[3] * spin(x, -1, 1))
                        + (weight[4] * spin(x, 1, 1) + weight[5] * take(above))
                        + (weight[6] * take(under) + change)
                    )
                    target[pl.ds(target_base + cell * species, species), :] = value
            return carry

        for group in range(levels // 4):
            body(group, 0)

    for field in range(FIELDS):
        write(field, [wet[k] * x for k, x in enumerate(read(field))])
    size = levels * TILE * species
    source, base = now_ref, 0
    lit = None
    for step in range(STEPS):
        dynamics(step)
        for sub in range(SUB):
            last = step == STEPS - 1 and sub == SUB - 1
            first = step == 0 and sub == 0
            target, target_base = (last_ref, 0) if last else (tracer, ((step * SUB + sub) % 2) * size)
            if not first:
                put_growth(growth, source, levels, species, total_lat, base)
            substep(step, source, base, target, target_base, first_ref if first else None)
            source, base = target, target_base
        lit = light(planes_of(source, 0, levels, species, base), surface_light(total_lat))
        warm = []
        for k, x in enumerate(read(2)):
            _, top_light, attenuate = lit[k]
            heating = heat_gain * sea[k] * (top_light * (1.0 - jnp.exp(-attenuate)))
            warm.append(wet[k] * (x + time_step * heating))
        write(2, warm)

    for r_low in range(4):
        both = jnp.concatenate(
            [ocean[pl.ds(r_high * 4 + r_low, half, stride=TILE), :] for r_high in range(2)], axis=0
        )
        work[r_low * LANES : (r_low + 1) * LANES, :] = both.T
        for q in range(own):
            for j in range(2):
                sent[pl.ds(q * TILE + j * 4 + r_low, count, stride=own * TILE), :] = work[
                    pl.ds(r_low * LANES + q * total_lat + j, count, stride=2), :
                ]
    send = pltpu.make_async_copy(sent, sent_out, done)
    send.start()
    send.wait()


def unpack_tracers(last_ref, out_ref):
    species, levels, columns, total_lat = out_ref.shape
    for level in range(levels):
        for kind in range(species):
            whole = last_ref[pl.ds(level * TILE * species + kind, TILE, stride=species), :]
            for q in range(columns // TILE):
                out_ref[kind, level, TILE * q : TILE * (q + 1), :] = whole[:, q * total_lat : (q + 1) * total_lat]


def unpack_ocean(received, out_ref, turned, flat):
    fields, levels, lat_rows, total_lon = out_ref.shape
    half = fields * levels
    for i in range(total_lon // TILE):
        turned[TILE * i : TILE * (i + 1), :] = swap_halves(received[TILE * i : TILE * (i + 1), :])
    flat[...] = turned[...].T
    for index in range(half):
        field, level = divmod(index, levels)
        for row in range(lat_rows):
            out_ref[field, level, row : row + 1, :] = flat[row * half + index : row * half + index + 1, :]


def grids(*shapes):
    return [pltpu.VMEM(shape, jnp.float32) for shape in shapes]


def far(*shape):
    return pltpu.HBM(shape, jnp.float32)


def near(*shape, dtype=jnp.float32):
    return pltpu.VMEM(shape, dtype)


def placed(space, *arrays):
    return [pltpu.with_memory_space_constraint(x, space) for x in arrays]


def shards(ocean_state, bottom, tracers, land_sea, biome_id, rate_table):
    count = lax.axis_size("lat")
    if not fits(ocean_state, tracers, count):
        return general_shards(ocean_state, bottom, tracers, land_sea, biome_id, rate_table)
    _, levels, _, total_lon = ocean_state.shape
    species, _, columns, total_lat = tracers.shape
    cells = levels * TILE
    size = cells * species
    own = columns // TILE

    edge_rows = (species + 1) * (levels * total_lat // LANES) * HALO + 2 * HALO
    kinds = rate_table.shape[0]
    roomy = pltpu.CompilerParams(vmem_limit_bytes=GRANT)
    ocean_state, bottom, tracers, land_sea, biome_id, rate_table = placed(
        pltpu.HBM, ocean_state, bottom, tracers, land_sea, biome_id, rate_table
    )
    vmem = pl.BlockSpec(memory_space=pltpu.VMEM)
    hbm = pl.BlockSpec(memory_space=pltpu.HBM)

    pairs = [(i, i ^ 1) for i in range(count)]
    others = [((a + 1) % count, (b + 1) % count) for a, b in pairs]
    sizes = (levels, species, total_lat, columns, kinds)
    edge_shape = (species, levels, TILE, total_lat)

    packed, to_first, to_second = pl.pallas_call(
        pack,
        out_shape=[far(count * (own + 1) * TILE, LANES), near(edge_rows, LANES), near(edge_rows, LANES)],
        in_specs=[hbm] * 5,
        out_specs=[hbm, vmem, vmem],
        scratch_shapes=grids((LANES, total_lon), (TILE, total_lon), ocean_state.shape)
        + [pltpu.VMEM(bottom.shape, bottom.dtype)]
        + grids(edge_shape, edge_shape)
        + [pltpu.VMEM(x.shape, x.dtype) for x in (land_sea, biome_id)]
        + grids((count * (own + 1) * TILE, LANES))
        + [pltpu.SemaphoreType.DMA((6,)), pltpu.SemaphoreType.DMA],
        compiler_params=roomy,
        name="pack",
    )(ocean_state, bottom, tracers, land_sea, biome_id)
    received = lax.all_to_all(
        packed.reshape(count, (own + 1) * TILE, LANES), "lat", split_axis=0, concat_axis=0, tiled=True
    ).reshape(packed.shape)
    from_first = lax.ppermute(to_first, "lat", pairs)
    from_second = lax.ppermute(to_second, "lat", others)
    from_first, from_second, received = placed(pltpu.VMEM, from_first, from_second, received)

    inside = pl.pallas_call(
        prepare_own,
        out_shape=[
            near(size, LANES),
            near(cells, LANES),
            near(TILE, LANES),
            near(kinds * species, 3 * species, dtype=jnp.bfloat16),
        ],
        in_specs=[hbm] * 4,
        out_specs=[vmem] * 4,
        scratch_shapes=[pltpu.VMEM(x.shape, x.dtype) for x in (tracers, land_sea, biome_id, rate_table)]
        + [pltpu.SemaphoreType.DMA((4,))],
        compiler_params=roomy,
        name="prepare_own",
    )(tracers, land_sea, biome_id, rate_table)
    pieces = inside[3]

    def prepare(*refs):
        prepare_all(*refs, sizes)

    now, wet, biomes, first = pl.pallas_call(
        prepare,
        out_shape=[near(size, LANES), near(cells, LANES), near(TILE, LANES), near(size, LANES)],
        in_specs=[vmem] * 6,
        out_specs=[vmem] * 4,
        scratch_shapes=grids((cells, LANES)),
        compiler_params=roomy,
        name="prepare",
    )(*inside, from_first, from_second)

    def run(*refs):
        advance(*refs, sizes)

    sent, last = pl.pallas_call(
        run,
        out_shape=[far(count * own * TILE, LANES), near(size, LANES)],
        in_specs=[vmem] * 6,
        out_specs=[hbm, vmem],
        scratch_shapes=grids(
            (count * own * TILE, LANES),
            (4 * LANES, LANES),
            (FIELDS * cells, LANES),
            (STEPS * 7 * cells, LANES),
            (2 * size, LANES),
            (cells, LANES),
        )
        + [pltpu.SemaphoreType.DMA],
        compiler_params=pltpu.CompilerParams(vmem_limit_bytes=GRANT),
        name="advance",
    )(received, now, wet, biomes, pieces, first)
    back = lax.all_to_all(
        sent.reshape(count, own * TILE, LANES), "lat", split_axis=0, concat_axis=0, tiled=True
    ).reshape(sent.shape)
    (back,) = placed(pltpu.VMEM, back)
    (last,) = placed(pltpu.VMEM, last)
    tracers_out = pl.pallas_call(
        unpack_tracers,
        out_shape=far(*tracers.shape),
        in_specs=[vmem],
        out_specs=vmem,
        compiler_params=roomy,
        name="unpack_tracers",
    )(last)
    state_out = pl.pallas_call(
        unpack_ocean,
        out_shape=far(*ocean_state.shape),
        in_specs=[vmem],
        out_specs=vmem,
        scratch_shapes=grids((total_lon, LANES), (LANES, total_lon)),
        compiler_params=roomy,
        name="unpack_ocean",
    )(back)
    return (state_out, tracers_out)


def solution(mesh):
    in_specs = (
        P(None, None, ("groups", "lat"), None),
        P(("groups", "lat"), None),
        P(None, None, ("groups", "lat"), None),
        P(None, ("groups", "lat"), None),
        P(("groups", "lat"), None),
        P(),
    )
    out_specs = (P(None, None, ("groups", "lat"), None), P(None, None, ("groups", "lat"), None))
    return jax.shard_map(shards, mesh=mesh, in_specs=in_specs, out_specs=out_specs, check_vma=False)
```

```python
import jax
import jax.numpy as jnp
from jax import lax
from jax.experimental import pallas as pl
from jax.experimental.pallas import tpu as pltpu
from jax.sharding import PartitionSpec as P


STEPS = 2
SUB = 2


time_step = 0.1
viscosity = 0.1
heat_diff = 0.08
salt_diff = 0.06
therm_coef = 0.2
haline_coef = 0.15
gravity = 0.5
coriolis = 0.6
vert_ratio = 0.25
tracer_step = 0.1
tracer_diff = 0.1
water_atten = 0.04
chl_atten = 0.05
growth_rate = 0.8
heat_gain = 10.0


def extended(block, sides, width, periodic):
    for axis, dim in sides:
        count = lax.axis_size(axis)
        forward = [(i, i + 1) for i in range(count - 1)]
        if periodic:
            forward.append((count - 1, 0))
        backward = [(target, source) for source, target in forward]
        low = lax.ppermute(
            lax.slice_in_dim(block, block.shape[dim] - width, None, axis=dim), axis, forward
        )
        high = lax.ppermute(lax.slice_in_dim(block, 0, width, axis=dim), axis, backward)
        block = jnp.concatenate([low, block, high], axis=dim)
    return block


def laplace_rows(field):
    center = field[:, 1:-1, :]
    return (
        jnp.roll(center, 1, 2)
        + jnp.roll(center, -1, 2)
        + field[:, 2:, :]
        + field[:, :-2, :]
        - 4.0 * center
    )


def ocean_core(padded, wet_mask, lat_start, total_lat):
    speed_u, speed_v, temper, salty = (padded[0], padded[1], padded[2], padded[3])
    east_mid = speed_u[:, 1:-1, :]
    north_mid = speed_v[:, 1:-1, :]
    temp_mid = temper[:, 1:-1, :]
    salt_mid = salty[:, 1:-1, :]
    pressure = gravity * jnp.cumsum(haline_coef * salty - therm_coef * temper, axis=0)
    press_mid = pressure[:, 1:-1, :]
    row_index = (lat_start + jnp.arange(wet_mask.shape[1], dtype=jnp.int32)).astype(jnp.float32)
    spin_rate = (coriolis * (2.0 * (row_index + 0.5) / total_lat - 1.0))[None, :, None]
    slope_east = 0.5 * (jnp.roll(press_mid, -1, 2) - jnp.roll(press_mid, 1, 2))
    slope_north = 0.5 * (pressure[:, 2:, :] - pressure[:, :-2, :])
    new_u = wet_mask * (
        east_mid
        + time_step * (spin_rate * north_mid - slope_east + viscosity * laplace_rows(speed_u))
    )
    new_v = wet_mask * (
        north_mid
        + time_step * (-spin_rate * east_mid - slope_north + viscosity * laplace_rows(speed_v))
    )
    new_s = wet_mask * (salt_mid + time_step * salt_diff * laplace_rows(salty))
    part_t = temp_mid + time_step * heat_diff * laplace_rows(temper)
    spread = 0.5 * (jnp.roll(east_mid, -1, 2) - jnp.roll(east_mid, 1, 2)) + 0.5 * (
        speed_v[:, 2:, :] - speed_v[:, :-2, :]
    )
    rise_flux = -vert_ratio * jnp.flip(jnp.cumsum(jnp.flip(spread, 0), axis=0), 0)
    fluxes = jnp.stack([east_mid, north_mid, rise_flux])
    return (new_u, new_v, part_t, new_s, fluxes)


def light_field(plankton):
    chloro = jax.nn.softplus(plankton)
    attenuate = water_atten + chl_atten * chloro
    depth = jnp.cumsum(attenuate, axis=0) - attenuate
    row_index = jnp.arange(plankton.shape[-1], dtype=jnp.int32).astype(jnp.float32)
    place = 2.0 * (row_index + 0.5) / plankton.shape[-1] - 1.0
    surface = 1.0 - 0.5 * place * place
    top_light = surface * jnp.exp(-depth)
    return (chloro, top_light, top_light * (1.0 - jnp.exp(-attenuate)))


def tracer_core(tracer_ext, flux_ext, sea_mask, onehot, rate_table):
    center = tracer_ext[:, :, 1:-1, :]
    east_face = 0.5 * (flux_ext[0, :, :-1, :] + flux_ext[0, :, 1:, :])
    across = (
        jnp.maximum(east_face, 0.0) * tracer_ext[:, :, :-1, :]
        + jnp.minimum(east_face, 0.0) * tracer_ext[:, :, 1:, :]
    )
    div_east = across[:, :, 1:, :] - across[:, :, :-1, :]
    north_speed = flux_ext[1, :, 1:-1, :]
    north_face = 0.5 * (north_speed[:, :, :-1] + north_speed[:, :, 1:])
    along = (
        jnp.maximum(north_face, 0.0) * center[..., :-1]
        + jnp.minimum(north_face, 0.0) * center[..., 1:]
    )
    along = jnp.pad(along, ((0, 0), (0, 0), (0, 0), (1, 1)))
    div_north = along[..., 1:] - along[..., :-1]
    rise_face = flux_ext[2, 1:, 1:-1, :]
    upward = (
        jnp.maximum(rise_face, 0.0) * center[:, 1:] + jnp.minimum(rise_face, 0.0) * center[:, :-1]
    )
    upward = jnp.pad(upward, ((0, 0), (1, 1), (0, 0), (0, 0)))
    div_up = upward[:, :-1] - upward[:, 1:]
    side = jnp.pad(center, ((0, 0), (0, 0), (0, 0), (1, 1)))
    diffuse = (
        tracer_ext[:, :, 2:, :]
        + tracer_ext[:, :, :-2, :]
        + side[..., 2:]
        + side[..., :-2]
        - 4.0 * center
    )
    chloro, top_light, _ = light_field(center[0])
    nutrient = center[1] * center[1]
    uptake = growth_rate * top_light * chloro * nutrient / (1.0 + nutrient)
    rate_cell = jnp.einsum("bst,bij->stij", rate_table, onehot, precision=lax.Precision.HIGHEST)
    reaction = jnp.einsum("stij,tkij->skij", rate_cell, center, precision=lax.Precision.HIGHEST)
    reaction = reaction.at[0].add(uptake).at[1].add(-uptake)
    tendency = tracer_diff * diffuse + reaction - (div_east + div_north + div_up)
    return sea_mask[None] * (center + tracer_step * tendency)


def general_shards(ocean_state, bottom, tracers, land_sea, biome_id, rate_table):
    levels = ocean_state.shape[1]
    lat_rows = ocean_state.shape[2]
    lat_count = lax.axis_size("lat")
    total_lat = lat_rows * lat_count
    lat_start = lax.axis_index("lat") * lat_rows
    wet_mask = (jnp.arange(levels, dtype=jnp.int32)[:, None, None] < bottom[None]).astype(
        jnp.float32
    )
    sea_mask = land_sea.astype(jnp.float32)
    onehot = (
        biome_id[None] == jnp.arange(rate_table.shape[0], dtype=jnp.int32)[:, None, None]
    ).astype(jnp.float32)
    state = ocean_state
    tracer_now = tracers
    for _ in range(STEPS):
        state = state * wet_mask[None]
        padded = extended(state, (("lat", 2),), 1, False)
        new_u, new_v, part_t, new_s, fluxes = ocean_core(padded, wet_mask, lat_start, total_lat)
        flux_t = lax.all_to_all(
            jnp.transpose(fluxes, (0, 1, 3, 2)), "lat", split_axis=2, concat_axis=3, tiled=True
        )
        tracer_now = tracer_now * sea_mask[None]
        flux_ext = extended(flux_t, (("lat", 2),), 1, True)
        for _ in range(SUB):
            tracer_ext = extended(tracer_now, (("lat", 2),), 1, True)
            tracer_now = tracer_core(tracer_ext, flux_ext, sea_mask, onehot, rate_table)
        heating = heat_gain * sea_mask * light_field(tracer_now[0])[2]
        heat_ocean = jnp.transpose(
            lax.all_to_all(heating, "lat", split_axis=2, concat_axis=1, tiled=True), (0, 2, 1)
        )
        new_t = wet_mask * (part_t + time_step * heat_ocean)
        state = jnp.stack([new_u, new_v, new_t, new_s])
    return (state, tracer_now)


HALO = STEPS * SUB
LANES = 128
TILE = 8
FIELDS = 4
GRANT = 16 * 1024 * 1024


def fits(ocean_state, tracers, lat_count):
    _, levels, lat_rows, total_lon = ocean_state.shape
    species, _, columns, total_lat = tracers.shape
    return (
        lat_rows == 2
        and HALO == TILE // 2
        and lat_rows * lat_count == total_lat
        and columns * lat_count == total_lon
        and columns == 3 * TILE
        and LANES == 4 * total_lat
        and levels == 2 * TILE
        and species == 2 * TILE
        and lat_count % 2 == 0
    )


def rows_of(shape=(TILE, LANES)):
    return lax.broadcasted_iota(jnp.int32, shape, 0)


def lanes_of(shape=(TILE, LANES)):
    return lax.broadcasted_iota(jnp.int32, shape, 1)


def spin(block, amount, axis):
    size = block.shape[axis]
    amount = amount % size
    return block if amount == 0 else pltpu.roll(block, amount, axis)


def pack_ocean(ocean_ref, bottom_ref, own_ref, out_ref, turned, lined):
    fields, levels, lat_rows, total_lon = ocean_ref.shape
    half = fields * levels
    parts = 3
    count = out_ref.shape[0] // (parts * TILE)
    columns = total_lon // count
    own = columns // TILE
    for index in range(half):
        field, level = divmod(index, levels)
        for row in range(lat_rows):
            own_ref[row * half + index : row * half + index + 1, :] = ocean_ref[field, level, row : row + 1, :]
    own_ref[2 * half : 2 * half + TILE, :] = jnp.zeros((TILE, total_lon), jnp.float32)
    for row in range(lat_rows):
        own_ref[2 * half + row : 2 * half + row + 1, :] = bottom_ref[row : row + 1, :].astype(jnp.float32)

    def rows(row, field):
        return own_ref[row * half + field * levels : row * half + (field + 1) * levels, :]

    stack = [rows(row, field) for field in range(2) for row in range(lat_rows)]
    stack += [gravity * (haline_coef * rows(row, 3) - therm_coef * rows(row, 2)) for row in range(lat_rows)]
    stack.append(jnp.zeros((LANES - 2 * parts * levels, total_lon), jnp.float32))
    turned[...] = jnp.concatenate(stack, axis=0).T
    tiles = total_lon // TILE
    group = lanes_of((tiles, LANES)) // levels
    joined = [jnp.zeros((tiles, LANES), jnp.float32) for _ in range(parts * lat_rows)]
    for r in range(TILE):
        line = turned[pl.ds(r, tiles, stride=TILE), :]
        joined = [jnp.where(group == r, spin(line, (r - i) * levels, 1), x) for i, x in enumerate(joined)]
    block = tiles + 2 * TILE
    for i, x in enumerate(joined):
        lined[i * block : i * block + TILE, :] = x[tiles - TILE :, :]
        lined[i * block + TILE : i * block + TILE + tiles, :] = x
        lined[i * block + TILE + tiles : (i + 1) * block, :] = x[:TILE, :]
    lane = lanes_of()
    span = (lane >= 3 * levels) & (lane < 4 * levels)
    index = rows_of()
    for row in range(lat_rows):
        floor = jnp.broadcast_to(own_ref[2 * half + row : 2 * half + row + 1, :], (TILE, total_lon))
        lines = {1: [], 2: []}
        for start in range(0, count, TILE):
            near_ones = jnp.zeros((TILE, LANES), jnp.float32)
            far_ones = near_ones
            for i in range(TILE):
                first = (start + i) * columns
                inner = spin(floor, 3 * levels - first, 1)[:, :LANES]
                outer = spin(floor, 2 * levels - first, 1)[:, :LANES]
                wrap = spin(floor, 4 * levels - first, 1)[:, :LANES]
                near_ones = jnp.where(index == i, inner, near_ones)
                far_ones = jnp.where(index == i, jnp.where(lane < 4 * levels - HALO, outer, wrap), far_ones)
            lines[1].append(near_ones)
            lines[2].append(far_ones)
        for part in range(parts):
            base = (part * lat_rows + row) * block + TILE
            for q in range(own):
                out_ref[pl.ds(part * TILE + q * 2 + row, count, stride=parts * TILE), :] = lined[
                    pl.ds(base + q, count, stride=own), :
                ]
            lane_all = lanes_of((count, LANES))
            edge = jnp.where(
                lane_all < HALO * levels,
                lined[pl.ds(base + own, count, stride=own), :],
                lined[pl.ds(base - 1, count, stride=own), :],
            )
            if part > 0:
                edge = jnp.concatenate(
                    [jnp.where(span, lines[part][i], edge[TILE * i : TILE * (i + 1), :]) for i in range(count // TILE)], axis=0
                )
            out_ref[pl.ds(part * TILE + own * 2 + row, count, stride=parts * TILE), :] = edge


def pack_edges(low_ref, high_ref, sea_ref, biome_ref, first_ref, second_ref, even):
    species, levels, _, total_lat = low_ref.shape
    columns = sea_ref.shape[1]
    blocks = LANES // total_lat
    groups = levels // blocks
    low = rows_of((TILE, total_lat)) < HALO
    last = columns - TILE

    def put(start, both):
        flipped = spin(both, HALO, 0)
        here = jnp.where(even, flipped, both)
        first_ref[start : start + HALO, :] = here[:HALO, :]
        second_ref[start : start + HALO, :] = here[HALO:, :]

    for group in range(groups):
        wet = [
            jnp.where(low, sea_ref[group * blocks + b, 0:TILE, :], sea_ref[group * blocks + b, last:columns, :]).astype(
                jnp.float32
            )
            for b in range(blocks)
        ]
        joined = jnp.concatenate(wet, axis=1)
        put(species * groups * HALO + group * HALO, joined)
        for kind in range(species):
            parts = [
                jnp.where(low, low_ref[kind, group * blocks + b], high_ref[kind, group * blocks + b])
                for b in range(blocks)
            ]
            put((kind * groups + group) * HALO, jnp.concatenate(parts, axis=1) * joined)
    biome = jnp.where(low, biome_ref[0:TILE, :], biome_ref[last:columns, :]).astype(jnp.float32)
    start = (species + 1) * groups * HALO
    put(start, jnp.concatenate([biome] * blocks, axis=1))
    first_ref[start + HALO : start + 2 * HALO, :] = jnp.zeros((HALO, LANES), jnp.float32)
    second_ref[start + HALO : start + 2 * HALO, :] = jnp.zeros((HALO, LANES), jnp.float32)


def fetch(sources, targets, ready):
    copies = [pltpu.make_async_copy(a, b, ready.at[i]) for i, (a, b) in enumerate(zip(sources, targets, strict=True))]
    for copy in copies:
        copy.start()
    return copies


def is_even():
    return lax.axis_index("lat") % 2 == 0


def pack(ocean, bottom, tracers, sea, biome, *refs):
    out, edges, home_out, (turned, lined), held = refs[0], refs[1:3], refs[3], refs[4:6], refs[6:12]
    result, home, ready, gone = refs[12:16]
    columns = tracers.shape[2]
    sources = [ocean, bottom, tracers.at[:, :, 0:TILE, :], tracers.at[:, :, columns - TILE : columns, :], sea, biome]
    copies = fetch(sources, held, ready)
    copies[0].wait()
    copies[1].wait()
    pack_ocean(held[0], held[1], home, result, turned, lined)
    leaving = fetch([result, home], [out, home_out], gone)
    for copy in copies[2:]:
        copy.wait()
    pack_edges(*held[2:], *edges, is_even())
    for copy in leaving:
        copy.wait()


def light(plankton, surface):
    result = []
    depth = jnp.zeros(surface.shape, jnp.float32)
    for value in plankton:
        chloro = jnp.maximum(value, 0.0) + jnp.log(1.0 + jnp.exp(-jnp.abs(value)))
        attenuate = water_atten + chl_atten * chloro
        result.append((chloro, surface * jnp.exp(-depth), attenuate))
        depth = depth + attenuate
    return result


def surface_light(total_lat):
    row_index = (lanes_of() % total_lat).astype(jnp.float32)
    place = 2.0 * (row_index + 0.5) / total_lat - 1.0
    return 1.0 - 0.5 * place * place


def planes_of(ref, kind, levels, species, base=0):
    return [ref[pl.ds(base + level * TILE * species + kind, TILE, stride=species), :] for level in range(levels)]


def put_growth(growth_ref, tracer_ref, levels, species, total_lat, base=0):
    lit = light(planes_of(tracer_ref, 0, levels, species, base), surface_light(total_lat))
    food = planes_of(tracer_ref, 1, levels, species, base)
    for level, (chloro, top_light, _) in enumerate(lit):
        nutrient = food[level] * food[level]
        uptake = growth_rate * top_light * chloro * nutrient / (1.0 + nutrient)
        growth_ref[level * TILE : (level + 1) * TILE, :] = tracer_step * uptake
    return lit


def rate_pieces(rate_table_ref):
    kinds, species, _ = rate_table_ref.shape
    rates = tracer_step * rate_table_ref[...].reshape(kinds * species, species)
    high = rates.astype(jnp.bfloat16)
    low = (rates - high.astype(jnp.float32)).astype(jnp.bfloat16)
    return jnp.concatenate([high, low, high], axis=1)


def reaction(source_ref, base, pieces, chosen, growth_ref, row, levels, species):
    index = rows_of()
    sign = jnp.where(index == 0, 1.0, jnp.where(index == 1, -1.0, 0.0))
    sums = []
    for pair in range(0, len(levels), 2):
        near = levels[pair : pair + 2]
        values = jnp.concatenate(
            [source_ref[pl.ds(base + (level * TILE + row) * species, species), :] for level in near], axis=1
        )
        high = values.astype(jnp.bfloat16)
        low = (values - high.astype(jnp.float32)).astype(jnp.bfloat16)
        every = jnp.dot(
            pieces, jnp.concatenate([high, high, low], axis=0), preferred_element_type=jnp.float32
        )
        for place, level in enumerate(near):
            mine = every[:, place * LANES : (place + 1) * LANES]
            total = mine[:species, :]
            for kind, mask in enumerate(chosen):
                total = jnp.where(mask, mine[(kind + 1) * species : (kind + 2) * species, :], total)
            uptake = sign * growth_ref[pl.ds(level * TILE + row, TILE, stride=0), :]
            sums.append(jnp.concatenate([total[:TILE, :] + uptake, total[TILE:, :]], axis=0))
    return sums


def biome_masks(biome_ref, row, kinds, species):
    here = jnp.broadcast_to(biome_ref[row : row + 1, :], (species, LANES))
    return [here == float(kind) for kind in range(1, kinds)]


def prepare_own(tracers, sea, biome, rate_table, own_ref, wet_ref, biomes_ref, pieces_ref, *refs):
    held, ready = refs[:4], refs[4]
    tracer_ref, sea_ref, biome_ref, rate_table_ref = held
    species, levels, columns, total_lat = tracers.shape
    own = columns // TILE
    copies = fetch([tracers, sea, biome, rate_table], held, ready)
    blank = jnp.zeros((TILE, total_lat), jnp.float32)
    for copy in copies[1:]:
        copy.wait()

    def plane(parts):
        return jnp.concatenate(parts + [blank], axis=1)

    pieces_ref[...] = rate_pieces(rate_table_ref)
    biomes_ref[...] = plane([biome_ref[TILE * q : TILE * (q + 1), :].astype(jnp.float32) for q in range(own)])
    for level in range(levels):
        parts = [sea_ref[level, TILE * q : TILE * (q + 1), :].astype(jnp.float32) for q in range(own)]
        wet_ref[level * TILE : (level + 1) * TILE, :] = plane(parts)
    copies[0].wait()
    for level in range(levels):
        wet = wet_ref[level * TILE : (level + 1) * TILE, :]
        for kind in range(species):
            parts = [tracer_ref[kind, level, TILE * q : TILE * (q + 1), :] for q in range(own)]
            own_ref[pl.ds(level * TILE * species + kind, TILE, stride=species), :] = plane(parts) * wet


def prepare_all(
    own_ref, own_wet_ref, own_biomes_ref, pieces_ref, from_first, from_second, now_ref, wet_ref, biomes_ref, first_ref, growth, sizes
):
    levels, species, total_lat, columns, kinds = sizes
    blocks = LANES // total_lat
    groups = levels // blocks
    inner = lanes_of() < columns // TILE * total_lat
    even = is_even()

    def halo(start):
        both = jnp.concatenate([from_first[start : start + HALO, :], from_second[start : start + HALO, :]], axis=0)
        return jnp.where(even, both, spin(both, HALO, 0))

    def joined(inside, edge, block):
        return jnp.where(inner, inside, spin(edge, LANES - (block + 1) * total_lat, 1))

    for group in range(groups):
        edge = halo((species * groups + group) * HALO)
        for block in range(blocks):
            place = slice((group * blocks + block) * TILE, (group * blocks + block + 1) * TILE)
            wet_ref[place, :] = joined(own_wet_ref[place, :], edge, block)
    biomes_ref[...] = joined(own_biomes_ref[...], halo((species + 1) * groups * HALO), 0)
    for kind in range(species):
        for group in range(groups):
            edge = halo((kind * groups + group) * HALO)
            for block in range(blocks):
                place = pl.ds((group * blocks + block) * TILE * species + kind, TILE, stride=species)
                now_ref[place, :] = joined(own_ref[place, :], edge, block)
    put_growth(growth, now_ref, levels, species, total_lat)
    pieces = pieces_ref[...]
    for row in range(TILE):
        chosen = biome_masks(biomes_ref, row, kinds, species)
        every = list(range(levels))
        for level, change in zip(every, reaction(now_ref, 0, pieces, chosen, growth, row, every, species), strict=True):
            mask = wet_ref[pl.ds(level * TILE + row, species, stride=0), :]
            first_ref[pl.ds((level * TILE + row) * species, species), :] = mask * change


def advance(
    received, now_ref, wet_ref, biomes_ref, pieces_ref, first_ref, sent_out, last_ref, sent, work, ocean, coef, tracer, growth,
    heat, done, sizes,
):
    levels, species, total_lat, columns, kinds = sizes
    pieces = pieces_ref[...]
    count = total_lat // 2
    own = columns // TILE
    row, lane = rows_of(), lanes_of()
    lat = lane % total_lat

    turned = []
    for part in range(3):
        for q in range(own + 1):
            for j in range(2):
                work[pl.ds(part * LANES + q * total_lat + j, count, stride=2), :] = received[
                    pl.ds(part * TILE + q * 2 + j, count, stride=3 * TILE), :
                ]
        turned.append(work[part * LANES : (part + 1) * LANES, :].T)
        for r in range(TILE):
            ocean[pl.ds(part * levels * TILE + r, levels, stride=TILE), :] = turned[part][r * levels : (r + 1) * levels, :]
    spare = 3 * levels
    floors = [turned[1 + q // 2][spare + q % 2 * TILE : spare + (q % 2 + 1) * TILE, :] for q in range(own + 1)]
    floor = floors[own]
    for q in range(own):
        floor = jnp.where(lane // total_lat == q, spin(floors[q], (q - own) * total_lat, 1), floor)
    wet = [(float(level) < floor).astype(jnp.float32) for level in range(levels)]
    sea = [wet_ref[level * TILE : (level + 1) * TILE, :] for level in range(levels)]

    def read(field):
        return [ocean[(field * levels + k) * TILE : (field * levels + k + 1) * TILE, :] for k in range(levels)]

    def write(field, values):
        for k in range(levels):
            ocean[(field * levels + k) * TILE : (field * levels + k + 1) * TILE, :] = values[k]

    def east(x):
        y = spin(x, -1, 0)
        return jnp.where(row == TILE - 1, spin(y, -total_lat, 1), y)

    def west(x):
        y = spin(x, 1, 0)
        return jnp.where(row == 0, spin(y, total_lat, 1), y)

    def north(x):
        return jnp.where(lat == total_lat - 1, 0.0, spin(x, -1, 1))

    def south(x):
        return jnp.where(lat == 0, 0.0, spin(x, 1, 1))

    spin_rate = coriolis * (2.0 * (lat.astype(jnp.float32) + 0.5) / total_lat - 1.0)
    plane = levels * TILE

    def dynamics(step):
        speed_u, speed_v, steps = read(0), read(1), read(2)
        spread, new_u, new_v = [], [], []
        pressure = None
        for k in range(levels):
            u, v = speed_u[k], speed_v[k]
            u_east, u_west, v_north, v_south = east(u), west(u), north(v), south(v)
            if step < STEPS - 1:
                pressure = steps[k] if pressure is None else pressure + steps[k]
                slope_east = 0.5 * (east(pressure) - west(pressure))
                slope_north = 0.5 * (north(pressure) - south(pressure))
                lap_u = u_east + u_west + north(u) + south(u) - 4.0 * u
                lap_v = east(v) + west(v) + v_north + v_south - 4.0 * v
                new_u.append(wet[k] * (u + time_step * (spin_rate * v - slope_east + viscosity * lap_u)))
                new_v.append(wet[k] * (v + time_step * (-spin_rate * u - slope_north + viscosity * lap_v)))
            spread.append(0.5 * (u_east - u_west) + 0.5 * (v_north - v_south))
            face_east = 0.5 * (u + u_east)
            face_west = west(face_east)
            face_north = jnp.where(lat == total_lat - 1, 0.0, 0.5 * (v + v_north))
            face_south = spin(face_north, 1, 1)
            up_east, down_east = jnp.maximum(face_east, 0.0), jnp.minimum(face_east, 0.0)
            up_west, down_west = jnp.maximum(face_west, 0.0), jnp.minimum(face_west, 0.0)
            up_north, down_north = jnp.maximum(face_north, 0.0), jnp.minimum(face_north, 0.0)
            up_south, down_south = jnp.maximum(face_south, 0.0), jnp.minimum(face_south, 0.0)
            mask = tracer_step * sea[k]
            at = step * 7 * plane + k * TILE
            coef[pl.ds(at + plane, TILE), :] = mask * (tracer_diff - down_east)
            coef[pl.ds(at + 2 * plane, TILE), :] = mask * (tracer_diff + up_west)
            coef[pl.ds(at + 3 * plane, TILE), :] = jnp.where(
                lat == total_lat - 1, 0.0, mask * (tracer_diff - down_north)
            )
            coef[pl.ds(at + 4 * plane, TILE), :] = jnp.where(lat == 0, 0.0, mask * (tracer_diff + up_south))
            coef[pl.ds(at, TILE), :] = -4.0 * tracer_diff - up_east + down_west - up_north + down_south
        total = jnp.zeros((TILE, LANES), jnp.float32)
        below_up, below_down = total, total
        for k in reversed(range(levels)):
            total = total + spread[k]
            rise = -vert_ratio * total if k > 0 else jnp.zeros((TILE, LANES), jnp.float32)
            up, down = jnp.maximum(rise, 0.0), jnp.minimum(rise, 0.0)
            mask = tracer_step * sea[k]
            at = step * 7 * plane + k * TILE
            coef[pl.ds(at, TILE), :] = sea[k] + mask * (coef[pl.ds(at, TILE), :] - up + below_down)
            coef[pl.ds(at + 5 * plane, TILE), :] = -mask * down
            coef[pl.ds(at + 6 * plane, TILE), :] = mask * below_up
            below_up, below_down = up, down
        if step < STEPS - 1:
            write(0, new_u)
            write(1, new_v)

    def substep(step, source, base, target, target_base, ready):
        start = step * 7 * plane

        def body(group, carry):
            near = [group * 4 + i for i in range(4)]
            for r in range(TILE):
                if ready is None:
                    chosen = biome_masks(biomes_ref, r, kinds, species)
                    sums = reaction(source, base, pieces, chosen, growth, r, near, species)
                for place, level in enumerate(near):
                    cell = level * TILE + r
                    above = max(level - 1, 0) * TILE + r
                    under = min(level + 1, levels - 1) * TILE + r
                    weight = [coef[pl.ds(start + i * plane + cell, species, stride=0), :] for i in range(7)]
                    mask = None if ready is not None else wet_ref[pl.ds(cell, species, stride=0), :]

                    def take(index):
                        return source[pl.ds(base + index * species, species), :]

                    x = take(cell)
                    x_east = take(cell + 1) if r < TILE - 1 else spin(take(cell - r), -total_lat, 1)
                    x_west = take(cell - 1) if r > 0 else spin(take(cell + TILE - 1), total_lat, 1)
                    change = mask * sums[place] if ready is None else ready[pl.ds(cell * species, species), :]
                    value = (
                        (weight[0] * x + weight[1] * x_east)
                        + (weight[2] * x_west + weight[3] * spin(x, -1, 1))
                        + (weight[4] * spin(x, 1, 1) + weight[5] * take(above))
                        + (weight[6] * take(under) + change)
                    )
                    target[pl.ds(target_base + cell * species, species), :] = value
            return carry

        for group in range(levels // 4):
            body(group, 0)

    for field in range(3):
        write(field, [wet[k] * x for k, x in enumerate(read(field))])
    size = levels * TILE * species
    source, base = now_ref, 0
    lit = None
    for step in range(STEPS):
        dynamics(step)
        for sub in range(SUB):
            last = step == STEPS - 1 and sub == SUB - 1
            first = step == 0 and sub == 0
            target, target_base = (last_ref, 0) if last else (tracer, ((step * SUB + sub) % 2) * size)
            if not first:
                put_growth(growth, source, levels, species, total_lat, base)
            substep(step, source, base, target, target_base, first_ref if first else None)
            source, base = target, target_base
        lit = light(planes_of(source, 0, levels, species, base), surface_light(total_lat))
        for k in range(levels):
            _, top_light, attenuate = lit[k]
            heating = heat_gain * sea[k] * (top_light * (1.0 - jnp.exp(-attenuate)))
            for place, shift in enumerate(range(-1, 3) if step < STEPS - 1 else range(2)):
                at = ((place + 4 * step) * levels + k) * TILE
                heat[at : at + TILE, :] = spin(heating, -shift, 1)

    kinds_of_row = 6 * levels
    blank = jnp.zeros((LANES - kinds_of_row, LANES), jnp.float32)
    for r in range(TILE):
        work[r * LANES : (r + 1) * LANES, :] = jnp.concatenate(
            [heat[pl.ds(r, kinds_of_row, stride=TILE), :], blank], axis=0
        ).T
        for q in range(own):
            sent[pl.ds(q * TILE + r, count, stride=own * TILE), :] = work[
                pl.ds(r * LANES + q * total_lat, count, stride=2), :
            ]
    send = pltpu.make_async_copy(sent, sent_out, done)
    send.start()
    send.wait()


def unpack_tracers(last_ref, out_ref):
    species, levels, columns, total_lat = out_ref.shape
    for level in range(levels):
        for kind in range(species):
            whole = last_ref[pl.ds(level * TILE * species + kind, TILE, stride=species), :]
            for q in range(columns // TILE):
                out_ref[kind, level, TILE * q : TILE * (q + 1), :] = whole[:, q * total_lat : (q + 1) * total_lat]


def down_sum(x):
    index = rows_of(x.shape)
    step = 1
    while step < x.shape[0]:
        x = x + jnp.where(index >= step, spin(x, step, 0), 0.0)
        step *= 2
    return x


def slope(x):
    return 0.5 * (spin(x, -1, 1) - spin(x, 1, 1))


def lap(before, x, after):
    return spin(x, -1, 1) + spin(x, 1, 1) + after + before - 4.0 * x


def at_home(own_ref, first_ref, second_ref, base_ref, wet_ref, levels, total_lat):
    half = FIELDS * levels
    rows = range(-2, 4)
    start = lax.axis_index("lat") * 2
    even = is_even()

    def raw(at, size, offset):
        place = slice(at % 2 * offset[0] + offset[1], at % 2 * offset[0] + offset[1] + size)
        if 0 <= at < 2:
            return own_ref[place, :]
        return jnp.where(even == (at > 0), first_ref[place, :], second_ref[place, :])

    wet, u, v, t, s = {}, {}, {}, {}, {}
    for j in rows:
        floor = raw(j, 1, (1, 2 * half))
        level = rows_of((levels, floor.shape[1])).astype(jnp.float32)
        wet[j] = (level < floor).astype(jnp.float32)
        u[j], v[j], t[j], s[j] = [wet[j] * raw(j, levels, (half, field * levels)) for field in range(FIELDS)]

    def step(u, v, t, s, inner):
        pressure = {j: gravity * down_sum(haline_coef * s[j] - therm_coef * t[j]) for j in u}
        fresh = ({}, {}, {}, {})
        for j in inner:
            turn = coriolis * (2.0 * ((start + j).astype(jnp.float32) + 0.5) / total_lat - 1.0)
            north_slope = 0.5 * (pressure[j + 1] - pressure[j - 1])
            laps = [lap(x[j - 1], x[j], x[j + 1]) for x in (u, v, t, s)]
            fresh[0][j] = wet[j] * (u[j] + time_step * (turn * v[j] - slope(pressure[j]) + viscosity * laps[0]))
            fresh[1][j] = wet[j] * (v[j] + time_step * (-turn * u[j] - north_slope + viscosity * laps[1]))
            fresh[2][j] = wet[j] * (t[j] + time_step * heat_diff * laps[2])
            fresh[3][j] = wet[j] * (s[j] + time_step * salt_diff * laps[3])
        return fresh

    final = step(*step(u, v, t, s, range(-1, 3)), range(2))
    for j in range(2):
        for field in range(FIELDS):
            begin = j * half + field * levels
            base_ref[begin : begin + levels, :] = final[field][j]
    for j in range(-1, 3):
        wet_ref[(j + 1) * levels : (j + 2) * levels, :] = wet[j]


def finish(received, base_ref, wet_ref, out_ref, flat):
    fields, levels, _, _ = out_ref.shape
    half = fields * levels
    heating = received[...].T

    def part(ref, place):
        return ref[place * levels : (place + 1) * levels, :]

    wet = {j: part(wet_ref, j + 1) for j in range(-1, 3)}
    warm = {j: time_step * (wet[j] * part(heating, j + 1)) for j in wet}
    push = {j: (gravity * therm_coef) * down_sum(warm[j]) for j in wet}
    for j in range(2):
        u, v, t, s = [part(base_ref, j * fields + field) for field in range(fields)]
        late = wet[j] * part(heating, 4 + j)
        spread = lap(warm[j - 1], warm[j], warm[j + 1])
        results = (
            u + wet[j] * (time_step * slope(push[j])),
            v + wet[j] * (time_step * (0.5 * (push[j + 1] - push[j - 1]))),
            t + wet[j] * (warm[j] + time_step * heat_diff * spread) + time_step * late,
            s,
        )
        for field, value in enumerate(results):
            begin = j * half + field * levels
            flat[begin : begin + levels, :] = value
    for index in range(half):
        field, level = divmod(index, levels)
        for row in range(2):
            out_ref[field, level, row : row + 1, :] = flat[row * half + index : row * half + index + 1, :]


def grids(*shapes):
    return [pltpu.VMEM(shape, jnp.float32) for shape in shapes]


def far(*shape):
    return pltpu.HBM(shape, jnp.float32)


def near(*shape, dtype=jnp.float32):
    return pltpu.VMEM(shape, dtype)


def placed(space, *arrays):
    return [pltpu.with_memory_space_constraint(x, space) for x in arrays]


def shards(ocean_state, bottom, tracers, land_sea, biome_id, rate_table):
    count = lax.axis_size("lat")
    if not fits(ocean_state, tracers, count):
        return general_shards(ocean_state, bottom, tracers, land_sea, biome_id, rate_table)
    _, levels, _, total_lon = ocean_state.shape
    species, _, columns, total_lat = tracers.shape
    cells = levels * TILE
    size = cells * species
    own = columns // TILE

    edge_rows = (species + 1) * (levels * total_lat // LANES) * HALO + 2 * HALO
    packed_rows = count * 3 * TILE
    home_shape = (LANES + TILE, total_lon)
    kinds = rate_table.shape[0]
    roomy = pltpu.CompilerParams(vmem_limit_bytes=GRANT)
    ocean_state, bottom, tracers, land_sea, biome_id, rate_table = placed(
        pltpu.HBM, ocean_state, bottom, tracers, land_sea, biome_id, rate_table
    )
    vmem = pl.BlockSpec(memory_space=pltpu.VMEM)
    hbm = pl.BlockSpec(memory_space=pltpu.HBM)

    pairs = [(i, i ^ 1) for i in range(count)]
    others = [((a + 1) % count, (b + 1) % count) for a, b in pairs]
    sizes = (levels, species, total_lat, columns, kinds)
    edge_shape = (species, levels, TILE, total_lat)

    packed, to_first, to_second, home = pl.pallas_call(
        pack,
        out_shape=[far(packed_rows, LANES), near(edge_rows, LANES), near(edge_rows, LANES), far(*home_shape)],
        in_specs=[hbm] * 5,
        out_specs=[hbm, vmem, vmem, hbm],
        scratch_shapes=grids((total_lon, LANES), (6 * (total_lon // TILE + 2 * TILE), LANES), ocean_state.shape)
        + [pltpu.VMEM(bottom.shape, bottom.dtype)]
        + grids(edge_shape, edge_shape)
        + [pltpu.VMEM(x.shape, x.dtype) for x in (land_sea, biome_id)]
        + grids((packed_rows, LANES), home_shape)
        + [pltpu.SemaphoreType.DMA((6,)), pltpu.SemaphoreType.DMA((2,))],
        compiler_params=roomy,
        name="pack",
    )(ocean_state, bottom, tracers, land_sea, biome_id)
    received = lax.all_to_all(
        packed.reshape(count, packed_rows // count, LANES), "lat", split_axis=0, concat_axis=0, tiled=True
    ).reshape(packed.shape)
    from_first = lax.ppermute(to_first, "lat", pairs)
    from_second = lax.ppermute(to_second, "lat", others)
    first_rows = lax.ppermute(home, "lat", pairs)
    inner = [(a, b) for a, b in others if abs(a - b) == 1]
    second_rows = lax.ppermute(home, "lat", inner)
    from_first, from_second, received = placed(pltpu.VMEM, from_first, from_second, received)

    inside = pl.pallas_call(
        prepare_own,
        out_shape=[
            near(size, LANES),
            near(cells, LANES),
            near(TILE, LANES),
            near(kinds * species, 3 * species, dtype=jnp.bfloat16),
        ],
        in_specs=[hbm] * 4,
        out_specs=[vmem] * 4,
        scratch_shapes=[pltpu.VMEM(x.shape, x.dtype) for x in (tracers, land_sea, biome_id, rate_table)]
        + [pltpu.SemaphoreType.DMA((4,))],
        compiler_params=roomy,
        name="prepare_own",
    )(tracers, land_sea, biome_id, rate_table)
    pieces = inside[3]

    def prepare(*refs):
        prepare_all(*refs, sizes)

    now, wet, biomes, first = pl.pallas_call(
        prepare,
        out_shape=[near(size, LANES), near(cells, LANES), near(TILE, LANES), near(size, LANES)],
        in_specs=[vmem] * 6,
        out_specs=[vmem] * 4,
        scratch_shapes=grids((cells, LANES)),
        compiler_params=roomy,
        name="prepare",
    )(*inside, from_first, from_second)

    def run(*refs):
        advance(*refs, sizes)

    sent, last = pl.pallas_call(
        run,
        out_shape=[far(count * own * TILE, LANES), near(size, LANES)],
        in_specs=[vmem] * 6,
        out_specs=[hbm, vmem],
        scratch_shapes=grids(
            (count * own * TILE, LANES),
            (TILE * LANES, LANES),
            (3 * cells, LANES),
            (STEPS * 7 * cells, LANES),
            (2 * size, LANES),
            (cells, LANES),
            (6 * cells, LANES),
        )
        + [pltpu.SemaphoreType.DMA],
        compiler_params=pltpu.CompilerParams(vmem_limit_bytes=GRANT),
        name="advance",
    )(received, now, wet, biomes, pieces, first)
    back = lax.all_to_all(
        sent.reshape(count, own * TILE, LANES), "lat", split_axis=0, concat_axis=0, tiled=True
    ).reshape(sent.shape)

    def stay(*refs):
        at_home(*refs, levels, total_lat)

    base, masks = pl.pallas_call(
        stay,
        out_shape=[near(LANES, total_lon), near(4 * levels, total_lon)],
        in_specs=[vmem] * 3,
        out_specs=[vmem] * 2,
        compiler_params=roomy,
        name="at_home",
    )(*placed(pltpu.HBM, home, first_rows, second_rows))
    (back,) = placed(pltpu.VMEM, back)
    (last,) = placed(pltpu.VMEM, last)
    tracers_out = pl.pallas_call(
        unpack_tracers,
        out_shape=far(*tracers.shape),
        in_specs=[vmem],
        out_specs=vmem,
        compiler_params=roomy,
        name="unpack_tracers",
    )(last)
    state_out = pl.pallas_call(
        finish,
        out_shape=far(*ocean_state.shape),
        in_specs=[vmem] * 3,
        out_specs=vmem,
        scratch_shapes=grids((LANES, total_lon)),
        compiler_params=roomy,
        name="finish",
    )(back, base, masks)
    return (state_out, tracers_out)


def solution(mesh):
    in_specs = (
        P(None, None, ("groups", "lat"), None),
        P(("groups", "lat"), None),
        P(None, None, ("groups", "lat"), None),
        P(None, ("groups", "lat"), None),
        P(("groups", "lat"), None),
        P(),
    )
    out_specs = (P(None, None, ("groups", "lat"), None), P(None, None, ("groups", "lat"), None))
    return jax.shard_map(shards, mesh=mesh, in_specs=in_specs, out_specs=out_specs, check_vma=False)
```

```python
import jax
import jax.numpy as jnp
from jax import lax
from jax.experimental import pallas as pl
from jax.experimental.pallas import tpu as pltpu
from jax.sharding import PartitionSpec as P


STEPS = 2
SUB = 2


time_step = 0.1
viscosity = 0.1
heat_diff = 0.08
salt_diff = 0.06
therm_coef = 0.2
haline_coef = 0.15
gravity = 0.5
coriolis = 0.6
vert_ratio = 0.25
tracer_step = 0.1
tracer_diff = 0.1
water_atten = 0.04
chl_atten = 0.05
growth_rate = 0.8
heat_gain = 10.0


def extended(block, sides, width, periodic):
    for axis, dim in sides:
        count = lax.axis_size(axis)
        forward = [(i, i + 1) for i in range(count - 1)]
        if periodic:
            forward.append((count - 1, 0))
        backward = [(target, source) for source, target in forward]
        low = lax.ppermute(
            lax.slice_in_dim(block, block.shape[dim] - width, None, axis=dim), axis, forward
        )
        high = lax.ppermute(lax.slice_in_dim(block, 0, width, axis=dim), axis, backward)
        block = jnp.concatenate([low, block, high], axis=dim)
    return block


def laplace_rows(field):
    center = field[:, 1:-1, :]
    return (
        jnp.roll(center, 1, 2)
        + jnp.roll(center, -1, 2)
        + field[:, 2:, :]
        + field[:, :-2, :]
        - 4.0 * center
    )


def ocean_core(padded, wet_mask, lat_start, total_lat):
    speed_u, speed_v, temper, salty = (padded[0], padded[1], padded[2], padded[3])
    east_mid = speed_u[:, 1:-1, :]
    north_mid = speed_v[:, 1:-1, :]
    temp_mid = temper[:, 1:-1, :]
    salt_mid = salty[:, 1:-1, :]
    pressure = gravity * jnp.cumsum(haline_coef * salty - therm_coef * temper, axis=0)
    press_mid = pressure[:, 1:-1, :]
    row_index = (lat_start + jnp.arange(wet_mask.shape[1], dtype=jnp.int32)).astype(jnp.float32)
    spin_rate = (coriolis * (2.0 * (row_index + 0.5) / total_lat - 1.0))[None, :, None]
    slope_east = 0.5 * (jnp.roll(press_mid, -1, 2) - jnp.roll(press_mid, 1, 2))
    slope_north = 0.5 * (pressure[:, 2:, :] - pressure[:, :-2, :])
    new_u = wet_mask * (
        east_mid
        + time_step * (spin_rate * north_mid - slope_east + viscosity * laplace_rows(speed_u))
    )
    new_v = wet_mask * (
        north_mid
        + time_step * (-spin_rate * east_mid - slope_north + viscosity * laplace_rows(speed_v))
    )
    new_s = wet_mask * (salt_mid + time_step * salt_diff * laplace_rows(salty))
    part_t = temp_mid + time_step * heat_diff * laplace_rows(temper)
    spread = 0.5 * (jnp.roll(east_mid, -1, 2) - jnp.roll(east_mid, 1, 2)) + 0.5 * (
        speed_v[:, 2:, :] - speed_v[:, :-2, :]
    )
    rise_flux = -vert_ratio * jnp.flip(jnp.cumsum(jnp.flip(spread, 0), axis=0), 0)
    fluxes = jnp.stack([east_mid, north_mid, rise_flux])
    return (new_u, new_v, part_t, new_s, fluxes)


def light_field(plankton):
    chloro = jax.nn.softplus(plankton)
    attenuate = water_atten + chl_atten * chloro
    depth = jnp.cumsum(attenuate, axis=0) - attenuate
    row_index = jnp.arange(plankton.shape[-1], dtype=jnp.int32).astype(jnp.float32)
    place = 2.0 * (row_index + 0.5) / plankton.shape[-1] - 1.0
    surface = 1.0 - 0.5 * place * place
    top_light = surface * jnp.exp(-depth)
    return (chloro, top_light, top_light * (1.0 - jnp.exp(-attenuate)))


def tracer_core(tracer_ext, flux_ext, sea_mask, onehot, rate_table):
    center = tracer_ext[:, :, 1:-1, :]
    east_face = 0.5 * (flux_ext[0, :, :-1, :] + flux_ext[0, :, 1:, :])
    across = (
        jnp.maximum(east_face, 0.0) * tracer_ext[:, :, :-1, :]
        + jnp.minimum(east_face, 0.0) * tracer_ext[:, :, 1:, :]
    )
    div_east = across[:, :, 1:, :] - across[:, :, :-1, :]
    north_speed = flux_ext[1, :, 1:-1, :]
    north_face = 0.5 * (north_speed[:, :, :-1] + north_speed[:, :, 1:])
    along = (
        jnp.maximum(north_face, 0.0) * center[..., :-1]
        + jnp.minimum(north_face, 0.0) * center[..., 1:]
    )
    along = jnp.pad(along, ((0, 0), (0, 0), (0, 0), (1, 1)))
    div_north = along[..., 1:] - along[..., :-1]
    rise_face = flux_ext[2, 1:, 1:-1, :]
    upward = (
        jnp.maximum(rise_face, 0.0) * center[:, 1:] + jnp.minimum(rise_face, 0.0) * center[:, :-1]
    )
    upward = jnp.pad(upward, ((0, 0), (1, 1), (0, 0), (0, 0)))
    div_up = upward[:, :-1] - upward[:, 1:]
    side = jnp.pad(center, ((0, 0), (0, 0), (0, 0), (1, 1)))
    diffuse = (
        tracer_ext[:, :, 2:, :]
        + tracer_ext[:, :, :-2, :]
        + side[..., 2:]
        + side[..., :-2]
        - 4.0 * center
    )
    chloro, top_light, _ = light_field(center[0])
    nutrient = center[1] * center[1]
    uptake = growth_rate * top_light * chloro * nutrient / (1.0 + nutrient)
    rate_cell = jnp.einsum("bst,bij->stij", rate_table, onehot, precision=lax.Precision.HIGHEST)
    reaction = jnp.einsum("stij,tkij->skij", rate_cell, center, precision=lax.Precision.HIGHEST)
    reaction = reaction.at[0].add(uptake).at[1].add(-uptake)
    tendency = tracer_diff * diffuse + reaction - (div_east + div_north + div_up)
    return sea_mask[None] * (center + tracer_step * tendency)


def general_shards(ocean_state, bottom, tracers, land_sea, biome_id, rate_table):
    levels = ocean_state.shape[1]
    lat_rows = ocean_state.shape[2]
    lat_count = lax.axis_size("lat")
    total_lat = lat_rows * lat_count
    lat_start = lax.axis_index("lat") * lat_rows
    wet_mask = (jnp.arange(levels, dtype=jnp.int32)[:, None, None] < bottom[None]).astype(
        jnp.float32
    )
    sea_mask = land_sea.astype(jnp.float32)
    onehot = (
        biome_id[None] == jnp.arange(rate_table.shape[0], dtype=jnp.int32)[:, None, None]
    ).astype(jnp.float32)
    state = ocean_state
    tracer_now = tracers
    for _ in range(STEPS):
        state = state * wet_mask[None]
        padded = extended(state, (("lat", 2),), 1, False)
        new_u, new_v, part_t, new_s, fluxes = ocean_core(padded, wet_mask, lat_start, total_lat)
        flux_t = lax.all_to_all(
            jnp.transpose(fluxes, (0, 1, 3, 2)), "lat", split_axis=2, concat_axis=3, tiled=True
        )
        tracer_now = tracer_now * sea_mask[None]
        flux_ext = extended(flux_t, (("lat", 2),), 1, True)
        for _ in range(SUB):
            tracer_ext = extended(tracer_now, (("lat", 2),), 1, True)
            tracer_now = tracer_core(tracer_ext, flux_ext, sea_mask, onehot, rate_table)
        heating = heat_gain * sea_mask * light_field(tracer_now[0])[2]
        heat_ocean = jnp.transpose(
            lax.all_to_all(heating, "lat", split_axis=2, concat_axis=1, tiled=True), (0, 2, 1)
        )
        new_t = wet_mask * (part_t + time_step * heat_ocean)
        state = jnp.stack([new_u, new_v, new_t, new_s])
    return (state, tracer_now)


HALO = STEPS * SUB
LANES = 128
TILE = 8
FIELDS = 4
GRANT = 16 * 1024 * 1024


def fits(ocean_state, tracers, lat_count):
    _, levels, lat_rows, total_lon = ocean_state.shape
    species, _, columns, total_lat = tracers.shape
    return (
        lat_rows == 2
        and HALO == TILE // 2
        and lat_rows * lat_count == total_lat
        and columns * lat_count == total_lon
        and columns == 3 * TILE
        and LANES == 4 * total_lat
        and levels == 2 * TILE
        and species == 2 * TILE
        and lat_count % 2 == 0
    )


def rows_of(shape=(TILE, LANES)):
    return lax.broadcasted_iota(jnp.int32, shape, 0)


def lanes_of(shape=(TILE, LANES)):
    return lax.broadcasted_iota(jnp.int32, shape, 1)


def spin(block, amount, axis):
    size = block.shape[axis]
    amount = amount % size
    return block if amount == 0 else pltpu.roll(block, amount, axis)


def pack_ocean(ocean_ref, bottom_ref, own_ref, out_ref, turned, lined):
    fields, levels, lat_rows, total_lon = ocean_ref.shape
    half = fields * levels
    parts = 3
    count = out_ref.shape[0] // (parts * TILE)
    columns = total_lon // count
    own = columns // TILE
    for index in range(half):
        field, level = divmod(index, levels)
        for row in range(lat_rows):
            own_ref[row * half + index : row * half + index + 1, :] = ocean_ref[field, level, row : row + 1, :]
    own_ref[2 * half : 2 * half + TILE, :] = jnp.zeros((TILE, total_lon), jnp.float32)
    for row in range(lat_rows):
        own_ref[2 * half + row : 2 * half + row + 1, :] = bottom_ref[row : row + 1, :].astype(jnp.float32)

    def rows(row, field):
        return own_ref[row * half + field * levels : row * half + (field + 1) * levels, :]

    stack = [rows(row, field) for field in range(2) for row in range(lat_rows)]
    stack += [gravity * (haline_coef * rows(row, 3) - therm_coef * rows(row, 2)) for row in range(lat_rows)]
    stack.append(jnp.zeros((LANES - 2 * parts * levels, total_lon), jnp.float32))
    turned[...] = jnp.concatenate(stack, axis=0).T
    tiles = total_lon // TILE
    group = lanes_of((tiles, LANES)) // levels
    joined = [jnp.zeros((tiles, LANES), jnp.float32) for _ in range(parts * lat_rows)]
    for r in range(TILE):
        line = turned[pl.ds(r, tiles, stride=TILE), :]
        joined = [jnp.where(group == r, spin(line, (r - i) * levels, 1), x) for i, x in enumerate(joined)]
    block = tiles + 2 * TILE
    for i, x in enumerate(joined):
        lined[i * block : i * block + TILE, :] = x[tiles - TILE :, :]
        lined[i * block + TILE : i * block + TILE + tiles, :] = x
        lined[i * block + TILE + tiles : (i + 1) * block, :] = x[:TILE, :]
    lane = lanes_of()
    span = (lane >= 3 * levels) & (lane < 4 * levels)
    index = rows_of()
    for row in range(lat_rows):
        floor = jnp.broadcast_to(own_ref[2 * half + row : 2 * half + row + 1, :], (TILE, total_lon))
        lines = {1: [], 2: []}
        for start in range(0, count, TILE):
            near_ones = jnp.zeros((TILE, LANES), jnp.float32)
            far_ones = near_ones
            for i in range(TILE):
                first = (start + i) * columns
                inner = spin(floor, 3 * levels - first, 1)[:, :LANES]
                outer = spin(floor, 2 * levels - first, 1)[:, :LANES]
                wrap = spin(floor, 4 * levels - first, 1)[:, :LANES]
                near_ones = jnp.where(index == i, inner, near_ones)
                far_ones = jnp.where(index == i, jnp.where(lane < 4 * levels - HALO, outer, wrap), far_ones)
            lines[1].append(near_ones)
            lines[2].append(far_ones)
        for part in range(parts):
            base = (part * lat_rows + row) * block + TILE
            for q in range(own):
                out_ref[pl.ds(part * TILE + q * 2 + row, count, stride=parts * TILE), :] = lined[
                    pl.ds(base + q, count, stride=own), :
                ]
            lane_all = lanes_of((count, LANES))
            edge = jnp.where(
                lane_all < HALO * levels,
                lined[pl.ds(base + own, count, stride=own), :],
                lined[pl.ds(base - 1, count, stride=own), :],
            )
            if part > 0:
                edge = jnp.concatenate(
                    [jnp.where(span, lines[part][i], edge[TILE * i : TILE * (i + 1), :]) for i in range(count // TILE)], axis=0
                )
            out_ref[pl.ds(part * TILE + own * 2 + row, count, stride=parts * TILE), :] = edge


def pack_edges(low_ref, high_ref, sea_ref, biome_ref, first_ref, second_ref, even):
    species, levels, _, total_lat = low_ref.shape
    columns = sea_ref.shape[1]
    blocks = LANES // total_lat
    groups = levels // blocks
    low = rows_of((TILE, total_lat)) < HALO
    last = columns - TILE

    def put(start, both):
        flipped = spin(both, HALO, 0)
        here = jnp.where(even, flipped, both)
        first_ref[start : start + HALO, :] = here[:HALO, :]
        second_ref[start : start + HALO, :] = here[HALO:, :]

    for group in range(groups):
        wet = [
            jnp.where(low, sea_ref[group * blocks + b, 0:TILE, :], sea_ref[group * blocks + b, last:columns, :]).astype(
                jnp.float32
            )
            for b in range(blocks)
        ]
        joined = jnp.concatenate(wet, axis=1)
        put(species * groups * HALO + group * HALO, joined)
        for kind in range(species):
            parts = [
                jnp.where(low, low_ref[kind, group * blocks + b], high_ref[kind, group * blocks + b])
                for b in range(blocks)
            ]
            put((kind * groups + group) * HALO, jnp.concatenate(parts, axis=1) * joined)
    biome = jnp.where(low, biome_ref[0:TILE, :], biome_ref[last:columns, :]).astype(jnp.float32)
    start = (species + 1) * groups * HALO
    put(start, jnp.concatenate([biome] * blocks, axis=1))
    first_ref[start + HALO : start + 2 * HALO, :] = jnp.zeros((HALO, LANES), jnp.float32)
    second_ref[start + HALO : start + 2 * HALO, :] = jnp.zeros((HALO, LANES), jnp.float32)


def fetch(sources, targets, ready):
    copies = [pltpu.make_async_copy(a, b, ready.at[i]) for i, (a, b) in enumerate(zip(sources, targets, strict=True))]
    for copy in copies:
        copy.start()
    return copies


def is_even():
    return lax.axis_index("lat") % 2 == 0


def pack(ocean, bottom, tracers, sea, biome, *refs):
    out, edges, home_out, (turned, lined), held = refs[0], refs[1:3], refs[3], refs[4:6], refs[6:12]
    result, home, ready, gone = refs[12:16]
    columns = tracers.shape[2]
    sources = [ocean, bottom, tracers.at[:, :, 0:TILE, :], tracers.at[:, :, columns - TILE : columns, :], sea, biome]
    copies = fetch(sources, held, ready)
    copies[0].wait()
    copies[1].wait()
    pack_ocean(held[0], held[1], home, result, turned, lined)
    leaving = fetch([result, home], [out, home_out], gone)
    for copy in copies[2:]:
        copy.wait()
    pack_edges(*held[2:], *edges, is_even())
    for copy in leaving:
        copy.wait()


def light(plankton, surface):
    result = []
    depth = jnp.zeros(surface.shape, jnp.float32)
    for value in plankton:
        chloro = jnp.maximum(value, 0.0) + jnp.log(1.0 + jnp.exp(-jnp.abs(value)))
        attenuate = water_atten + chl_atten * chloro
        result.append((chloro, surface * jnp.exp(-depth), attenuate))
        depth = depth + attenuate
    return result


def surface_light(total_lat):
    row_index = (lanes_of() % total_lat).astype(jnp.float32)
    place = 2.0 * (row_index + 0.5) / total_lat - 1.0
    return 1.0 - 0.5 * place * place


def planes_of(ref, kind, levels, species, base=0):
    return [ref[pl.ds(base + level * TILE * species + kind, TILE, stride=species), :] for level in range(levels)]


def put_growth(growth_ref, tracer_ref, levels, species, total_lat, base=0):
    lit = light(planes_of(tracer_ref, 0, levels, species, base), surface_light(total_lat))
    food = planes_of(tracer_ref, 1, levels, species, base)
    for level, (chloro, top_light, _) in enumerate(lit):
        nutrient = food[level] * food[level]
        uptake = growth_rate * top_light * chloro * nutrient / (1.0 + nutrient)
        growth_ref[level * TILE : (level + 1) * TILE, :] = tracer_step * uptake
    return lit


def rate_pieces(rate_table_ref):
    kinds, species, _ = rate_table_ref.shape
    rates = tracer_step * rate_table_ref[...].reshape(kinds * species, species)
    high = rates.astype(jnp.bfloat16)
    low = (rates - high.astype(jnp.float32)).astype(jnp.bfloat16)
    return jnp.concatenate([high, low, high], axis=1)


def reaction(source_ref, base, pieces, chosen, growth_ref, row, levels, species):
    index = rows_of()
    sign = jnp.where(index == 0, 1.0, jnp.where(index == 1, -1.0, 0.0))
    sums = []
    for pair in range(0, len(levels), 2):
        near = levels[pair : pair + 2]
        values = jnp.concatenate(
            [source_ref[pl.ds(base + (level * TILE + row) * species, species), :] for level in near], axis=1
        )
        high = values.astype(jnp.bfloat16)
        low = (values - high.astype(jnp.float32)).astype(jnp.bfloat16)
        every = jnp.dot(
            pieces, jnp.concatenate([high, high, low], axis=0), preferred_element_type=jnp.float32
        )
        for place, level in enumerate(near):
            mine = every[:, place * LANES : (place + 1) * LANES]
            total = mine[:species, :]
            for kind, mask in enumerate(chosen):
                total = jnp.where(mask, mine[(kind + 1) * species : (kind + 2) * species, :], total)
            uptake = sign * growth_ref[pl.ds(level * TILE + row, TILE, stride=0), :]
            sums.append(jnp.concatenate([total[:TILE, :] + uptake, total[TILE:, :]], axis=0))
    return sums


def biome_masks(biome_ref, row, kinds, species):
    here = jnp.broadcast_to(biome_ref[row : row + 1, :], (species, LANES))
    return [here == float(kind) for kind in range(1, kinds)]


def prepare_own(tracers, sea, biome, rate_table, own_ref, wet_ref, biomes_ref, pieces_ref, *refs):
    held, ready = refs[:4], refs[4]
    tracer_ref, sea_ref, biome_ref, rate_table_ref = held
    species, levels, columns, total_lat = tracers.shape
    own = columns // TILE
    copies = fetch([tracers, sea, biome, rate_table], held, ready)
    blank = jnp.zeros((TILE, total_lat), jnp.float32)
    for copy in copies[1:]:
        copy.wait()

    def plane(parts):
        return jnp.concatenate(parts + [blank], axis=1)

    pieces_ref[...] = rate_pieces(rate_table_ref)
    biomes_ref[...] = plane([biome_ref[TILE * q : TILE * (q + 1), :].astype(jnp.float32) for q in range(own)])
    for level in range(levels):
        parts = [sea_ref[level, TILE * q : TILE * (q + 1), :].astype(jnp.float32) for q in range(own)]
        wet_ref[level * TILE : (level + 1) * TILE, :] = plane(parts)
    copies[0].wait()
    for level in range(levels):
        wet = wet_ref[level * TILE : (level + 1) * TILE, :]
        for kind in range(species):
            parts = [tracer_ref[kind, level, TILE * q : TILE * (q + 1), :] for q in range(own)]
            own_ref[pl.ds(level * TILE * species + kind, TILE, stride=species), :] = plane(parts) * wet


def prepare_all(
    own_ref, own_wet_ref, own_biomes_ref, pieces_ref, from_first, from_second, now_ref, wet_ref, biomes_ref, first_ref, growth, sizes
):
    levels, species, total_lat, columns, kinds = sizes
    blocks = LANES // total_lat
    groups = levels // blocks
    inner = lanes_of() < columns // TILE * total_lat
    even = is_even()

    def halo(start):
        both = jnp.concatenate([from_first[start : start + HALO, :], from_second[start : start + HALO, :]], axis=0)
        return jnp.where(even, both, spin(both, HALO, 0))

    def joined(inside, edge, block):
        return jnp.where(inner, inside, spin(edge, LANES - (block + 1) * total_lat, 1))

    for group in range(groups):
        edge = halo((species * groups + group) * HALO)
        for block in range(blocks):
            place = slice((group * blocks + block) * TILE, (group * blocks + block + 1) * TILE)
            wet_ref[place, :] = joined(own_wet_ref[place, :], edge, block)
    biomes_ref[...] = joined(own_biomes_ref[...], halo((species + 1) * groups * HALO), 0)
    for kind in range(species):
        for group in range(groups):
            edge = halo((kind * groups + group) * HALO)
            for block in range(blocks):
                place = pl.ds((group * blocks + block) * TILE * species + kind, TILE, stride=species)
                now_ref[place, :] = joined(own_ref[place, :], edge, block)
    put_growth(growth, now_ref, levels, species, total_lat)
    pieces = pieces_ref[...]
    for row in range(TILE):
        chosen = biome_masks(biomes_ref, row, kinds, species)
        every = list(range(levels))
        for level, change in zip(every, reaction(now_ref, 0, pieces, chosen, growth, row, every, species), strict=True):
            mask = wet_ref[pl.ds(level * TILE + row, species, stride=0), :]
            first_ref[pl.ds((level * TILE + row) * species, species), :] = mask * change


def advance(
    received, now_ref, wet_ref, biomes_ref, pieces_ref, first_ref, sent_out, last_ref, sent, work, ocean, coef, tracer, growth,
    heat, done, sizes,
):
    levels, species, total_lat, columns, kinds = sizes
    pieces = pieces_ref[...]
    count = total_lat // 2
    own = columns // TILE
    row, lane = rows_of(), lanes_of()
    lat = lane % total_lat

    turned = []
    for part in range(3):
        for q in range(own + 1):
            for j in range(2):
                work[pl.ds(part * LANES + q * total_lat + j, count, stride=2), :] = received[
                    pl.ds(part * TILE + q * 2 + j, count, stride=3 * TILE), :
                ]
        turned.append(work[part * LANES : (part + 1) * LANES, :].T)
        for r in range(TILE):
            ocean[pl.ds(part * levels * TILE + r, levels, stride=TILE), :] = turned[part][r * levels : (r + 1) * levels, :]
    spare = 3 * levels
    floors = [turned[1 + q // 2][spare + q % 2 * TILE : spare + (q % 2 + 1) * TILE, :] for q in range(own + 1)]
    floor = floors[own]
    for q in range(own):
        floor = jnp.where(lane // total_lat == q, spin(floors[q], (q - own) * total_lat, 1), floor)
    wet = [(float(level) < floor).astype(jnp.float32) for level in range(levels)]
    sea = [wet_ref[level * TILE : (level + 1) * TILE, :] for level in range(levels)]

    def read(field):
        return [ocean[(field * levels + k) * TILE : (field * levels + k + 1) * TILE, :] for k in range(levels)]

    def write(field, values):
        for k in range(levels):
            ocean[(field * levels + k) * TILE : (field * levels + k + 1) * TILE, :] = values[k]

    def east(x):
        y = spin(x, -1, 0)
        return jnp.where(row == TILE - 1, spin(y, -total_lat, 1), y)

    def west(x):
        y = spin(x, 1, 0)
        return jnp.where(row == 0, spin(y, total_lat, 1), y)

    def north(x):
        return jnp.where(lat == total_lat - 1, 0.0, spin(x, -1, 1))

    def south(x):
        return jnp.where(lat == 0, 0.0, spin(x, 1, 1))

    spin_rate = coriolis * (2.0 * (lat.astype(jnp.float32) + 0.5) / total_lat - 1.0)
    plane = levels * TILE

    def dynamics(step):
        speed_u, speed_v, steps = read(0), read(1), read(2)
        spread, new_u, new_v = [], [], []
        pressure = None
        for k in range(levels):
            u, v = speed_u[k], speed_v[k]
            u_east, u_west, v_north, v_south = east(u), west(u), north(v), south(v)
            if step < STEPS - 1:
                pressure = steps[k] if pressure is None else pressure + steps[k]
                slope_east = 0.5 * (east(pressure) - west(pressure))
                slope_north = 0.5 * (north(pressure) - south(pressure))
                lap_u = u_east + u_west + north(u) + south(u) - 4.0 * u
                lap_v = east(v) + west(v) + v_north + v_south - 4.0 * v
                new_u.append(wet[k] * (u + time_step * (spin_rate * v - slope_east + viscosity * lap_u)))
                new_v.append(wet[k] * (v + time_step * (-spin_rate * u - slope_north + viscosity * lap_v)))
            spread.append(0.5 * (u_east - u_west) + 0.5 * (v_north - v_south))
            face_east = 0.5 * (u + u_east)
            face_west = west(face_east)
            face_north = jnp.where(lat == total_lat - 1, 0.0, 0.5 * (v + v_north))
            face_south = spin(face_north, 1, 1)
            up_east, down_east = jnp.maximum(face_east, 0.0), jnp.minimum(face_east, 0.0)
            up_west, down_west = jnp.maximum(face_west, 0.0), jnp.minimum(face_west, 0.0)
            up_north, down_north = jnp.maximum(face_north, 0.0), jnp.minimum(face_north, 0.0)
            up_south, down_south = jnp.maximum(face_south, 0.0), jnp.minimum(face_south, 0.0)
            mask = tracer_step * sea[k]
            at = step * 7 * plane + k * TILE
            coef[pl.ds(at + plane, TILE), :] = mask * (tracer_diff - down_east)
            coef[pl.ds(at + 2 * plane, TILE), :] = mask * (tracer_diff + up_west)
            coef[pl.ds(at + 3 * plane, TILE), :] = jnp.where(
                lat == total_lat - 1, 0.0, mask * (tracer_diff - down_north)
            )
            coef[pl.ds(at + 4 * plane, TILE), :] = jnp.where(lat == 0, 0.0, mask * (tracer_diff + up_south))
            coef[pl.ds(at, TILE), :] = -4.0 * tracer_diff - up_east + down_west - up_north + down_south
        total = jnp.zeros((TILE, LANES), jnp.float32)
        below_up, below_down = total, total
        for k in reversed(range(levels)):
            total = total + spread[k]
            rise = -vert_ratio * total if k > 0 else jnp.zeros((TILE, LANES), jnp.float32)
            up, down = jnp.maximum(rise, 0.0), jnp.minimum(rise, 0.0)
            mask = tracer_step * sea[k]
            at = step * 7 * plane + k * TILE
            coef[pl.ds(at, TILE), :] = sea[k] + mask * (coef[pl.ds(at, TILE), :] - up + below_down)
            coef[pl.ds(at + 5 * plane, TILE), :] = -mask * down
            coef[pl.ds(at + 6 * plane, TILE), :] = mask * below_up
            below_up, below_down = up, down
        if step < STEPS - 1:
            write(0, new_u)
            write(1, new_v)

    def substep(step, source, base, target, target_base, ready):
        start = step * 7 * plane

        def body(group, carry):
            near = [group * 4 + i for i in range(4)]
            for r in range(TILE):
                if ready is None:
                    chosen = biome_masks(biomes_ref, r, kinds, species)
                    sums = reaction(source, base, pieces, chosen, growth, r, near, species)
                for place, level in enumerate(near):
                    cell = level * TILE + r
                    above = max(level - 1, 0) * TILE + r
                    under = min(level + 1, levels - 1) * TILE + r
                    weight = [coef[pl.ds(start + i * plane + cell, species, stride=0), :] for i in range(7)]
                    mask = None if ready is not None else wet_ref[pl.ds(cell, species, stride=0), :]

                    def take(index):
                        return source[pl.ds(base + index * species, species), :]

                    x = take(cell)
                    x_east = take(cell + 1) if r < TILE - 1 else spin(take(cell - r), -total_lat, 1)
                    x_west = take(cell - 1) if r > 0 else spin(take(cell + TILE - 1), total_lat, 1)
                    change = mask * sums[place] if ready is None else ready[pl.ds(cell * species, species), :]
                    value = (
                        (weight[0] * x + weight[1] * x_east)
                        + (weight[2] * x_west + weight[3] * spin(x, -1, 1))
                        + (weight[4] * spin(x, 1, 1) + weight[5] * take(above))
                        + (weight[6] * take(under) + change)
                    )
                    target[pl.ds(target_base + cell * species, species), :] = value
            return carry

        for group in range(levels // 4):
            body(group, 0)

    for field in range(3):
        write(field, [wet[k] * x for k, x in enumerate(read(field))])
    size = levels * TILE * species
    source, base = now_ref, 0
    lit = None
    for step in range(STEPS):
        dynamics(step)
        for sub in range(SUB):
            last = step == STEPS - 1 and sub == SUB - 1
            first = step == 0 and sub == 0
            target, target_base = (last_ref, 0) if last else (tracer, ((step * SUB + sub) % 2) * size)
            if not first:
                put_growth(growth, source, levels, species, total_lat, base)
            substep(step, source, base, target, target_base, first_ref if first else None)
            source, base = target, target_base
        lit = light(planes_of(source, 0, levels, species, base), surface_light(total_lat))
        for k in range(levels):
            _, top_light, attenuate = lit[k]
            heating = heat_gain * sea[k] * (top_light * (1.0 - jnp.exp(-attenuate)))
            for place, shift in enumerate(range(-1, 3) if step < STEPS - 1 else range(2)):
                at = ((place + 4 * step) * levels + k) * TILE
                heat[at : at + TILE, :] = spin(heating, -shift, 1)

    each = own * 6
    early, late = 4 * levels, 2 * levels
    for block in range(6):
        if block < 4:
            parts = [heat[pl.ds(2 * block + i, early, stride=TILE), :] for i in range(2)]
        else:
            parts = [heat[pl.ds(early * TILE + 4 * (block - 4) + i, late, stride=TILE), :] for i in range(4)]
        work[block * LANES : (block + 1) * LANES, :] = jnp.concatenate(parts, axis=0).T
        for q in range(own):
            place = q * 4 + block if block < 4 else own * 4 + q * 2 + block - 4
            sent[pl.ds(place, count, stride=each), :] = work[pl.ds(block * LANES + q * total_lat, count, stride=2), :]
    send = pltpu.make_async_copy(sent, sent_out, done)
    send.start()
    send.wait()


def unpack_tracers(last_ref, out_ref):
    species, levels, columns, total_lat = out_ref.shape
    for level in range(levels):
        for kind in range(species):
            whole = last_ref[pl.ds(level * TILE * species + kind, TILE, stride=species), :]
            for q in range(columns // TILE):
                out_ref[kind, level, TILE * q : TILE * (q + 1), :] = whole[:, q * total_lat : (q + 1) * total_lat]


def down_sum(x):
    index = rows_of(x.shape)
    step = 1
    while step < x.shape[0]:
        x = x + jnp.where(index >= step, spin(x, step, 0), 0.0)
        step *= 2
    return x


def slope(x):
    return 0.5 * (spin(x, -1, 1) - spin(x, 1, 1))


def lap(before, x, after):
    return spin(x, -1, 1) + spin(x, 1, 1) + after + before - 4.0 * x


def at_home(own_ref, first_ref, second_ref, base_ref, wet_ref, levels, total_lat):
    half = FIELDS * levels
    rows = range(-2, 4)
    start = lax.axis_index("lat") * 2
    even = is_even()

    def raw(at, size, offset):
        place = slice(at % 2 * offset[0] + offset[1], at % 2 * offset[0] + offset[1] + size)
        if 0 <= at < 2:
            return own_ref[place, :]
        return jnp.where(even == (at > 0), first_ref[place, :], second_ref[place, :])

    wet, u, v, t, s = {}, {}, {}, {}, {}
    for j in rows:
        floor = raw(j, 1, (1, 2 * half))
        level = rows_of((levels, floor.shape[1])).astype(jnp.float32)
        wet[j] = (level < floor).astype(jnp.float32)
        u[j], v[j], t[j], s[j] = [wet[j] * raw(j, levels, (half, field * levels)) for field in range(FIELDS)]

    def step(u, v, t, s, inner):
        pressure = {j: gravity * down_sum(haline_coef * s[j] - therm_coef * t[j]) for j in u}
        fresh = ({}, {}, {}, {})
        for j in inner:
            turn = coriolis * (2.0 * ((start + j).astype(jnp.float32) + 0.5) / total_lat - 1.0)
            north_slope = 0.5 * (pressure[j + 1] - pressure[j - 1])
            laps = [lap(x[j - 1], x[j], x[j + 1]) for x in (u, v, t, s)]
            fresh[0][j] = wet[j] * (u[j] + time_step * (turn * v[j] - slope(pressure[j]) + viscosity * laps[0]))
            fresh[1][j] = wet[j] * (v[j] + time_step * (-turn * u[j] - north_slope + viscosity * laps[1]))
            fresh[2][j] = wet[j] * (t[j] + time_step * heat_diff * laps[2])
            fresh[3][j] = wet[j] * (s[j] + time_step * salt_diff * laps[3])
        return fresh

    final = step(*step(u, v, t, s, range(-1, 3)), range(2))
    for j in range(2):
        for field in range(FIELDS):
            begin = j * half + field * levels
            base_ref[begin : begin + levels, :] = final[field][j]
    for j in range(-1, 3):
        wet_ref[(j + 1) * levels : (j + 2) * levels, :] = wet[j]


def finish(received, base_ref, wet_ref, out_ref, early, late, flat):
    fields, levels, _, _ = out_ref.shape
    half = fields * levels
    columns = 3 * TILE
    count = out_ref.shape[3] // columns
    each = received.shape[0] // count
    for place in range(each):
        line = received[pl.ds(place, count, stride=each), :]
        if place < columns // 2:
            for i in range(2):
                early[pl.ds(2 * place + i, count, stride=columns), :] = spin(line, -i * LANES // 2, 1)
        else:
            for i in range(4):
                begin = 4 * (place - columns // 2) + i
                late[pl.ds(begin, count, stride=columns), :] = spin(line, (2 - i) * LANES // 4, 1)
    heating = jnp.where(lanes_of(early.shape) < LANES // 2, early[...], late[...]).T

    def part(ref, place):
        return ref[place * levels : (place + 1) * levels, :]

    wet = {j: part(wet_ref, j + 1) for j in range(-1, 3)}
    warm = {j: time_step * (wet[j] * part(heating, j + 1)) for j in wet}
    push = {j: (gravity * therm_coef) * down_sum(warm[j]) for j in wet}
    for j in range(2):
        u, v, t, s = [part(base_ref, j * fields + field) for field in range(fields)]
        late = wet[j] * part(heating, 4 + j)
        spread = lap(warm[j - 1], warm[j], warm[j + 1])
        results = (
            u + wet[j] * (time_step * slope(push[j])),
            v + wet[j] * (time_step * (0.5 * (push[j + 1] - push[j - 1]))),
            t + wet[j] * (warm[j] + time_step * heat_diff * spread) + time_step * late,
            s,
        )
        for field, value in enumerate(results):
            begin = j * half + field * levels
            flat[begin : begin + levels, :] = value
    for index in range(half):
        field, level = divmod(index, levels)
        for row in range(2):
            out_ref[field, level, row : row + 1, :] = flat[row * half + index : row * half + index + 1, :]


def grids(*shapes):
    return [pltpu.VMEM(shape, jnp.float32) for shape in shapes]


def far(*shape):
    return pltpu.HBM(shape, jnp.float32)


def near(*shape, dtype=jnp.float32):
    return pltpu.VMEM(shape, dtype)


def placed(space, *arrays):
    return [pltpu.with_memory_space_constraint(x, space) for x in arrays]


def shards(ocean_state, bottom, tracers, land_sea, biome_id, rate_table):
    count = lax.axis_size("lat")
    if not fits(ocean_state, tracers, count):
        return general_shards(ocean_state, bottom, tracers, land_sea, biome_id, rate_table)
    _, levels, _, total_lon = ocean_state.shape
    species, _, columns, total_lat = tracers.shape
    cells = levels * TILE
    size = cells * species
    own = columns // TILE

    edge_rows = (species + 1) * (levels * total_lat // LANES) * HALO + 2 * HALO
    packed_rows = count * 3 * TILE
    home_shape = (LANES + TILE, total_lon)
    kinds = rate_table.shape[0]
    roomy = pltpu.CompilerParams(vmem_limit_bytes=GRANT)
    ocean_state, bottom, tracers, land_sea, biome_id, rate_table = placed(
        pltpu.HBM, ocean_state, bottom, tracers, land_sea, biome_id, rate_table
    )
    vmem = pl.BlockSpec(memory_space=pltpu.VMEM)
    hbm = pl.BlockSpec(memory_space=pltpu.HBM)

    pairs = [(i, i ^ 1) for i in range(count)]
    others = [((a + 1) % count, (b + 1) % count) for a, b in pairs]
    sizes = (levels, species, total_lat, columns, kinds)
    edge_shape = (species, levels, TILE, total_lat)

    packed, to_first, to_second, home = pl.pallas_call(
        pack,
        out_shape=[far(packed_rows, LANES), near(edge_rows, LANES), near(edge_rows, LANES), far(*home_shape)],
        in_specs=[hbm] * 5,
        out_specs=[hbm, vmem, vmem, hbm],
        scratch_shapes=grids((total_lon, LANES), (6 * (total_lon // TILE + 2 * TILE), LANES), ocean_state.shape)
        + [pltpu.VMEM(bottom.shape, bottom.dtype)]
        + grids(edge_shape, edge_shape)
        + [pltpu.VMEM(x.shape, x.dtype) for x in (land_sea, biome_id)]
        + grids((packed_rows, LANES), home_shape)
        + [pltpu.SemaphoreType.DMA((6,)), pltpu.SemaphoreType.DMA((2,))],
        compiler_params=roomy,
        name="pack",
    )(ocean_state, bottom, tracers, land_sea, biome_id)
    received = lax.all_to_all(
        packed.reshape(count, packed_rows // count, LANES), "lat", split_axis=0, concat_axis=0, tiled=True
    ).reshape(packed.shape)
    from_first = lax.ppermute(to_first, "lat", pairs)
    from_second = lax.ppermute(to_second, "lat", others)
    first_rows = lax.ppermute(home, "lat", pairs)
    inner = [(a, b) for a, b in others if abs(a - b) == 1]
    second_rows = lax.ppermute(home, "lat", inner)
    from_first, from_second, received = placed(pltpu.VMEM, from_first, from_second, received)

    inside = pl.pallas_call(
        prepare_own,
        out_shape=[
            near(size, LANES),
            near(cells, LANES),
            near(TILE, LANES),
            near(kinds * species, 3 * species, dtype=jnp.bfloat16),
        ],
        in_specs=[hbm] * 4,
        out_specs=[vmem] * 4,
        scratch_shapes=[pltpu.VMEM(x.shape, x.dtype) for x in (tracers, land_sea, biome_id, rate_table)]
        + [pltpu.SemaphoreType.DMA((4,))],
        compiler_params=roomy,
        name="prepare_own",
    )(tracers, land_sea, biome_id, rate_table)
    pieces = inside[3]

    def prepare(*refs):
        prepare_all(*refs, sizes)

    now, wet, biomes, first = pl.pallas_call(
        prepare,
        out_shape=[near(size, LANES), near(cells, LANES), near(TILE, LANES), near(size, LANES)],
        in_specs=[vmem] * 6,
        out_specs=[vmem] * 4,
        scratch_shapes=grids((cells, LANES)),
        compiler_params=roomy,
        name="prepare",
    )(*inside, from_first, from_second)

    def run(*refs):
        advance(*refs, sizes)

    sent, last = pl.pallas_call(
        run,
        out_shape=[far(count * own * 6, LANES), near(size, LANES)],
        in_specs=[vmem] * 6,
        out_specs=[hbm, vmem],
        scratch_shapes=grids(
            (count * own * 6, LANES),
            (TILE * LANES, LANES),
            (3 * cells, LANES),
            (STEPS * 7 * cells, LANES),
            (2 * size, LANES),
            (cells, LANES),
            (6 * cells, LANES),
        )
        + [pltpu.SemaphoreType.DMA],
        compiler_params=pltpu.CompilerParams(vmem_limit_bytes=GRANT),
        name="advance",
    )(received, now, wet, biomes, pieces, first)
    back = lax.all_to_all(
        sent.reshape(count, 1, own * 6 * LANES), "lat", split_axis=0, concat_axis=0, tiled=True
    ).reshape(sent.shape)

    def stay(*refs):
        at_home(*refs, levels, total_lat)

    base, masks = pl.pallas_call(
        stay,
        out_shape=[near(LANES, total_lon), near(4 * levels, total_lon)],
        in_specs=[vmem] * 3,
        out_specs=[vmem] * 2,
        compiler_params=roomy,
        name="at_home",
    )(*placed(pltpu.HBM, home, first_rows, second_rows))
    (back,) = placed(pltpu.VMEM, back)
    (last,) = placed(pltpu.VMEM, last)
    tracers_out = pl.pallas_call(
        unpack_tracers,
        out_shape=far(*tracers.shape),
        in_specs=[vmem],
        out_specs=vmem,
        compiler_params=roomy,
        name="unpack_tracers",
    )(last)
    state_out = pl.pallas_call(
        finish,
        out_shape=far(*ocean_state.shape),
        in_specs=[vmem] * 3,
        out_specs=vmem,
        scratch_shapes=grids((total_lon, LANES), (total_lon, LANES), (LANES, total_lon)),
        compiler_params=roomy,
        name="finish",
    )(back, base, masks)
    return (state_out, tracers_out)


def solution(mesh):
    in_specs = (
        P(None, None, ("groups", "lat"), None),
        P(("groups", "lat"), None),
        P(None, None, ("groups", "lat"), None),
        P(None, ("groups", "lat"), None),
        P(("groups", "lat"), None),
        P(),
    )
    out_specs = (P(None, None, ("groups", "lat"), None), P(None, None, ("groups", "lat"), None))
    return jax.shard_map(shards, mesh=mesh, in_specs=in_specs, out_specs=out_specs, check_vma=False)
```
